32 devices in a mesh: groups: 2 (over x), paths: 16 (over z, y, core).
Axes of the slice: x: 2, y: 2, z: 4, core: 2. Of those that a mesh axis runs over, the one named last changes fastest.
Arguments:
- path_basis: bfloat16 [4096, 512], P(('groups', 'paths')), parts along dimension 0, may hold values from -6 to 6
- proxy_weight: bfloat16 [4096, 512], P(('groups', 'paths')), parts along dimension 0, may hold values from -0.25 to 0.25
- notional: bfloat16 [4096], P(('groups', 'paths')), parts along dimension 0, may hold values from -4 to 4
- set_of: int32 [4096], P('groups'), parts along dimension 0, may hold values from 0 to 511
- threshold_index: int32 [1024], P('groups'), parts along dimension 0, may hold values from 0 to 15
- threshold_levels: float32 [32], P('groups'), parts along dimension 0, may hold values from 0.5 to 20
- loss_rate: float32 [1024], P('groups'), parts along dimension 0, may hold values from 0.4 to 1
Outputs:
- expected_loss: float32 [2], P('groups'), parts along dimension 0
- basis_adjoint: float32 [4096, 512], P(('groups', 'paths')), parts along dimension 0
- weight_adjoint: float32 [4096, 512], P(('groups', 'paths')), parts along dimension 0
The draws below stay inside these ranges and needn't reach their ends.
There are 2 independent parts, one for each index of `groups`. The reference program is written for one: setup_inputs(seed, part) draws one part's arguments, and reference() takes and returns one part's arrays. A program takes and returns all parts, laid end to end along the dimension named above; each array names one. Nothing has to cross between parts.
Inputs may be any that keep to these rules, and one draw needn't show every extreme that they name: `set_of`: netting set of each trade; set sizes are uneven.
All inputs are finite; a program needn't handle non-finite values.
Results may differ from the reference program's by a relative error of at most 0.0041.
Values may be sent and summed in bfloat16 or wider, within the bound.
A program may use at most 64 MiB of HBM per device.

```python
import math
import jax
import jax.numpy as jnp
import numpy as np
from jax import lax

FEATURES = 512
TRADES = 2048
SETS = 512
REGRESSORS = 32
LEVELS = 16
PATHS = 2048


def plant(array, rng, smallest, high):
    spot = [jax.random.randint(jax.random.fold_in(rng, axis), (), 0, length) for axis, length in enumerate(array.shape)]
    main_axis = array.shape.index(max(array.shape))
    next_to = spot[:main_axis] + [(spot[main_axis] + 1) % array.shape[main_axis]] + spot[main_axis + 1:]
    return array.at[tuple(spot)].set(smallest).at[tuple(next_to)].set(high)


def block_scale(key, extent, shards, smallest, high):
    def one(dim, parts):
        heights = jax.random.uniform(jax.random.fold_in(jax.random.fold_in(key, 6), dim), (parts,), jnp.float32, smallest / len(shards), high / len(shards))
        return jnp.repeat(jnp.exp(heights), extent[dim] // parts).reshape((-1,) + (1,) * (len(extent) - dim - 1))

    level = one(*shards[0])
    for cut in shards[1:]:
        level = level * one(*cut)
    return level


def rank_bounds(number_of, slope):
    portions = [(1 << 20) // math.isqrt(standing ** slope) + 1 for standing in range(1, number_of + 1)]
    deviation = 1 + sum(portions) // (1 << 30)
    return np.cumsum(np.array([max(1, weight // deviation) for weight in portions]))


def ranked(own_key, shape, count, lean):
    grid = rank_bounds(count, lean)
    pick = jax.random.randint(jax.random.fold_in(own_key, 1), shape, 0, int(grid[count - 1]))
    standing = jnp.searchsorted(jnp.asarray(grid, jnp.int32), pick, side="right")
    return jax.random.permutation(jax.random.fold_in(own_key, 2), count)[standing].astype(jnp.int32)


def gaussian(stream_key, dims, spread, most, cuts=(), kind=jnp.bfloat16):
    level = block_scale(stream_key, dims, cuts, -0.22, 0.18) if cuts else 1.0
    entries = jax.random.normal(stream_key, dims, jnp.float32) * spread * level
    return jnp.minimum(jnp.maximum(entries, -most), most).astype(kind)


def setup_inputs(seed: int = 0, part: int = 0) -> dict:
    key_list = jax.random.split(jax.random.key(seed), 8)
    part_keys = jax.random.split(jax.random.fold_in(key_list[7], part), 8)
    return {
        "path_basis": gaussian(part_keys[0], (PATHS, FEATURES), 1.0, 6.0, ((0, 16),)),
        "proxy_weight": gaussian(part_keys[1], (TRADES, FEATURES), FEATURES ** -0.5, 0.25, ((0, 16),)),
        "notional": jnp.clip(jax.random.uniform(part_keys[2], (TRADES,), jnp.float32, -4.0, 4.0) * block_scale(part_keys[2], (TRADES,), ((0, 16),), -0.4, 0.0), -4.0, 4.0).astype(jnp.bfloat16),
        "set_of": plant(ranked(part_keys[3], (TRADES,), SETS, 2), jax.random.fold_in(part_keys[3], 3), 0, SETS - 1).astype(jnp.int32),
        "threshold_index": plant(jax.random.randint(part_keys[4], (SETS,), 0, LEVELS), jax.random.fold_in(part_keys[4], 1), 0, LEVELS - 1).astype(jnp.int32),
        "threshold_levels": jnp.clip(jnp.exp(jax.random.uniform(part_keys[5], (LEVELS,), jnp.float32, math.log(0.5), math.log(20.0))), 0.5, 20.0),
        "loss_rate": jnp.clip(jax.random.uniform(part_keys[6], (SETS,), jnp.float32, 0.4, 1.0), 0.4, 1.0),
    }


RIDGE_SCALE = 0.01
PRECISE = lax.Precision.HIGHEST

def table_rows(labels, classes, target_type):
    return (labels[:, None] == jnp.arange(classes, dtype=jnp.int32)[None, :]).astype(target_type)

def contract_rows(former, latter):
    return lax.dot_general(former.astype(jnp.float32), latter.astype(jnp.float32), (((0,), (0,)), ((), ())), precision=PRECISE, preferred_element_type=jnp.float32)

def contract_cols(former, latter):
    return lax.dot_general(former.astype(jnp.float32), latter.astype(jnp.float32), (((1,), (1,)), ((), ())), precision=PRECISE, preferred_element_type=jnp.float32)

def matrix_product(former, latter):
    return jnp.dot(former.astype(jnp.float32), latter.astype(jnp.float32), precision=PRECISE, preferred_element_type=jnp.float32)

def spd_solve(matrix, target):
    lower_factor = jnp.linalg.cholesky(matrix)
    halfway = lax.linalg.triangular_solve(lower_factor, target, left_side=True, lower=True)
    return lax.linalg.triangular_solve(lower_factor, halfway, left_side=True, lower=True, transpose_a=True)

def reference(path_basis, proxy_weight, notional, set_of, threshold_index, threshold_levels, loss_rate):
    path_count = path_basis.shape[0]
    trade_count, feature_count = proxy_weight.shape
    set_total = loss_rate.shape[0]
    block_cols = math.gcd(256, trade_count)
    block_count = trade_count // block_cols
    weight_blocks = proxy_weight.reshape(block_count, block_cols, feature_count)
    notional_blocks = notional.astype(jnp.float32).reshape(block_count, block_cols)
    set_blocks = set_of.reshape(block_count, block_cols)

    def forward_step(running, pieces):
        weight_block, notional_block, set_block = pieces
        pre_act = lax.dot_general(path_basis.astype(jnp.float32), weight_block.astype(jnp.float32), (((1,), (1,)), ((), ())), preferred_element_type=jnp.float32)
        trade_value = (notional_block[None, :] * jax.nn.softplus(pre_act)).astype(jnp.bfloat16)
        return (running + jnp.dot(trade_value.astype(jnp.float32), table_rows(set_block, set_total, jnp.bfloat16).astype(jnp.float32), preferred_element_type=jnp.float32), None)
    exposure, _ = lax.scan(forward_step, jnp.zeros((path_count, set_total), jnp.float32), (weight_blocks, notional_blocks, set_blocks))
    thresholds = lax.optimization_barrier(jnp.sum(table_rows(threshold_index, threshold_levels.shape[0], jnp.float32) * threshold_levels[None, :], axis=1))
    design = jnp.concatenate([jnp.ones((path_count, 1), jnp.float32), path_basis[:, :REGRESSORS - 1].astype(jnp.float32)], axis=1)
    gram_matrix = contract_rows(design, design) + RIDGE_SCALE * path_count * jnp.eye(REGRESSORS, dtype=jnp.float32)
    coeffs = spd_solve(gram_matrix, contract_rows(design, exposure))
    fitted = matrix_product(design, coeffs)
    excess = fitted - thresholds[None, :]
    expected_loss = (jnp.sum(loss_rate[None, :] * jax.nn.softplus(excess)) / (path_count * set_total)).reshape(1)
    seed_adjoint = loss_rate[None, :] * jax.nn.sigmoid(excess)
    solve_adjoint = spd_solve(gram_matrix, contract_rows(design, seed_adjoint))
    adjoint_full = matrix_product(design, solve_adjoint)
    exposure_adjoint = adjoint_full.astype(jnp.bfloat16)
    design_adjoint = contract_cols(seed_adjoint - adjoint_full, coeffs) + contract_cols(exposure - fitted, solve_adjoint)

    def backward_step(running, pieces):
        weight_block, notional_block, set_block = pieces
        pre_trans = lax.dot_general(weight_block.astype(jnp.float32), path_basis.astype(jnp.float32), (((1,), (1,)), ((), ())), preferred_element_type=jnp.float32)
        spread_trans = lax.dot_general(table_rows(set_block, set_total, jnp.bfloat16).astype(jnp.float32), exposure_adjoint.astype(jnp.float32), (((1,), (1,)), ((), ())), preferred_element_type=jnp.float32)
        slope_trans = (notional_block[:, None] * jax.nn.sigmoid(pre_trans) * spread_trans).astype(jnp.bfloat16)
        running = running + lax.dot_general(slope_trans.astype(jnp.float32), weight_block.astype(jnp.float32), (((0,), (0,)), ((), ())), preferred_element_type=jnp.float32)
        return (running, jnp.dot(slope_trans.astype(jnp.float32), path_basis.astype(jnp.float32), preferred_element_type=jnp.float32))
    back_total, weight_rows = lax.scan(backward_step, jnp.zeros((path_count, feature_count), jnp.float32), (weight_blocks, notional_blocks, set_blocks))
    padding = jnp.zeros((path_count, feature_count - REGRESSORS + 1), jnp.float32)
    basis_adjoint = back_total + jnp.concatenate([design_adjoint[:, 1:], padding], axis=1)
    weight_adjoint = weight_rows.reshape(trade_count, feature_count) * (1.0 / math.sqrt(path_count))
    return (expected_loss, basis_adjoint, weight_adjoint)
```

```python
import functools
import math

import jax
import jax.numpy as jnp
from jax import lax
from jax.experimental import pallas as pl
from jax.experimental.pallas import tpu as pltpu
from jax.sharding import PartitionSpec as P

REGRESSORS = 32
RIDGE_SCALE = 0.01
PRECISE = lax.Precision.HIGHEST
LANES = 128
PIECES = 4
FIRST_STEPS = 12
COPIES = 64
F32 = jnp.float32
BF16 = jnp.bfloat16

NN = (((1,), (0,)), ((), ()))
NT = (((1,), (1,)), ((), ()))
TN = (((0,), (0,)), ((), ()))


def mm(a, b, dims=NN):
    return lax.dot_general(a, b, dims, preferred_element_type=F32)


def precise(a, b, dims=NN):
    return lax.dot_general(a, b, dims, precision=PRECISE, preferred_element_type=F32)


def split3(x):
    hi = x.astype(BF16)
    rest = x - hi.astype(F32)
    mid = rest.astype(BF16)
    lo = (rest - mid.astype(F32)).astype(BF16)
    return hi, mid, lo


def stack3(x):
    hi, mid, lo = split3(x)
    return jnp.concatenate([hi, mid, lo, jnp.zeros_like(hi)], axis=0)


def design_of(basis):
    front = pltpu.roll(basis[:, :LANES].astype(F32), 1, 1)
    lane = lax.broadcasted_iota(jnp.int32, front.shape, 1)
    return jnp.where(lane == 0, 1.0, jnp.where(lane < REGRESSORS, front, 0.0))


def triple(design):
    return (
        design + pltpu.roll(design, REGRESSORS, 1) + pltpu.roll(design, 2 * REGRESSORS, 1)
    ).astype(BF16)


def augmented(gram):
    row = lax.broadcasted_iota(jnp.int32, gram.shape, 0)
    lane = lax.broadcasted_iota(jnp.int32, gram.shape, 1)
    return jnp.where(lane < REGRESSORS, gram, jnp.where(lane == row + REGRESSORS, 1.0, 0.0))


def eliminate(work, first, last):
    row = lax.broadcasted_iota(jnp.int32, work.shape, 0)
    for k in range(first, last):
        column = jnp.broadcast_to(work[:, k : k + 1], work.shape)
        pivot = work[k : k + 1, :] / column[k : k + 1, :]
        work = jnp.where(row == k, pivot, work - column * pivot)
    return work


def spd_inverse(gram):
    work = eliminate(augmented(gram), 0, REGRESSORS)
    return pltpu.roll(work, LANES - REGRESSORS, 1)


def set_table(labels, set_total):
    sets = lax.broadcasted_iota(jnp.int32, (set_total, labels.shape[1]), 0)
    return jnp.where(sets == labels, 1.0, 0.0).astype(BF16)


def partner(index, step, count):
    if count & (count - 1):
        return lax.rem(index + step, count)
    result, weight = 0, 1
    while weight < count:
        bit = lax.rem(lax.div(index, weight), 2)
        result = result + weight * (1 - bit if step & weight else bit)
        weight *= 2
    return result


def kernel(
    inner, outer, paths_all, set_total,
    pb_hbm, w_hbm, not_hbm, set_hbm, tidx_hbm, level_hbm, rate_hbm,
    loss_ref, basis_ref, wadj_ref,
    not_ref, set_ref, tidx_ref, level_ref, rate_ref,
    pall, wall, nall, nsend, gown, gall, gq, dstack, table, invert,
    bown, bq, bzsend, bz, csend, cq, ssend, sq,
    eown, eq, wown, wz, pown, pq, nsig, tval,
    local, zsend, zrecv, qsend, qrecv,
):
    rows, feats = basis_ref.shape
    trades = wadj_ref.shape[0]
    quarter = set_total // inner
    me = lax.axis_index("paths")
    q = lax.rem(me, inner)
    z = lax.div(me, inner)

    loads = [
        pltpu.make_async_copy(source, target, local.at[i])
        for i, (source, target) in enumerate(
            [
                (pb_hbm, pall.at[q]),
                (not_hbm, not_ref),
                (w_hbm, wall.at[z]),
                (set_hbm, set_ref),
                (tidx_hbm, tidx_ref),
                (level_hbm, level_ref),
                (rate_hbm, rate_ref),
            ]
        )
    ]
    for load in loads:
        load.start()

    barrier = pltpu.get_barrier_semaphore()
    for d in range(1, inner):
        pl.semaphore_signal(
            barrier, inc=1, device_id={"paths": z * inner + lax.rem(q + d, inner)},
            device_id_type=pl.DeviceIdType.MESH,
        )
    for d in range(1, outer):
        pl.semaphore_signal(
            barrier, inc=1, device_id={"paths": lax.rem(z + d, outer) * inner + q},
            device_id_type=pl.DeviceIdType.MESH,
        )

    pending = []

    def over_q(which, source, target):
        copies = []
        for d in range(inner - 1, 0, -1):
            peer = partner(q, d, inner)
            copy = pltpu.make_async_remote_copy(
                src_ref=source(peer), dst_ref=target.at[q],
                send_sem=qsend.at[which, d - 1], recv_sem=qrecv.at[which, d - 1],
                device_id={"paths": z * inner + peer},
                device_id_type=pl.DeviceIdType.MESH,
            )
            copy.start()
            copies.append(copy)
        pending.extend(copies)
        return copies

    def over_z(which, source, target):
        copies = []
        for d in range(outer - 1, 0, -1):
            peer = partner(z, d, outer)
            copy = pltpu.make_async_remote_copy(
                src_ref=source(peer), dst_ref=target.at[z],
                send_sem=zsend.at[which, d - 1], recv_sem=zrecv.at[which, d - 1],
                device_id={"paths": peer * inner + q},
                device_id_type=pl.DeviceIdType.MESH,
            )
            copy.start()
            copies.append(copy)
        pending.extend(copies)
        return copies

    def arrive(copies):
        for copy in copies:
            copy.wait_recv()

    def total(ref, count):
        result = ref[0].astype(F32)
        for i in range(1, count):
            result = result + ref[i].astype(F32)
        return result

    loads[0].wait()
    own_design = design_of(pall[q])
    own_triple = triple(own_design)
    own_turned = jnp.transpose(own_design)[:REGRESSORS, :].astype(BF16)
    gown[...] = own_turned
    loads[1].wait()
    nrow = jnp.broadcast_to(not_ref[...].astype(F32), (8, trades))
    nsend[...] = nrow
    loads[2].wait()
    pl.semaphore_wait(barrier, inner + outer - 2)

    gram_z = over_z(0, lambda peer: gown, gall)
    note_z = over_z(1, lambda peer: nsend, nall)
    trade_z = over_z(2, lambda peer: wall.at[z], wall)
    path_q = over_q(0, lambda peer: pall.at[q], pall)
    gall[z] = own_turned
    nall[z] = nrow

    arrive(gram_z)
    gram_q = over_q(1, lambda peer: gall, gq)
    gq[q] = gall[...]

    for load in loads[3:]:
        load.wait()
    all_levels = tidx_ref[...]
    all_thresholds = jnp.zeros((inner, quarter), F32)
    levels = tidx_ref[pl.ds(q, 1), :]
    thresholds = jnp.zeros((1, quarter), F32)
    for i in range(level_ref.shape[0]):
        thresholds = jnp.where(levels == i, level_ref[i], thresholds)
        all_thresholds = jnp.where(all_levels == i, level_ref[i], all_thresholds)
    thresholds = jnp.transpose(jnp.broadcast_to(thresholds, (quarter, quarter)))[:, :1]
    rate = jnp.transpose(
        jnp.broadcast_to(rate_ref[pl.ds(q, 1), :], (quarter, quarter))
    )[:, :1]
    all_rates = rate_ref[...]
    labels = jnp.concatenate(
        [set_ref[pl.ds(i * inner + q, 1), :] for i in range(outer)], axis=1
    )
    table[...] = set_table(labels, set_total)

    arrive(path_q)
    paths = pall[...].reshape(inner * rows, feats)
    design = design_of(paths)
    design3 = triple(design)
    design_t = jnp.transpose(design)[:REGRESSORS, :].astype(BF16)

    arrive(gram_q)
    turned_all = jnp.concatenate(
        [gq[i, j] for i in range(inner) for j in range(outer)], axis=1
    )
    dstack[...] = jnp.concatenate(
        [turned_all, turned_all, turned_all, jnp.zeros_like(turned_all)], axis=0
    )
    gram = mm(turned_all, dstack[...], NT)
    gram_row = lax.broadcasted_iota(jnp.int32, (REGRESSORS, LANES), 0)
    gram_lane = lax.broadcasted_iota(jnp.int32, (REGRESSORS, LANES), 1)
    ridge = jnp.where(gram_row == gram_lane, RIDGE_SCALE * paths_all, 0.0)
    invert[...] = spd_inverse(gram + ridge)

    arrive(note_z)
    notional = jnp.concatenate([nall[i][0:1, :] for i in range(outer)], axis=1)
    arrive(trade_z)
    weights = wall[...].reshape(outer * trades, feats)
    pre_act = mm(paths, weights, NT)
    small = jnp.exp(-jnp.abs(pre_act))
    tval[...] = (notional * (jnp.maximum(pre_act, 0.0) + jnp.log1p(small))).astype(BF16)
    nsig[...] = notional * (jnp.where(pre_act >= 0.0, 1.0, small) / (1.0 + small))

    by_trade = mm(design_t, tval[...])
    by_set = mm(jnp.concatenate(split3(by_trade), axis=0), table[...], NT)
    moments = (
        by_set[:REGRESSORS] + by_set[REGRESSORS : 2 * REGRESSORS] + by_set[2 * REGRESSORS :]
    )
    for i in range(inner):
        bown[i] = moments[:, i * quarter : (i + 1) * quarter]
    moment_q = over_q(2, lambda peer: bown.at[peer], bq)
    bq[q] = bown[q]
    arrive(moment_q)
    moment_mid = total(bq, inner)
    bzsend[...] = moment_mid
    moment_z = over_z(3, lambda peer: bzsend, bz)
    bz[z] = moment_mid
    arrive(moment_z)
    inverse = invert[:, :REGRESSORS]
    coeffs = precise(inverse, total(bz, outer))
    csend[...] = coeffs
    coeffs_q = over_q(3, lambda peer: csend, cq)
    cq[q] = coeffs
    excess = mm(stack3(coeffs), dstack[...], TN) - thresholds
    fade = jnp.exp(-jnp.abs(excess))
    loss = jnp.maximum(excess, 0.0) + jnp.log1p(fade)
    seed = rate * (jnp.where(excess >= 0.0, 1.0, fade) / (1.0 + fade))
    seed_cut = mm(dstack[:REGRESSORS, :], jnp.concatenate(split3(seed), axis=0), NT)
    seed_sum = (
        seed_cut[:, :quarter] + seed_cut[:, quarter : 2 * quarter] + seed_cut[:, 2 * quarter :]
    )
    solved = precise(inverse, seed_sum)
    loss_part = jnp.sum(rate * jnp.sum(loss, axis=1, keepdims=True), axis=0, keepdims=True)
    answer = jnp.concatenate([solved, jnp.broadcast_to(loss_part, (8, quarter))], axis=0)
    ssend[...] = answer
    answer_q = over_q(4, lambda peer: ssend, sq)
    sq[q] = answer
    arrive(coeffs_q)
    coeffs_all = jnp.concatenate([cq[i] for i in range(inner)], axis=1)
    arrive(answer_q)
    answers = jnp.concatenate([sq[i] for i in range(inner)], axis=1)
    solved_all = answers[:REGRESSORS]
    loss_sum = jnp.sum(answers[REGRESSORS : REGRESSORS + 1], axis=1, keepdims=True) / quarter
    loss_ref[...] = jnp.broadcast_to(loss_sum / (paths_all * set_total), loss_ref.shape)

    picked = mm(jnp.concatenate(split3(solved_all), axis=0), table[...])
    solved3 = jnp.concatenate(
        [picked.astype(BF16), jnp.zeros((LANES - 3 * REGRESSORS, picked.shape[1]), BF16)], axis=0
    )
    spread = mm(design3, solved3).astype(BF16).astype(F32)
    slopes = (nsig[...] * spread).astype(BF16)
    scale = 1.0 / math.sqrt(paths_all)
    weight_part = mm(slopes, paths, TN) * scale
    wown[...] = weight_part.astype(BF16).reshape(outer, trades, feats)
    weight_z = over_z(4, lambda peer: wown.at[peer], wz)
    wz[z] = wown[z]

    pulled = mm(solved3, tval[...], NT)
    pulled = (
        pulled[:REGRESSORS]
        + pulled[REGRESSORS : 2 * REGRESSORS]
        + pulled[2 * REGRESSORS : 3 * REGRESSORS]
    )
    for i in range(inner):
        eown[i] = pulled[:, i * rows : (i + 1) * rows]
    pull_q = over_q(5, lambda peer: eown.at[peer], eq)
    eq[q] = eown[q]
    basis_part = mm(slopes, weights)
    pown[...] = basis_part.astype(BF16).reshape(inner, rows, feats)
    basis_q = over_q(6, lambda peer: pown.at[peer], pq)
    pq[q] = pown[q]

    fitted = mm(own_triple, stack3(coeffs_all))
    full_thresholds = jnp.concatenate([all_thresholds[i : i + 1] for i in range(inner)], axis=1)
    full_rates = jnp.concatenate([all_rates[i : i + 1] for i in range(inner)], axis=1)
    over = fitted - full_thresholds
    tail = jnp.exp(-jnp.abs(over))
    own_seed = full_rates * (jnp.where(over >= 0.0, 1.0, tail) / (1.0 + tail))
    residual = own_seed - mm(own_triple, stack3(solved_all))
    term = precise(coeffs_all, residual, NT) - precise(solved_all, fitted, NT)
    arrive(pull_q)
    term = term + total(eq, inner)
    padded = jnp.concatenate([term, jnp.zeros((LANES - REGRESSORS, rows), F32)], axis=0)
    turned = pltpu.roll(jnp.transpose(padded), LANES - 1, 1)
    lane = lax.broadcasted_iota(jnp.int32, turned.shape, 1)
    turned = jnp.where(lane < REGRESSORS - 1, turned, 0.0)
    arrive(basis_q)
    basis_ref[...] = total(pq, inner)
    basis_ref[:, :LANES] = basis_ref[:, :LANES] + turned
    arrive(weight_z)
    wadj_ref[...] = total(wz, outer)
    for copy in pending:
        copy.wait_send()


def square(
    paths_all, set_total,
    pb_hbm, w_hbm, not_hbm, set_hbm, tidx_hbm, level_hbm, rate_hbm,
    loss_ref, basis_ref, wadj_ref,
    not_ref, set_ref, tidx_ref, level_ref, rate_ref,
    pall, wall, small, dall, dgrid, dstack, dtri, dturn, table, invert,
    bown, bq, bzsend, bz, csend, cq, ssend, sq, lsend, lq, over_ref,
    tval, nsig, slopes,
    wsend, wvia, wnear, wjoin, wz, psend, pvia, pfar, pjoin, pq, esend, evia, ejoin, eq,
    local, send, recv,
):
    rows, feats = basis_ref.shape
    trades = wadj_ref.shape[0]
    quarter = set_total // 4
    me = lax.axis_index("paths")
    q, z = lax.rem(me, 4), lax.div(me, 4)
    peers = [me] + [partner(me, step, 16) for step in range(1, 16)]
    CORE, SIDE, NEAR, FAR = 1, 2, 4, 8
    trade_steps = (0, NEAR, SIDE, NEAR + SIDE)
    path_steps = (0, CORE, FAR, CORE + FAR)

    loads = [
        pltpu.make_async_copy(source, target, local.at[i])
        for i, (source, target) in enumerate(
            [
                (pb_hbm, pall.at[0]),
                (not_hbm, not_ref),
                (w_hbm, wall.at[0]),
                (set_hbm, set_ref),
                (tidx_hbm, tidx_ref),
                (level_hbm, level_ref),
                (rate_hbm, rate_ref),
            ]
        )
    ]
    barrier = pltpu.get_barrier_semaphore()
    for step in (CORE, SIDE, NEAR, FAR):
        pl.semaphore_signal(
            barrier, inc=1, device_id={"paths": peers[step]},
            device_id_type=pl.DeviceIdType.MESH,
        )
    for load in loads:
        load.start()

    copies = []

    def remote(source, target, step):
        k = len(copies)
        copy = pltpu.make_async_remote_copy(
            src_ref=source, dst_ref=target, send_sem=send.at[k], recv_sem=recv.at[k],
            device_id={"paths": peers[step]}, device_id_type=pl.DeviceIdType.MESH,
        )
        copies.append(copy)
        return copy

    def start(*group):
        for copy in group:
            copy.start()

    def arrive(*group):
        for copy in group:
            copy.wait_recv()

    def pieces(source, target, step, extent):
        part = extent // PIECES
        cuts = [pl.ds(p * part, part) for p in range(PIECES)]
        return [remote(source.at[cut], target.at[cut], step) for cut in cuts]

    def grouped(source, target, bits):
        return [remote(source(peers[s]), target, s) for s in bits]

    def place(i):
        design = design_of(pall[i])
        at = slice(i * rows, (i + 1) * rows)
        dtri[at, :] = triple(design)
        turned = jnp.transpose(design)[:REGRESSORS, :].astype(BF16)
        dturn[:, at] = turned
        return turned

    loads[0].wait()
    own_turned = place(0)
    loads[1].wait()
    note = jnp.broadcast_to(not_ref[...].astype(F32), (16, trades)).astype(BF16)
    small[0] = jnp.concatenate([own_turned, note], axis=0)
    loads[2].wait()
    pl.semaphore_wait(barrier, 4)

    small_near = remote(small.at[0], small.at[1], NEAR)
    small_side = remote(small.at[0], small.at[2], SIDE)
    trade_near = pieces(wall.at[0], wall.at[1], NEAR, trades)
    path_core = remote(pall.at[0], pall.at[1], CORE)
    trade_side = remote(wall.at[0], wall.at[2], SIDE)
    path_far = pieces(pall.at[0], pall.at[2], FAR, rows)
    start(small_near, small_side, *trade_near, path_core, trade_side, *path_far)
    small_pass = remote(small.at[1], small.at[3], SIDE)
    trade_pass = pieces(wall.at[1], wall.at[3], SIDE, trades)
    path_pass = pieces(pall.at[2], pall.at[3], CORE, rows)
    front = pl.ds(0, REGRESSORS)
    design_core = remote(small.at[:, front], dall.at[0], CORE)
    design_far = remote(small.at[:, front], dall.at[1], FAR)
    design_pass = remote(dall.at[1], dall.at[2], CORE)

    for load in loads[3:]:
        load.wait()
    labels = jnp.concatenate([set_ref[pl.ds(peers[s], 1), :] for s in trade_steps], axis=1)
    table[...] = set_table(labels, set_total)

    def value(first, last, left, right):
        paths = pall[first:last].reshape((last - first) * rows, feats)
        weights = wall[left:right].reshape((right - left) * trades, feats)
        notional = jnp.concatenate(
            [small[s, REGRESSORS:, :].astype(F32)[:1, :] for s in range(left, right)], axis=1
        )
        pre_act = mm(paths, weights, NT)
        fade = jnp.exp(-jnp.abs(pre_act))
        at = (slice(first * rows, last * rows), slice(left * trades, right * trades))
        tval[at] = (notional * (jnp.maximum(pre_act, 0.0) + jnp.log1p(fade))).astype(BF16)
        nsig[at] = notional * (jnp.where(pre_act >= 0.0, 1.0, fade) / (1.0 + fade))

    arrive(small_near)
    start(small_pass)
    arrive(path_core)
    place(1)
    value(0, 2, 0, 1)
    for copy, onward in zip(trade_near, trade_pass):
        arrive(copy)
        start(onward)
    value(0, 2, 1, 2)
    arrive(small_side, small_pass)
    start(design_core, design_far)
    arrive(trade_side)
    value(0, 2, 2, 3)
    for copy, onward in zip(path_far, path_pass):
        arrive(copy)
        start(onward)
    place(2)
    value(2, 3, 0, 3)
    arrive(*trade_pass)
    value(0, 3, 3, 4)
    head = 3 * rows
    by_trade = mm(dturn[:, :head], tval[:head, :])
    arrive(design_far)
    start(design_pass)
    arrive(*path_pass)
    place(3)
    value(3, 4, 0, 4)
    by_trade = by_trade + mm(dturn[:, head:], tval[head:, :])
    by_set = mm(jnp.concatenate(split3(by_trade), axis=0), table[...], NT)
    moments = (
        by_set[:REGRESSORS] + by_set[REGRESSORS : 2 * REGRESSORS] + by_set[2 * REGRESSORS :]
    )
    for i in range(4):
        bown[i] = moments[:, i * quarter : (i + 1) * quarter]
    quads = (CORE + SIDE, SIDE, CORE)
    lines = (NEAR + FAR, FAR, NEAR)

    def total(ref, count):
        result = ref[0].astype(F32)
        for i in range(1, count):
            result = result + ref[i].astype(F32)
        return result

    moment_q = grouped(lambda peer: bown.at[lax.rem(peer, 4)], bq.at[q], quads)
    start(*moment_q)
    bq[q] = bown[q]

    arrive(design_core, design_pass)
    for s in range(4):
        dgrid[peers[trade_steps[s]]] = small[s, :REGRESSORS, :]
    for k in range(1, 4):
        for s in range(4):
            dgrid[peers[trade_steps[s] + path_steps[k]]] = dall[k - 1, s]
    turned_all = jnp.concatenate([dgrid[i] for i in range(16)], axis=1)
    dstack[...] = jnp.concatenate(
        [turned_all, turned_all, turned_all, jnp.zeros_like(turned_all)], axis=0
    )
    gram = mm(turned_all, turned_all, NT)
    gram = jnp.concatenate([gram, jnp.zeros((REGRESSORS, LANES - REGRESSORS), F32)], axis=1)
    gram_row = lax.broadcasted_iota(jnp.int32, (REGRESSORS, LANES), 0)
    gram_lane = lax.broadcasted_iota(jnp.int32, (REGRESSORS, LANES), 1)
    ridge = jnp.where(gram_row == gram_lane, RIDGE_SCALE * paths_all, 0.0)
    work = eliminate(augmented(gram + ridge), 0, FIRST_STEPS)

    arrive(*moment_q)
    bzsend[...] = total(bq, 4)
    moment_z = grouped(lambda peer: bzsend, bz.at[z], lines)
    start(*moment_z)
    bz[z] = bzsend[...]
    work = eliminate(work, FIRST_STEPS, REGRESSORS)
    invert[...] = pltpu.roll(work, LANES - REGRESSORS, 1)
    all_levels = tidx_ref[...]
    all_thresholds = jnp.zeros((4, quarter), F32)
    levels = tidx_ref[pl.ds(q, 1), :]
    thresholds = jnp.zeros((1, quarter), F32)
    for i in range(level_ref.shape[0]):
        thresholds = jnp.where(levels == i, level_ref[i], thresholds)
        all_thresholds = jnp.where(all_levels == i, level_ref[i], all_thresholds)
    thresholds = jnp.transpose(jnp.broadcast_to(thresholds, (quarter, quarter)))[:, :1]
    rate = jnp.transpose(
        jnp.broadcast_to(rate_ref[pl.ds(q, 1), :], (quarter, quarter))
    )[:, :1]
    all_rates = rate_ref[...]
    full_thresholds = jnp.concatenate([all_thresholds[i : i + 1] for i in range(4)], axis=1)
    full_rates = jnp.concatenate([all_rates[i : i + 1] for i in range(4)], axis=1)

    arrive(*moment_z)
    inverse = invert[:, :REGRESSORS]
    coeffs = precise(inverse, total(bz, 4))
    csend[...] = coeffs
    coeffs_q = grouped(lambda peer: csend, cq.at[q], quads)
    start(*coeffs_q)
    cq[q] = coeffs
    excess = mm(stack3(coeffs), dstack[...], TN) - thresholds
    over_ref[...] = excess
    fade = jnp.exp(-jnp.abs(excess))
    seed = rate * (jnp.where(excess >= 0.0, 1.0, fade) / (1.0 + fade))
    seed_cut = mm(dstack[:REGRESSORS, :], jnp.concatenate(split3(seed), axis=0), NT)
    seed_sum = (
        seed_cut[:, :quarter] + seed_cut[:, quarter : 2 * quarter] + seed_cut[:, 2 * quarter :]
    )
    solved = precise(inverse, seed_sum)
    ssend[...] = solved
    answer_q = grouped(lambda peer: ssend, sq.at[q], quads)
    start(*answer_q)
    sq[q] = solved

    excess = over_ref[...]
    loss = jnp.maximum(excess, 0.0) + jnp.log1p(jnp.exp(-jnp.abs(excess)))
    loss_part = jnp.sum(rate * jnp.sum(loss, axis=1, keepdims=True), axis=0, keepdims=True)
    lsend[...] = jnp.broadcast_to(loss_part, lsend.shape)
    lq[q] = lsend[...]
    loss_q = grouped(lambda peer: lsend, lq.at[q], quads)

    arrive(*coeffs_q)
    own_triple = dtri[:rows, :]
    coeffs_all = jnp.concatenate([cq[i] for i in range(4)], axis=1)
    fitted = mm(own_triple, stack3(coeffs_all))
    over = fitted - full_thresholds
    fall = jnp.exp(-jnp.abs(over))
    own_seed = full_rates * (jnp.where(over >= 0.0, 1.0, fall) / (1.0 + fall))

    arrive(*answer_q)
    solved_all = jnp.concatenate([sq[i] for i in range(4)], axis=1)
    picked = mm(jnp.concatenate(split3(solved_all), axis=0), table[...])
    solved3 = jnp.concatenate(
        [picked.astype(BF16), jnp.zeros((LANES - 3 * REGRESSORS, picked.shape[1]), BF16)], axis=0
    )
    spread = mm(dtri[...], solved3).astype(BF16).astype(F32)
    slopes[...] = (nsig[...] * spread).astype(BF16)

    scale = 1.0 / math.sqrt(paths_all)

    def basis_part(first, last):
        return mm(slopes[first * rows : last * rows, :], wall[...].reshape(4 * trades, feats))

    def weight_part(left, right):
        cut = slopes[:, left * trades : right * trades]
        return mm(cut, pall[...].reshape(4 * rows, feats), TN) * scale

    psend[0] = basis_part(3, 4).astype(BF16)
    basis_via = pieces(psend.at[0], pvia, CORE, rows)
    start(*basis_via)
    part = weight_part(2, 4)
    wsend[0] = part[trades:].astype(BF16)
    weight_via = pieces(wsend.at[0], wvia, SIDE, trades)
    start(*weight_via)
    wsend[1] = part[:trades].astype(BF16)
    weight_side = remote(wsend.at[1], wz.at[0], SIDE)
    start(weight_side)
    part = basis_part(1, 3)
    psend[1] = part[:rows].astype(BF16)
    basis_core = remote(psend.at[1], pq.at[0], CORE)
    start(basis_core)
    pfar[...] = part[rows:]
    basis_far = pieces(pjoin, pq.at[1], FAR, rows)
    for p, (copy, onward) in enumerate(zip(basis_via, basis_far)):
        cut = slice(p * rows // PIECES, (p + 1) * rows // PIECES)
        arrive(copy)
        pjoin[cut, :] = (pfar[cut, :] + pvia[cut, :].astype(F32)).astype(BF16)
        start(onward)
    wnear[...] = weight_part(1, 2)
    pulled = mm(solved3, tval[...], NT)
    pulled = (
        pulled[:REGRESSORS]
        + pulled[REGRESSORS : 2 * REGRESSORS]
        + pulled[2 * REGRESSORS : 3 * REGRESSORS]
    )
    esend[0] = pulled[:, 3 * rows :]
    esend[1] = pulled[:, rows : 2 * rows]
    pull_via = remote(esend.at[0], evia, CORE)
    pull_core = remote(esend.at[1], eq.at[0], CORE)
    pull_far = remote(ejoin, eq.at[1], FAR)
    start(pull_via, pull_core, *loss_q)
    weight_near = pieces(wjoin, wz.at[1], NEAR, trades)
    for p, (copy, onward) in enumerate(zip(weight_via, weight_near)):
        cut = slice(p * trades // PIECES, (p + 1) * trades // PIECES)
        arrive(copy)
        wjoin[cut, :] = (wnear[cut, :] + wvia[cut, :].astype(F32)).astype(BF16)
        start(onward)
        if p == 0:
            arrive(pull_via)
            ejoin[...] = pulled[:, 2 * rows : 3 * rows] + evia[...]
            start(pull_far)
    wadj_ref[...] = weight_part(0, 1)
    basis_ref[...] = basis_part(0, 1)

    residual = own_seed - mm(own_triple, stack3(solved_all))
    term = precise(coeffs_all, residual, NT) - precise(solved_all, fitted, NT)
    arrive(*loss_q)
    answers = jnp.concatenate([lq[i] for i in range(4)], axis=1)
    loss_sum = jnp.sum(answers[:1], axis=1, keepdims=True) / quarter
    loss_ref[...] = jnp.broadcast_to(loss_sum / (paths_all * set_total), loss_ref.shape)
    arrive(pull_core, pull_far)
    term = term + pulled[:, :rows] + eq[0] + eq[1]
    padded = jnp.concatenate([term, jnp.zeros((LANES - REGRESSORS, rows), F32)], axis=0)
    turned = pltpu.roll(jnp.transpose(padded), LANES - 1, 1)
    lane = lax.broadcasted_iota(jnp.int32, turned.shape, 1)
    turned = jnp.where(lane < REGRESSORS - 1, turned, 0.0)
    basis_ref[:, :LANES] = basis_ref[:, :LANES] + turned
    arrive(basis_core, *basis_far)
    basis_ref[...] = basis_ref[...] + (pq[0].astype(F32) + pq[1].astype(F32))
    arrive(weight_side, *weight_near)
    wadj_ref[...] = wadj_ref[...] + (wz[0].astype(F32) + wz[1].astype(F32))
    for copy in copies:
        copy.wait_send()


def square_scratch(rows, trades, feats, set_total):
    size, quarter = REGRESSORS, set_total // 4
    return [
        pltpu.VMEM((4, rows, feats), BF16),
        pltpu.VMEM((4, trades, feats), BF16),
        pltpu.VMEM((4, size + 16, trades), BF16),
        pltpu.VMEM((3, 4, size, rows), BF16),
        pltpu.VMEM((16, size, rows), BF16),
        pltpu.VMEM((LANES, 16 * rows), BF16),
        pltpu.VMEM((4 * rows, LANES), BF16),
        pltpu.VMEM((size, 4 * rows), BF16),
        pltpu.VMEM((set_total, 4 * trades), BF16),
        pltpu.VMEM((size, LANES), F32),
        pltpu.VMEM((4, size, quarter), F32),
        pltpu.VMEM((4, size, quarter), F32),
        pltpu.VMEM((size, quarter), F32),
        pltpu.VMEM((4, size, quarter), F32),
        pltpu.VMEM((size, quarter), F32),
        pltpu.VMEM((4, size, quarter), F32),
        pltpu.VMEM((size, quarter), F32),
        pltpu.VMEM((4, size, quarter), F32),
        pltpu.VMEM((8, quarter), F32),
        pltpu.VMEM((4, 8, quarter), F32),
        pltpu.VMEM((quarter, 16 * rows), F32),
        pltpu.VMEM((4 * rows, 4 * trades), BF16),
        pltpu.VMEM((4 * rows, 4 * trades), F32),
        pltpu.VMEM((4 * rows, 4 * trades), BF16),
        pltpu.VMEM((2, trades, feats), BF16),
        pltpu.VMEM((trades, feats), BF16),
        pltpu.VMEM((trades, feats), F32),
        pltpu.VMEM((trades, feats), BF16),
        pltpu.VMEM((2, trades, feats), BF16),
        pltpu.VMEM((2, rows, feats), BF16),
        pltpu.VMEM((rows, feats), BF16),
        pltpu.VMEM((rows, feats), F32),
        pltpu.VMEM((rows, feats), BF16),
        pltpu.VMEM((2, rows, feats), BF16),
        pltpu.VMEM((2, size, rows), F32),
        pltpu.VMEM((size, rows), F32),
        pltpu.VMEM((size, rows), F32),
        pltpu.VMEM((2, size, rows), F32),
        pltpu.SemaphoreType.DMA((7,)),
        pltpu.SemaphoreType.DMA((COPIES,)),
        pltpu.SemaphoreType.DMA((COPIES,)),
    ]


def chain_scratch(inner, outer, rows, trades, feats, set_total):
    size, quarter, count = REGRESSORS, set_total // inner, inner * outer
    z_pairs, q_pairs = max(outer - 1, 1), max(inner - 1, 1)
    return [
        pltpu.VMEM((inner, rows, feats), BF16),
        pltpu.VMEM((outer, trades, feats), BF16),
        pltpu.VMEM((outer, 8, trades), F32),
        pltpu.VMEM((8, trades), F32),
        pltpu.VMEM((size, rows), BF16),
        pltpu.VMEM((outer, size, rows), BF16),
        pltpu.VMEM((inner, outer, size, rows), BF16),
        pltpu.VMEM((LANES, count * rows), BF16),
        pltpu.VMEM((set_total, outer * trades), BF16),
        pltpu.VMEM((size, LANES), F32),
        pltpu.VMEM((inner, size, quarter), F32),
        pltpu.VMEM((inner, size, quarter), F32),
        pltpu.VMEM((size, quarter), F32),
        pltpu.VMEM((outer, size, quarter), F32),
        pltpu.VMEM((size, quarter), F32),
        pltpu.VMEM((inner, size, quarter), F32),
        pltpu.VMEM((size + 8, quarter), F32),
        pltpu.VMEM((inner, size + 8, quarter), F32),
        pltpu.VMEM((inner, size, rows), F32),
        pltpu.VMEM((inner, size, rows), F32),
        pltpu.VMEM((outer, trades, feats), BF16),
        pltpu.VMEM((outer, trades, feats), BF16),
        pltpu.VMEM((inner, rows, feats), BF16),
        pltpu.VMEM((inner, rows, feats), BF16),
        pltpu.VMEM((inner * rows, outer * trades), F32),
        pltpu.VMEM((inner * rows, outer * trades), BF16),
        pltpu.SemaphoreType.DMA((7,)),
        pltpu.SemaphoreType.DMA((5, z_pairs)),
        pltpu.SemaphoreType.DMA((5, z_pairs)),
        pltpu.SemaphoreType.DMA((7, q_pairs)),
        pltpu.SemaphoreType.DMA((7, q_pairs)),
    ]


def shards(
    path_basis, proxy_weight, notional, set_of, threshold_index, threshold_levels, loss_rate
):
    count = lax.axis_size("paths")
    inner = math.gcd(4, count)
    outer = count // inner
    rows, feats = path_basis.shape
    trades = proxy_weight.shape[0]
    set_total = loss_rate.shape[0]
    quarter = set_total // inner
    vmem = pl.BlockSpec(memory_space=pltpu.VMEM)
    if count == 16 and rows == trades and rows % (16 * PIECES) == 0:
        body = functools.partial(square, rows * count, set_total)
        scratch = square_scratch(rows, trades, feats, set_total)
    else:
        body = functools.partial(kernel, inner, outer, rows * count, set_total)
        scratch = chain_scratch(inner, outer, rows, trades, feats, set_total)
    loss, basis_adjoint, weight_adjoint = pl.pallas_call(
        body,
        out_shape=(
            jax.ShapeDtypeStruct((1, LANES), F32),
            jax.ShapeDtypeStruct((rows, feats), F32),
            jax.ShapeDtypeStruct((trades, feats), F32),
        ),
        in_specs=[pl.BlockSpec(memory_space=pltpu.HBM)] * 7,
        out_specs=(vmem, vmem, vmem),
        scratch_shapes=[
            pltpu.VMEM((1, trades), BF16),
            pltpu.VMEM((inner * outer, trades), jnp.int32),
            pltpu.VMEM((inner, quarter), jnp.int32),
            pltpu.SMEM(threshold_levels.shape, F32),
            pltpu.VMEM((inner, quarter), F32),
            *scratch,
        ],
        compiler_params=pltpu.CompilerParams(
            collective_id=0, has_side_effects=True, vmem_limit_bytes=48 * 1024 * 1024
        ),
    )(
        *(
            pltpu.with_memory_space_constraint(operand, pltpu.HBM)
            for operand in (
                path_basis,
                proxy_weight,
                notional.reshape(1, trades),
                set_of.reshape(-1, trades),
                threshold_index.reshape(inner, quarter),
                threshold_levels,
                loss_rate.reshape(inner, quarter),
            )
        )
    )
    return loss[0, :1], basis_adjoint, weight_adjoint


def solution(mesh):
    placed = (
        P(("groups", "paths"), None),
        P(("groups", "paths"), None),
        P(("groups", "paths")),
        P("groups"),
        P("groups"),
        P("groups"),
        P("groups"),
    )
    return jax.shard_map(
        shards,
        mesh=mesh,
        in_specs=placed,
        out_specs=(P("groups"), P(("groups", "paths"), None), P(("groups", "paths"), None)),
        check_vma=False,
    )
```

```python
import functools
import math

import jax
import jax.numpy as jnp
from jax import lax
from jax.experimental import pallas as pl
from jax.experimental.pallas import tpu as pltpu
from jax.sharding import PartitionSpec as P

REGRESSORS = 32
RIDGE_SCALE = 0.01
PRECISE = lax.Precision.HIGHEST
LANES = 128
PIECES = 4
FIRST_STEPS = 10
COPIES = 64
F32 = jnp.float32
BF16 = jnp.bfloat16

NN = (((1,), (0,)), ((), ()))
NT = (((1,), (1,)), ((), ()))
TN = (((0,), (0,)), ((), ()))


def mm(a, b, dims=NN):
    return lax.dot_general(a, b, dims, preferred_element_type=F32)


def precise(a, b, dims=NN):
    return lax.dot_general(a, b, dims, precision=PRECISE, preferred_element_type=F32)


def split3(x):
    hi = x.astype(BF16)
    rest = x - hi.astype(F32)
    mid = rest.astype(BF16)
    lo = (rest - mid.astype(F32)).astype(BF16)
    return hi, mid, lo


def stack3(x):
    hi, mid, lo = split3(x)
    return jnp.concatenate([hi, mid, lo, jnp.zeros_like(hi)], axis=0)


def design_of(basis):
    front = pltpu.roll(basis[:, :LANES].astype(F32), 1, 1)
    lane = lax.broadcasted_iota(jnp.int32, front.shape, 1)
    return jnp.where(lane == 0, 1.0, jnp.where(lane < REGRESSORS, front, 0.0))


def triple(design):
    return (
        design + pltpu.roll(design, REGRESSORS, 1) + pltpu.roll(design, 2 * REGRESSORS, 1)
    ).astype(BF16)


def augmented(gram):
    row = lax.broadcasted_iota(jnp.int32, gram.shape, 0)
    lane = lax.broadcasted_iota(jnp.int32, gram.shape, 1)
    return jnp.where(lane < REGRESSORS, gram, jnp.where(lane == row + REGRESSORS, 1.0, 0.0))


def eliminate(work, first, last):
    row = lax.broadcasted_iota(jnp.int32, work.shape, 0)
    for k in range(first, last):
        column = jnp.broadcast_to(work[:, k : k + 1], work.shape)
        pivot = work[k : k + 1, :] / column[k : k + 1, :]
        work = jnp.where(row == k, pivot, work - column * pivot)
    return work


def spd_inverse(gram):
    work = eliminate(augmented(gram), 0, REGRESSORS)
    return pltpu.roll(work, LANES - REGRESSORS, 1)


def set_table(labels, set_total):
    sets = lax.broadcasted_iota(jnp.int32, (set_total, labels.shape[1]), 0)
    return jnp.where(sets == labels, 1.0, 0.0).astype(BF16)


def partner(index, step, count):
    if count & (count - 1):
        return lax.rem(index + step, count)
    result, weight = 0, 1
    while weight < count:
        bit = lax.rem(lax.div(index, weight), 2)
        result = result + weight * (1 - bit if step & weight else bit)
        weight *= 2
    return result


def kernel(
    inner, outer, paths_all, set_total,
    pb_hbm, w_hbm, not_hbm, set_hbm, tidx_hbm, level_hbm, rate_hbm,
    loss_ref, basis_ref, wadj_ref,
    not_ref, set_ref, tidx_ref, level_ref, rate_ref,
    pall, wall, nall, nsend, gown, gall, gq, dstack, table, invert,
    bown, bq, bzsend, bz, csend, cq, ssend, sq,
    eown, eq, wown, wz, pown, pq, nsig, tval,
    local, zsend, zrecv, qsend, qrecv,
):
    rows, feats = basis_ref.shape
    trades = wadj_ref.shape[0]
    quarter = set_total // inner
    me = lax.axis_index("paths")
    q = lax.rem(me, inner)
    z = lax.div(me, inner)

    loads = [
        pltpu.make_async_copy(source, target, local.at[i])
        for i, (source, target) in enumerate(
            [
                (pb_hbm, pall.at[q]),
                (not_hbm, not_ref),
                (w_hbm, wall.at[z]),
                (set_hbm, set_ref),
                (tidx_hbm, tidx_ref),
                (level_hbm, level_ref),
                (rate_hbm, rate_ref),
            ]
        )
    ]
    for load in loads:
        load.start()

    barrier = pltpu.get_barrier_semaphore()
    for d in range(1, inner):
        pl.semaphore_signal(
            barrier, inc=1, device_id={"paths": z * inner + lax.rem(q + d, inner)},
            device_id_type=pl.DeviceIdType.MESH,
        )
    for d in range(1, outer):
        pl.semaphore_signal(
            barrier, inc=1, device_id={"paths": lax.rem(z + d, outer) * inner + q},
            device_id_type=pl.DeviceIdType.MESH,
        )

    pending = []

    def over_q(which, source, target):
        copies = []
        for d in range(inner - 1, 0, -1):
            peer = partner(q, d, inner)
            copy = pltpu.make_async_remote_copy(
                src_ref=source(peer), dst_ref=target.at[q],
                send_sem=qsend.at[which, d - 1], recv_sem=qrecv.at[which, d - 1],
                device_id={"paths": z * inner + peer},
                device_id_type=pl.DeviceIdType.MESH,
            )
            copy.start()
            copies.append(copy)
        pending.extend(copies)
        return copies

    def over_z(which, source, target):
        copies = []
        for d in range(outer - 1, 0, -1):
            peer = partner(z, d, outer)
            copy = pltpu.make_async_remote_copy(
                src_ref=source(peer), dst_ref=target.at[z],
                send_sem=zsend.at[which, d - 1], recv_sem=zrecv.at[which, d - 1],
                device_id={"paths": peer * inner + q},
                device_id_type=pl.DeviceIdType.MESH,
            )
            copy.start()
            copies.append(copy)
        pending.extend(copies)
        return copies

    def arrive(copies):
        for copy in copies:
            copy.wait_recv()

    def total(ref, count):
        result = ref[0].astype(F32)
        for i in range(1, count):
            result = result + ref[i].astype(F32)
        return result

    loads[0].wait()
    own_design = design_of(pall[q])
    own_triple = triple(own_design)
    own_turned = jnp.transpose(own_design)[:REGRESSORS, :].astype(BF16)
    gown[...] = own_turned
    loads[1].wait()
    nrow = jnp.broadcast_to(not_ref[...].astype(F32), (8, trades))
    nsend[...] = nrow
    loads[2].wait()
    pl.semaphore_wait(barrier, inner + outer - 2)

    gram_z = over_z(0, lambda peer: gown, gall)
    note_z = over_z(1, lambda peer: nsend, nall)
    trade_z = over_z(2, lambda peer: wall.at[z], wall)
    path_q = over_q(0, lambda peer: pall.at[q], pall)
    gall[z] = own_turned
    nall[z] = nrow

    arrive(gram_z)
    gram_q = over_q(1, lambda peer: gall, gq)
    gq[q] = gall[...]

    for load in loads[3:]:
        load.wait()
    all_levels = tidx_ref[...]
    all_thresholds = jnp.zeros((inner, quarter), F32)
    levels = tidx_ref[pl.ds(q, 1), :]
    thresholds = jnp.zeros((1, quarter), F32)
    for i in range(level_ref.shape[0]):
        thresholds = jnp.where(levels == i, level_ref[i], thresholds)
        all_thresholds = jnp.where(all_levels == i, level_ref[i], all_thresholds)
    thresholds = jnp.transpose(jnp.broadcast_to(thresholds, (quarter, quarter)))[:, :1]
    rate = jnp.transpose(
        jnp.broadcast_to(rate_ref[pl.ds(q, 1), :], (quarter, quarter))
    )[:, :1]
    all_rates = rate_ref[...]
    labels = jnp.concatenate(
        [set_ref[pl.ds(i * inner + q, 1), :] for i in range(outer)], axis=1
    )
    table[...] = set_table(labels, set_total)

    arrive(path_q)
    paths = pall[...].reshape(inner * rows, feats)
    design = design_of(paths)
    design3 = triple(design)
    design_t = jnp.transpose(design)[:REGRESSORS, :].astype(BF16)

    arrive(gram_q)
    turned_all = jnp.concatenate(
        [gq[i, j] for i in range(inner) for j in range(outer)], axis=1
    )
    dstack[...] = jnp.concatenate(
        [turned_all, turned_all, turned_all, jnp.zeros_like(turned_all)], axis=0
    )
    gram = mm(turned_all, dstack[...], NT)
    gram_row = lax.broadcasted_iota(jnp.int32, (REGRESSORS, LANES), 0)
    gram_lane = lax.broadcasted_iota(jnp.int32, (REGRESSORS, LANES), 1)
    ridge = jnp.where(gram_row == gram_lane, RIDGE_SCALE * paths_all, 0.0)
    invert[...] = spd_inverse(gram + ridge)

    arrive(note_z)
    notional = jnp.concatenate([nall[i][0:1, :] for i in range(outer)], axis=1)
    arrive(trade_z)
    weights = wall[...].reshape(outer * trades, feats)
    pre_act = mm(paths, weights, NT)
    small = jnp.exp(-jnp.abs(pre_act))
    tval[...] = (notional * (jnp.maximum(pre_act, 0.0) + jnp.log1p(small))).astype(BF16)
    nsig[...] = notional * (jnp.where(pre_act >= 0.0, 1.0, small) / (1.0 + small))

    by_trade = mm(design_t, tval[...])
    by_set = mm(jnp.concatenate(split3(by_trade), axis=0), table[...], NT)
    moments = (
        by_set[:REGRESSORS] + by_set[REGRESSORS : 2 * REGRESSORS] + by_set[2 * REGRESSORS :]
    )
    for i in range(inner):
        bown[i] = moments[:, i * quarter : (i + 1) * quarter]
    moment_q = over_q(2, lambda peer: bown.at[peer], bq)
    bq[q] = bown[q]
    arrive(moment_q)
    moment_mid = total(bq, inner)
    bzsend[...] = moment_mid
    moment_z = over_z(3, lambda peer: bzsend, bz)
    bz[z] = moment_mid
    arrive(moment_z)
    inverse = invert[:, :REGRESSORS]
    coeffs = precise(inverse, total(bz, outer))
    csend[...] = coeffs
    coeffs_q = over_q(3, lambda peer: csend, cq)
    cq[q] = coeffs
    excess = mm(stack3(coeffs), dstack[...], TN) - thresholds
    fade = jnp.exp(-jnp.abs(excess))
    loss = jnp.maximum(excess, 0.0) + jnp.log1p(fade)
    seed = rate * (jnp.where(excess >= 0.0, 1.0, fade) / (1.0 + fade))
    seed_cut = mm(dstack[:REGRESSORS, :], jnp.concatenate(split3(seed), axis=0), NT)
    seed_sum = (
        seed_cut[:, :quarter] + seed_cut[:, quarter : 2 * quarter] + seed_cut[:, 2 * quarter :]
    )
    solved = precise(inverse, seed_sum)
    loss_part = jnp.sum(rate * jnp.sum(loss, axis=1, keepdims=True), axis=0, keepdims=True)
    answer = jnp.concatenate([solved, jnp.broadcast_to(loss_part, (8, quarter))], axis=0)
    ssend[...] = answer
    answer_q = over_q(4, lambda peer: ssend, sq)
    sq[q] = answer
    arrive(coeffs_q)
    coeffs_all = jnp.concatenate([cq[i] for i in range(inner)], axis=1)
    arrive(answer_q)
    answers = jnp.concatenate([sq[i] for i in range(inner)], axis=1)
    solved_all = answers[:REGRESSORS]
    loss_sum = jnp.sum(answers[REGRESSORS : REGRESSORS + 1], axis=1, keepdims=True) / quarter
    loss_ref[...] = jnp.broadcast_to(loss_sum / (paths_all * set_total), loss_ref.shape)

    picked = mm(jnp.concatenate(split3(solved_all), axis=0), table[...])
    solved3 = jnp.concatenate(
        [picked.astype(BF16), jnp.zeros((LANES - 3 * REGRESSORS, picked.shape[1]), BF16)], axis=0
    )
    spread = mm(design3, solved3).astype(BF16).astype(F32)
    slopes = (nsig[...] * spread).astype(BF16)
    scale = 1.0 / math.sqrt(paths_all)
    weight_part = mm(slopes, paths, TN) * scale
    wown[...] = weight_part.astype(BF16).reshape(outer, trades, feats)
    weight_z = over_z(4, lambda peer: wown.at[peer], wz)
    wz[z] = wown[z]

    pulled = mm(solved3, tval[...], NT)
    pulled = (
        pulled[:REGRESSORS]
        + pulled[REGRESSORS : 2 * REGRESSORS]
        + pulled[2 * REGRESSORS : 3 * REGRESSORS]
    )
    for i in range(inner):
        eown[i] = pulled[:, i * rows : (i + 1) * rows]
    pull_q = over_q(5, lambda peer: eown.at[peer], eq)
    eq[q] = eown[q]
    basis_part = mm(slopes, weights)
    pown[...] = basis_part.astype(BF16).reshape(inner, rows, feats)
    basis_q = over_q(6, lambda peer: pown.at[peer], pq)
    pq[q] = pown[q]

    fitted = mm(own_triple, stack3(coeffs_all))
    full_thresholds = jnp.concatenate([all_thresholds[i : i + 1] for i in range(inner)], axis=1)
    full_rates = jnp.concatenate([all_rates[i : i + 1] for i in range(inner)], axis=1)
    over = fitted - full_thresholds
    tail = jnp.exp(-jnp.abs(over))
    own_seed = full_rates * (jnp.where(over >= 0.0, 1.0, tail) / (1.0 + tail))
    residual = own_seed - mm(own_triple, stack3(solved_all))
    term = precise(coeffs_all, residual, NT) - precise(solved_all, fitted, NT)
    arrive(pull_q)
    term = term + total(eq, inner)
    padded = jnp.concatenate([term, jnp.zeros((LANES - REGRESSORS, rows), F32)], axis=0)
    turned = pltpu.roll(jnp.transpose(padded), LANES - 1, 1)
    lane = lax.broadcasted_iota(jnp.int32, turned.shape, 1)
    turned = jnp.where(lane < REGRESSORS - 1, turned, 0.0)
    arrive(basis_q)
    basis_ref[...] = total(pq, inner)
    basis_ref[:, :LANES] = basis_ref[:, :LANES] + turned
    arrive(weight_z)
    wadj_ref[...] = total(wz, outer)
    for copy in pending:
        copy.wait_send()


def square(
    paths_all, set_total,
    pb_hbm, w_hbm, not_hbm, set_hbm, tidx_hbm, level_hbm, rate_hbm,
    loss_ref, basis_ref, wadj_ref,
    not_ref, set_ref, tidx_ref, level_ref, rate_ref,
    pall, wall, small, dall, dgrid, dstack, dtri, dturn, table, invert,
    bown, bq, bzsend, bz, csend, cq, ssend, sq, lsend, lq, over_ref,
    tval, nsig, slopes,
    wsend, wvia, wnear, wjoin, wz, psend, pvia, pfar, pjoin, pq, esend, evia, ejoin, eq,
    local, send, recv, ready, order,
):
    rows, feats = basis_ref.shape
    trades = wadj_ref.shape[0]
    quarter = set_total // 4
    me = lax.axis_index("paths")
    q, z = lax.rem(me, 4), lax.div(me, 4)
    bits = [lax.rem(lax.div(me, weight), 2) for weight in (1, 2, 4, 8)]
    peers = [me] + [partner(me, step, 16) for step in range(1, 16)]
    CORE, SIDE, NEAR, FAR = around = 1, 2, 4, 8
    trade_steps = (0, NEAR, SIDE, NEAR + SIDE)
    path_steps = (0, CORE, FAR, CORE + FAR)

    loads = [
        pltpu.make_async_copy(source, target, local.at[i])
        for i, (source, target) in enumerate(
            [
                (pb_hbm, pall.at[pl.ds(0 * rows, rows)]),
                (not_hbm, not_ref),
                (w_hbm, wall.at[0]),
                (set_hbm, set_ref),
                (tidx_hbm, tidx_ref),
                (level_hbm, level_ref),
                (rate_hbm, rate_ref),
            ]
        )
    ]
    barrier = pltpu.get_barrier_semaphore()

    def greet(semaphore, step):
        pl.semaphore_signal(
            semaphore, inc=1, device_id={"paths": peers[step]},
            device_id_type=pl.DeviceIdType.MESH,
        )

    for i, step in enumerate(around):

        @pl.when(bits[i] == 0)
        def _():
            greet(barrier, step)

    for load in loads:
        load.start()

    copies = []

    def remote(source, target, step):
        k = len(copies)
        copy = pltpu.make_async_remote_copy(
            src_ref=source, dst_ref=target, send_sem=send.at[k], recv_sem=recv.at[k],
            device_id={"paths": peers[step]}, device_id_type=pl.DeviceIdType.MESH,
        )
        copies.append(copy)
        return copy

    def start(*group):
        for copy in group:
            copy.start()

    def fence():
        pl.semaphore_signal(order, inc=1)
        pl.semaphore_wait(order, 1)

    def arrive(*group):
        for copy in group:
            copy.wait_recv()

    def pieces(source, target, step, extent):
        part = extent // PIECES
        cuts = [pl.ds(p * part, part) for p in range(PIECES)]
        return [remote(source.at[cut], target.at[cut], step) for cut in cuts]

    def grouped(source, target, bits):
        return [remote(source(peers[s]), target, s) for s in bits]

    def place(i):
        design = design_of(pall[i * rows : (i + 1) * rows, :])
        at = slice(i * rows, (i + 1) * rows)
        dtri[at, :] = triple(design)
        turned = jnp.transpose(design)[:REGRESSORS, :].astype(BF16)
        dturn[:, at] = turned
        return turned

    path_core = remote(pb_hbm, pall.at[pl.ds(1 * rows, rows)], CORE)
    trade_side = remote(w_hbm, wall.at[2], SIDE)
    trade_near = pieces(w_hbm, wall.at[1], NEAR, trades)
    path_far = pieces(pb_hbm, pall.at[pl.ds(2 * rows, rows)], FAR, rows)
    small_side = remote(small.at[0], small.at[2], SIDE)
    small_near = remote(small.at[0], small.at[1], NEAR)

    lower = bits[0] + bits[1] + bits[2] + bits[3]

    @pl.when(lower > 0)
    def _():
        pl.semaphore_wait(barrier, lower)

    for i, step in enumerate(around):

        @pl.when(bits[i] == 1)
        def _():
            greet(ready.at[i], step)

    def down(i, *group):
        @pl.when(bits[i] == 1)
        def _():
            start(*group)

    def up(i, *group):
        @pl.when(bits[i] == 0)
        def _():
            pl.semaphore_wait(ready.at[i], 1)
            start(*group)

    down(2, *trade_near)
    down(1, trade_side)
    down(0, path_core)
    loads[0].wait()
    own_turned = place(0)
    loads[1].wait()
    note = jnp.broadcast_to(not_ref[...].astype(F32), (16, trades)).astype(BF16)
    small[0] = jnp.concatenate([own_turned, note], axis=0)
    up(0, path_core)
    up(1, trade_side)
    start(small_side)
    up(2, *trade_near)
    start(small_near)
    up(3)
    loads[2].wait()
    small_pass = remote(small.at[1], small.at[3], SIDE)
    trade_pass = pieces(wall.at[1], wall.at[3], SIDE, trades)
    path_pass = pieces(pall.at[pl.ds(2 * rows, rows)], pall.at[pl.ds(3 * rows, rows)], CORE, rows)
    front = pl.ds(0, REGRESSORS)
    design_core = remote(small.at[:, front], dall.at[0], CORE)
    design_far = remote(small.at[:, front], dall.at[1], FAR)
    design_pass = remote(dall.at[1], dall.at[2], CORE)

    for load in loads[3:]:
        load.wait()
    labels = jnp.concatenate([set_ref[pl.ds(peers[s], 1), :] for s in trade_steps], axis=1)
    table[...] = set_table(labels, set_total)

    def value(top, bottom, left, right):
        paths = pall[top:bottom, :]
        weights = wall[left:right].reshape((right - left) * trades, feats)
        notional = jnp.concatenate(
            [small[s, REGRESSORS:, :].astype(F32)[:1, :] for s in range(left, right)], axis=1
        )
        pre_act = mm(paths, weights, NT)
        fade = jnp.exp(-jnp.abs(pre_act))
        at = (slice(top, bottom), slice(left * trades, right * trades))
        tval[at] = (notional * (jnp.maximum(pre_act, 0.0) + jnp.log1p(fade))).astype(BF16)
        nsig[at] = notional * (jnp.where(pre_act >= 0.0, 1.0, fade) / (1.0 + fade))

    pair, head = 2 * rows, 3 * rows
    arrive(path_core)
    place(1)
    for p, (copy, onward) in enumerate(zip(trade_near, trade_pass)):
        arrive(copy)
        start(onward)
        if p == 0:
            start(*path_far)
    arrive(small_near)
    start(small_pass)
    greet(ready.at[4], FAR)
    arrive(trade_side, small_side)
    value(0, pair, 0, 3)
    for copy, onward in zip(path_far, path_pass):
        arrive(copy)
        start(onward)
    fence()
    place(2)
    value(pair, head, 0, 3)
    arrive(small_pass)
    start(design_core, design_far)
    fence()
    arrive(*trade_pass)
    value(0, head, 3, 4)
    by_trade = mm(dturn[:, :head], tval[:head, :])
    arrive(*path_pass)
    place(3)
    value(head, 4 * rows, 0, 4)
    by_trade = by_trade + mm(dturn[:, head:], tval[head:, :])
    by_set = mm(jnp.concatenate(split3(by_trade), axis=0), table[...], NT)
    moments = (
        by_set[:REGRESSORS] + by_set[REGRESSORS : 2 * REGRESSORS] + by_set[2 * REGRESSORS :]
    )
    for i in range(4):
        bown[i] = moments[:, i * quarter : (i + 1) * quarter]
    quads = (CORE + SIDE, SIDE, CORE)
    lines = (NEAR + FAR, FAR, NEAR)

    def total(ref, count):
        result = ref[0].astype(F32)
        for i in range(1, count):
            result = result + ref[i].astype(F32)
        return result

    moment_q = grouped(lambda peer: bown.at[lax.rem(peer, 4)], bq.at[q], quads)
    start(*moment_q)
    fence()
    bq[q] = bown[q]

    arrive(design_far)
    start(design_pass)
    fence()
    arrive(design_core, design_pass)
    for s in range(4):
        dgrid[peers[trade_steps[s]]] = small[s, :REGRESSORS, :]
    for k in range(1, 4):
        for s in range(4):
            dgrid[peers[trade_steps[s] + path_steps[k]]] = dall[k - 1, s]
    turned_all = jnp.concatenate([dgrid[i] for i in range(16)], axis=1)
    dstack[...] = jnp.concatenate(
        [turned_all, turned_all, turned_all, jnp.zeros_like(turned_all)], axis=0
    )
    gram = mm(turned_all, turned_all, NT)
    gram = jnp.concatenate([gram, jnp.zeros((REGRESSORS, LANES - REGRESSORS), F32)], axis=1)
    gram_row = lax.broadcasted_iota(jnp.int32, (REGRESSORS, LANES), 0)
    gram_lane = lax.broadcasted_iota(jnp.int32, (REGRESSORS, LANES), 1)
    ridge = jnp.where(gram_row == gram_lane, RIDGE_SCALE * paths_all, 0.0)
    work = eliminate(augmented(gram + ridge), 0, FIRST_STEPS)

    arrive(*moment_q)
    bzsend[...] = total(bq, 4)
    pl.semaphore_wait(ready.at[4], 1)
    moment_z = grouped(lambda peer: bzsend, bz.at[z], lines)
    start(*moment_z)
    fence()
    bz[z] = bzsend[...]
    work = eliminate(work, FIRST_STEPS, REGRESSORS)
    invert[...] = pltpu.roll(work, LANES - REGRESSORS, 1)
    all_levels = tidx_ref[...]
    all_thresholds = jnp.zeros((4, quarter), F32)
    levels = tidx_ref[pl.ds(q, 1), :]
    thresholds = jnp.zeros((1, quarter), F32)
    for i in range(level_ref.shape[0]):
        thresholds = jnp.where(levels == i, level_ref[i], thresholds)
        all_thresholds = jnp.where(all_levels == i, level_ref[i], all_thresholds)
    thresholds = jnp.transpose(jnp.broadcast_to(thresholds, (quarter, quarter)))[:, :1]
    rate = jnp.transpose(
        jnp.broadcast_to(rate_ref[pl.ds(q, 1), :], (quarter, quarter))
    )[:, :1]
    all_rates = rate_ref[...]
    full_thresholds = jnp.concatenate([all_thresholds[i : i + 1] for i in range(4)], axis=1)
    full_rates = jnp.concatenate([all_rates[i : i + 1] for i in range(4)], axis=1)

    arrive(*moment_z)
    inverse = invert[:, :REGRESSORS]
    coeffs = precise(inverse, total(bz, 4))
    csend[...] = coeffs
    coeffs_q = grouped(lambda peer: csend, cq.at[q], quads)
    cq[q] = coeffs
    excess = mm(stack3(coeffs), dstack[...], TN) - thresholds
    over_ref[...] = excess
    fade = jnp.exp(-jnp.abs(excess))
    seed = rate * (jnp.where(excess >= 0.0, 1.0, fade) / (1.0 + fade))
    seed_cut = mm(dstack[:REGRESSORS, :], jnp.concatenate(split3(seed), axis=0), NT)
    seed_sum = (
        seed_cut[:, :quarter] + seed_cut[:, quarter : 2 * quarter] + seed_cut[:, 2 * quarter :]
    )
    solved = precise(inverse, seed_sum)
    ssend[...] = solved
    answer_q = grouped(lambda peer: ssend, sq.at[q], quads)
    start(*answer_q)
    start(*coeffs_q)
    fence()
    sq[q] = solved

    excess = over_ref[...]
    loss = jnp.maximum(excess, 0.0) + jnp.log1p(jnp.exp(-jnp.abs(excess)))
    loss_part = jnp.sum(rate * jnp.sum(loss, axis=1, keepdims=True), axis=0, keepdims=True)
    lsend[...] = jnp.broadcast_to(loss_part, lsend.shape)
    lq[q] = lsend[...]
    loss_q = grouped(lambda peer: lsend, lq.at[q], quads)
    start(*loss_q)
    fence()

    arrive(*answer_q)
    solved_all = jnp.concatenate([sq[i] for i in range(4)], axis=1)
    picked = mm(jnp.concatenate(split3(solved_all), axis=0), table[...])
    solved3 = jnp.concatenate(
        [picked.astype(BF16), jnp.zeros((LANES - 3 * REGRESSORS, picked.shape[1]), BF16)], axis=0
    )

    def slope(top, bottom):
        spread = mm(dtri[top:bottom, :], solved3).astype(BF16).astype(F32)
        slopes[top:bottom, :] = (nsig[top:bottom, :] * spread).astype(BF16)

    scale = 1.0 / math.sqrt(paths_all)

    def basis_part(first, last):
        return mm(slopes[first * rows : last * rows, :], wall[...].reshape(4 * trades, feats))

    def weight_part(left, right):
        cut = slopes[:, left * trades : right * trades]
        return mm(cut, pall[...], TN) * scale

    slope(head, 4 * rows)
    psend[0] = basis_part(3, 4).astype(BF16)
    basis_via = pieces(psend.at[0], pvia, CORE, rows)
    start(*basis_via)
    fence()
    slope(0, head)
    part = weight_part(2, 4)
    wsend[0] = part[trades:].astype(BF16)
    weight_via = pieces(wsend.at[0], wvia, SIDE, trades)
    start(*weight_via)
    wsend[1] = part[:trades].astype(BF16)
    weight_side = remote(wsend.at[1], wz.at[0], SIDE)
    start(weight_side)
    fence()
    part = basis_part(1, 3)
    pfar[...] = part[rows:]
    basis_far = pieces(pjoin, pq.at[1], FAR, rows)
    for p, (copy, onward) in enumerate(zip(basis_via, basis_far)):
        cut = slice(p * rows // PIECES, (p + 1) * rows // PIECES)
        arrive(copy)
        pjoin[cut, :] = (pfar[cut, :] + pvia[cut, :].astype(F32)).astype(BF16)
        start(onward)
        fence()
    psend[1] = part[:rows].astype(BF16)
    basis_core = remote(psend.at[1], pq.at[0], CORE)
    start(basis_core)
    fence()
    wnear[...] = weight_part(1, 2)
    pulled = mm(solved3, tval[...], NT)
    pulled = (
        pulled[:REGRESSORS]
        + pulled[REGRESSORS : 2 * REGRESSORS]
        + pulled[2 * REGRESSORS : 3 * REGRESSORS]
    )
    esend[0] = pulled[:, 3 * rows :]
    esend[1] = pulled[:, rows : 2 * rows]
    pull_via = remote(esend.at[0], evia, CORE)
    pull_core = remote(esend.at[1], eq.at[0], CORE)
    pull_far = remote(ejoin, eq.at[1], FAR)
    start(pull_via, pull_core)
    fence()
    weight_near = pieces(wjoin, wz.at[1], NEAR, trades)
    for p, (copy, onward) in enumerate(zip(weight_via, weight_near)):
        cut = slice(p * trades // PIECES, (p + 1) * trades // PIECES)
        arrive(copy)
        wjoin[cut, :] = (wnear[cut, :] + wvia[cut, :].astype(F32)).astype(BF16)
        start(onward)
        if p == 0:
            arrive(pull_via)
            ejoin[...] = pulled[:, 2 * rows : 3 * rows] + evia[...]
            start(pull_far)
    fence()
    wadj_ref[...] = weight_part(0, 1)
    basis_ref[...] = basis_part(0, 1)

    arrive(*coeffs_q)
    own_triple = dtri[:rows, :]
    coeffs_all = jnp.concatenate([cq[i] for i in range(4)], axis=1)
    fitted = mm(own_triple, stack3(coeffs_all))
    over = fitted - full_thresholds
    fall = jnp.exp(-jnp.abs(over))
    own_seed = full_rates * (jnp.where(over >= 0.0, 1.0, fall) / (1.0 + fall))
    residual = own_seed - mm(own_triple, stack3(solved_all))
    term = precise(coeffs_all, residual, NT) - precise(solved_all, fitted, NT)
    term = term + pulled[:, :rows]
    arrive(*loss_q)
    answers = jnp.concatenate([lq[i] for i in range(4)], axis=1)
    loss_sum = jnp.sum(answers[:1], axis=1, keepdims=True) / quarter
    loss_ref[...] = jnp.broadcast_to(loss_sum / (paths_all * set_total), loss_ref.shape)
    arrive(basis_core)
    basis_ref[...] = basis_ref[...] + pq[0].astype(F32)
    arrive(weight_side)
    wadj_ref[...] = wadj_ref[...] + wz[0].astype(F32)
    arrive(*basis_far)
    basis_ref[...] = basis_ref[...] + pq[1].astype(F32)
    arrive(pull_core, pull_far)
    term = term + eq[0] + eq[1]
    padded = jnp.concatenate([term, jnp.zeros((LANES - REGRESSORS, rows), F32)], axis=0)
    turned = pltpu.roll(jnp.transpose(padded), LANES - 1, 1)
    lane = lax.broadcasted_iota(jnp.int32, turned.shape, 1)
    turned = jnp.where(lane < REGRESSORS - 1, turned, 0.0)
    basis_ref[:, :LANES] = basis_ref[:, :LANES] + turned
    for p, copy in enumerate(weight_near):
        cut = slice(p * trades // PIECES, (p + 1) * trades // PIECES)
        arrive(copy)
        wadj_ref[cut, :] = wadj_ref[cut, :] + wz[1, cut, :].astype(F32)
    for copy in copies:
        copy.wait_send()


def square_scratch(rows, trades, feats, set_total):
    size, quarter = REGRESSORS, set_total // 4
    return [
        pltpu.VMEM((4 * rows, feats), BF16),
        pltpu.VMEM((4, trades, feats), BF16),
        pltpu.VMEM((4, size + 16, trades), BF16),
        pltpu.VMEM((3, 4, size, rows), BF16),
        pltpu.VMEM((16, size, rows), BF16),
        pltpu.VMEM((LANES, 16 * rows), BF16),
        pltpu.VMEM((4 * rows, LANES), BF16),
        pltpu.VMEM((size, 4 * rows), BF16),
        pltpu.VMEM((set_total, 4 * trades), BF16),
        pltpu.VMEM((size, LANES), F32),
        pltpu.VMEM((4, size, quarter), F32),
        pltpu.VMEM((4, size, quarter), F32),
        pltpu.VMEM((size, quarter), F32),
        pltpu.VMEM((4, size, quarter), F32),
        pltpu.VMEM((size, quarter), F32),
        pltpu.VMEM((4, size, quarter), F32),
        pltpu.VMEM((size, quarter), F32),
        pltpu.VMEM((4, size, quarter), F32),
        pltpu.VMEM((8, quarter), F32),
        pltpu.VMEM((4, 8, quarter), F32),
        pltpu.VMEM((quarter, 16 * rows), F32),
        pltpu.VMEM((4 * rows, 4 * trades), BF16),
        pltpu.VMEM((4 * rows, 4 * trades), F32),
        pltpu.VMEM((4 * rows, 4 * trades), BF16),
        pltpu.VMEM((2, trades, feats), BF16),
        pltpu.VMEM((trades, feats), BF16),
        pltpu.VMEM((trades, feats), F32),
        pltpu.VMEM((trades, feats), BF16),
        pltpu.VMEM((2, trades, feats), BF16),
        pltpu.VMEM((2, rows, feats), BF16),
        pltpu.VMEM((rows, feats), BF16),
        pltpu.VMEM((rows, feats), F32),
        pltpu.VMEM((rows, feats), BF16),
        pltpu.VMEM((2, rows, feats), BF16),
        pltpu.VMEM((2, size, rows), F32),
        pltpu.VMEM((size, rows), F32),
        pltpu.VMEM((size, rows), F32),
        pltpu.VMEM((2, size, rows), F32),
        pltpu.SemaphoreType.DMA((7,)),
        pltpu.SemaphoreType.DMA((COPIES,)),
        pltpu.SemaphoreType.DMA((COPIES,)),
        pltpu.SemaphoreType.REGULAR((5,)),
        pltpu.SemaphoreType.REGULAR,
    ]


def chain_scratch(inner, outer, rows, trades, feats, set_total):
    size, quarter, count = REGRESSORS, set_total // inner, inner * outer
    z_pairs, q_pairs = max(outer - 1, 1), max(inner - 1, 1)
    return [
        pltpu.VMEM((inner, rows, feats), BF16),
        pltpu.VMEM((outer, trades, feats), BF16),
        pltpu.VMEM((outer, 8, trades), F32),
        pltpu.VMEM((8, trades), F32),
        pltpu.VMEM((size, rows), BF16),
        pltpu.VMEM((outer, size, rows), BF16),
        pltpu.VMEM((inner, outer, size, rows), BF16),
        pltpu.VMEM((LANES, count * rows), BF16),
        pltpu.VMEM((set_total, outer * trades), BF16),
        pltpu.VMEM((size, LANES), F32),
        pltpu.VMEM((inner, size, quarter), F32),
        pltpu.VMEM((inner, size, quarter), F32),
        pltpu.VMEM((size, quarter), F32),
        pltpu.VMEM((outer, size, quarter), F32),
        pltpu.VMEM((size, quarter), F32),
        pltpu.VMEM((inner, size, quarter), F32),
        pltpu.VMEM((size + 8, quarter), F32),
        pltpu.VMEM((inner, size + 8, quarter), F32),
        pltpu.VMEM((inner, size, rows), F32),
        pltpu.VMEM((inner, size, rows), F32),
        pltpu.VMEM((outer, trades, feats), BF16),
        pltpu.VMEM((outer, trades, feats), BF16),
        pltpu.VMEM((inner, rows, feats), BF16),
        pltpu.VMEM((inner, rows, feats), BF16),
        pltpu.VMEM((inner * rows, outer * trades), F32),
        pltpu.VMEM((inner * rows, outer * trades), BF16),
        pltpu.SemaphoreType.DMA((7,)),
        pltpu.SemaphoreType.DMA((5, z_pairs)),
        pltpu.SemaphoreType.DMA((5, z_pairs)),
        pltpu.SemaphoreType.DMA((7, q_pairs)),
        pltpu.SemaphoreType.DMA((7, q_pairs)),
    ]


def shards(
    path_basis, proxy_weight, notional, set_of, threshold_index, threshold_levels, loss_rate
):
    count = lax.axis_size("paths")
    inner = math.gcd(4, count)
    outer = count // inner
    rows, feats = path_basis.shape
    trades = proxy_weight.shape[0]
    set_total = loss_rate.shape[0]
    quarter = set_total // inner
    vmem = pl.BlockSpec(memory_space=pltpu.VMEM)
    if count == 16 and rows == trades and rows % (16 * PIECES) == 0:
        body = functools.partial(square, rows * count, set_total)
        scratch = square_scratch(rows, trades, feats, set_total)
    else:
        body = functools.partial(kernel, inner, outer, rows * count, set_total)
        scratch = chain_scratch(inner, outer, rows, trades, feats, set_total)
    loss, basis_adjoint, weight_adjoint = pl.pallas_call(
        body,
        out_shape=(
            jax.ShapeDtypeStruct((1, LANES), F32),
            jax.ShapeDtypeStruct((rows, feats), F32),
            jax.ShapeDtypeStruct((trades, feats), F32),
        ),
        in_specs=[pl.BlockSpec(memory_space=pltpu.HBM)] * 7,
        out_specs=(vmem, vmem, vmem),
        scratch_shapes=[
            pltpu.VMEM((1, trades), BF16),
            pltpu.VMEM((inner * outer, trades), jnp.int32),
            pltpu.VMEM((inner, quarter), jnp.int32),
            pltpu.SMEM(threshold_levels.shape, F32),
            pltpu.VMEM((inner, quarter), F32),
            *scratch,
        ],
        compiler_params=pltpu.CompilerParams(
            collective_id=0, has_side_effects=True, vmem_limit_bytes=48 * 1024 * 1024
        ),
    )(
        *(
            pltpu.with_memory_space_constraint(operand, pltpu.HBM)
            for operand in (
                path_basis,
                proxy_weight,
                notional.reshape(1, trades),
                set_of.reshape(-1, trades),
                threshold_index.reshape(inner, quarter),
                threshold_levels,
                loss_rate.reshape(inner, quarter),
            )
        )
    )
    return loss[0, :1], basis_adjoint, weight_adjoint


def solution(mesh):
    placed = (
        P(("groups", "paths"), None),
        P(("groups", "paths"), None),
        P(("groups", "paths")),
        P("groups"),
        P("groups"),
        P("groups"),
        P("groups"),
    )
    return jax.shard_map(
        shards,
        mesh=mesh,
        in_specs=placed,
        out_specs=(P("groups"), P(("groups", "paths"), None), P(("groups", "paths"), None)),
        check_vma=False,
    )
```

```python
import functools
import math

import jax
import jax.numpy as jnp
from jax import lax
from jax.experimental import pallas as pl
from jax.experimental.pallas import tpu as pltpu
from jax.sharding import PartitionSpec as P

REGRESSORS = 32
RIDGE_SCALE = 0.01
PRECISE = lax.Precision.HIGHEST
LANES = 128
PIECES = 4
FIRST_STEPS = 10
COPIES = 96
F32 = jnp.float32
BF16 = jnp.bfloat16

NN = (((1,), (0,)), ((), ()))
NT = (((1,), (1,)), ((), ()))
TN = (((0,), (0,)), ((), ()))


def mm(a, b, dims=NN):
    return lax.dot_general(a, b, dims, preferred_element_type=F32)


def precise(a, b, dims=NN):
    return lax.dot_general(a, b, dims, precision=PRECISE, preferred_element_type=F32)


def split3(x):
    hi = x.astype(BF16)
    rest = x - hi.astype(F32)
    mid = rest.astype(BF16)
    lo = (rest - mid.astype(F32)).astype(BF16)
    return hi, mid, lo


def stack3(x):
    hi, mid, lo = split3(x)
    return jnp.concatenate([hi, mid, lo, jnp.zeros_like(hi)], axis=0)


def design_of(basis):
    front = pltpu.roll(basis[:, :LANES].astype(F32), 1, 1)
    lane = lax.broadcasted_iota(jnp.int32, front.shape, 1)
    return jnp.where(lane == 0, 1.0, jnp.where(lane < REGRESSORS, front, 0.0))


def triple(design):
    return (
        design + pltpu.roll(design, REGRESSORS, 1) + pltpu.roll(design, 2 * REGRESSORS, 1)
    ).astype(BF16)


def augmented(gram):
    row = lax.broadcasted_iota(jnp.int32, gram.shape, 0)
    lane = lax.broadcasted_iota(jnp.int32, gram.shape, 1)
    return jnp.where(lane < REGRESSORS, gram, jnp.where(lane == row + REGRESSORS, 1.0, 0.0))


def eliminate(work, first, last):
    row = lax.broadcasted_iota(jnp.int32, work.shape, 0)
    for k in range(first, last):
        column = jnp.broadcast_to(work[:, k : k + 1], work.shape)
        pivot = work[k : k + 1, :] / column[k : k + 1, :]
        work = jnp.where(row == k, pivot, work - column * pivot)
    return work


def spd_inverse(gram):
    work = eliminate(augmented(gram), 0, REGRESSORS)
    return pltpu.roll(work, LANES - REGRESSORS, 1)


def set_table(labels, set_total):
    sets = lax.broadcasted_iota(jnp.int32, (set_total, labels.shape[1]), 0)
    return jnp.where(sets == labels, 1.0, 0.0).astype(BF16)


def partner(index, step, count):
    if count & (count - 1):
        return lax.rem(index + step, count)
    result, weight = 0, 1
    while weight < count:
        bit = lax.rem(lax.div(index, weight), 2)
        result = result + weight * (1 - bit if step & weight else bit)
        weight *= 2
    return result


def kernel(
    inner, outer, paths_all, set_total,
    pb_hbm, w_hbm, not_hbm, set_hbm, tidx_hbm, level_hbm, rate_hbm,
    loss_ref, basis_ref, wadj_ref,
    not_ref, set_ref, tidx_ref, level_ref, rate_ref,
    pall, wall, nall, nsend, gown, gall, gq, dstack, table, invert,
    bown, bq, bzsend, bz, csend, cq, ssend, sq,
    eown, eq, wown, wz, pown, pq, nsig, tval,
    local, zsend, zrecv, qsend, qrecv,
):
    rows, feats = basis_ref.shape
    trades = wadj_ref.shape[0]
    quarter = set_total // inner
    me = lax.axis_index("paths")
    q = lax.rem(me, inner)
    z = lax.div(me, inner)

    loads = [
        pltpu.make_async_copy(source, target, local.at[i])
        for i, (source, target) in enumerate(
            [
                (pb_hbm, pall.at[q]),
                (not_hbm, not_ref),
                (w_hbm, wall.at[z]),
                (set_hbm, set_ref),
                (tidx_hbm, tidx_ref),
                (level_hbm, level_ref),
                (rate_hbm, rate_ref),
            ]
        )
    ]
    for load in loads:
        load.start()

    barrier = pltpu.get_barrier_semaphore()
    for d in range(1, inner):
        pl.semaphore_signal(
            barrier, inc=1, device_id={"paths": z * inner + lax.rem(q + d, inner)},
            device_id_type=pl.DeviceIdType.MESH,
        )
    for d in range(1, outer):
        pl.semaphore_signal(
            barrier, inc=1, device_id={"paths": lax.rem(z + d, outer) * inner + q},
            device_id_type=pl.DeviceIdType.MESH,
        )

    pending = []

    def over_q(which, source, target):
        copies = []
        for d in range(inner - 1, 0, -1):
            peer = partner(q, d, inner)
            copy = pltpu.make_async_remote_copy(
                src_ref=source(peer), dst_ref=target.at[q],
                send_sem=qsend.at[which, d - 1], recv_sem=qrecv.at[which, d - 1],
                device_id={"paths": z * inner + peer},
                device_id_type=pl.DeviceIdType.MESH,
            )
            copy.start()
            copies.append(copy)
        pending.extend(copies)
        return copies

    def over_z(which, source, target):
        copies = []
        for d in range(outer - 1, 0, -1):
            peer = partner(z, d, outer)
            copy = pltpu.make_async_remote_copy(
                src_ref=source(peer), dst_ref=target.at[z],
                send_sem=zsend.at[which, d - 1], recv_sem=zrecv.at[which, d - 1],
                device_id={"paths": peer * inner + q},
                device_id_type=pl.DeviceIdType.MESH,
            )
            copy.start()
            copies.append(copy)
        pending.extend(copies)
        return copies

    def arrive(copies):
        for copy in copies:
            copy.wait_recv()

    def total(ref, count):
        result = ref[0].astype(F32)
        for i in range(1, count):
            result = result + ref[i].astype(F32)
        return result

    loads[0].wait()
    own_design = design_of(pall[q])
    own_triple = triple(own_design)
    own_turned = jnp.transpose(own_design)[:REGRESSORS, :].astype(BF16)
    gown[...] = own_turned
    loads[1].wait()
    nrow = jnp.broadcast_to(not_ref[...].astype(F32), (8, trades))
    nsend[...] = nrow
    loads[2].wait()
    pl.semaphore_wait(barrier, inner + outer - 2)

    gram_z = over_z(0, lambda peer: gown, gall)
    note_z = over_z(1, lambda peer: nsend, nall)
    trade_z = over_z(2, lambda peer: wall.at[z], wall)
    path_q = over_q(0, lambda peer: pall.at[q], pall)
    gall[z] = own_turned
    nall[z] = nrow

    arrive(gram_z)
    gram_q = over_q(1, lambda peer: gall, gq)
    gq[q] = gall[...]

    for load in loads[3:]:
        load.wait()
    all_levels = tidx_ref[...]
    all_thresholds = jnp.zeros((inner, quarter), F32)
    levels = tidx_ref[pl.ds(q, 1), :]
    thresholds = jnp.zeros((1, quarter), F32)
    for i in range(level_ref.shape[0]):
        thresholds = jnp.where(levels == i, level_ref[i], thresholds)
        all_thresholds = jnp.where(all_levels == i, level_ref[i], all_thresholds)
    thresholds = jnp.transpose(jnp.broadcast_to(thresholds, (quarter, quarter)))[:, :1]
    rate = jnp.transpose(
        jnp.broadcast_to(rate_ref[pl.ds(q, 1), :], (quarter, quarter))
    )[:, :1]
    all_rates = rate_ref[...]
    labels = jnp.concatenate(
        [set_ref[pl.ds(i * inner + q, 1), :] for i in range(outer)], axis=1
    )
    table[...] = set_table(labels, set_total)

    arrive(path_q)
    paths = pall[...].reshape(inner * rows, feats)
    design = design_of(paths)
    design3 = triple(design)
    design_t = jnp.transpose(design)[:REGRESSORS, :].astype(BF16)

    arrive(gram_q)
    turned_all = jnp.concatenate(
        [gq[i, j] for i in range(inner) for j in range(outer)], axis=1
    )
    dstack[...] = jnp.concatenate(
        [turned_all, turned_all, turned_all, jnp.zeros_like(turned_all)], axis=0
    )
    gram = mm(turned_all, dstack[...], NT)
    gram_row = lax.broadcasted_iota(jnp.int32, (REGRESSORS, LANES), 0)
    gram_lane = lax.broadcasted_iota(jnp.int32, (REGRESSORS, LANES), 1)
    ridge = jnp.where(gram_row == gram_lane, RIDGE_SCALE * paths_all, 0.0)
    invert[...] = spd_inverse(gram + ridge)

    arrive(note_z)
    notional = jnp.concatenate([nall[i][0:1, :] for i in range(outer)], axis=1)
    arrive(trade_z)
    weights = wall[...].reshape(outer * trades, feats)
    pre_act = mm(paths, weights, NT)
    small = jnp.exp(-jnp.abs(pre_act))
    tval[...] = (notional * (jnp.maximum(pre_act, 0.0) + jnp.log1p(small))).astype(BF16)
    nsig[...] = notional * (jnp.where(pre_act >= 0.0, 1.0, small) / (1.0 + small))

    by_trade = mm(design_t, tval[...])
    by_set = mm(jnp.concatenate(split3(by_trade), axis=0), table[...], NT)
    moments = (
        by_set[:REGRESSORS] + by_set[REGRESSORS : 2 * REGRESSORS] + by_set[2 * REGRESSORS :]
    )
    for i in range(inner):
        bown[i] = moments[:, i * quarter : (i + 1) * quarter]
    moment_q = over_q(2, lambda peer: bown.at[peer], bq)
    bq[q] = bown[q]
    arrive(moment_q)
    moment_mid = total(bq, inner)
    bzsend[...] = moment_mid
    moment_z = over_z(3, lambda peer: bzsend, bz)
    bz[z] = moment_mid
    arrive(moment_z)
    inverse = invert[:, :REGRESSORS]
    coeffs = precise(inverse, total(bz, outer))
    csend[...] = coeffs
    coeffs_q = over_q(3, lambda peer: csend, cq)
    cq[q] = coeffs
    excess = mm(stack3(coeffs), dstack[...], TN) - thresholds
    fade = jnp.exp(-jnp.abs(excess))
    loss = jnp.maximum(excess, 0.0) + jnp.log1p(fade)
    seed = rate * (jnp.where(excess >= 0.0, 1.0, fade) / (1.0 + fade))
    seed_cut = mm(dstack[:REGRESSORS, :], jnp.concatenate(split3(seed), axis=0), NT)
    seed_sum = (
        seed_cut[:, :quarter] + seed_cut[:, quarter : 2 * quarter] + seed_cut[:, 2 * quarter :]
    )
    solved = precise(inverse, seed_sum)
    loss_part = jnp.sum(rate * jnp.sum(loss, axis=1, keepdims=True), axis=0, keepdims=True)
    answer = jnp.concatenate([solved, jnp.broadcast_to(loss_part, (8, quarter))], axis=0)
    ssend[...] = answer
    answer_q = over_q(4, lambda peer: ssend, sq)
    sq[q] = answer
    arrive(coeffs_q)
    coeffs_all = jnp.concatenate([cq[i] for i in range(inner)], axis=1)
    arrive(answer_q)
    answers = jnp.concatenate([sq[i] for i in range(inner)], axis=1)
    solved_all = answers[:REGRESSORS]
    loss_sum = jnp.sum(answers[REGRESSORS : REGRESSORS + 1], axis=1, keepdims=True) / quarter
    loss_ref[...] = jnp.broadcast_to(loss_sum / (paths_all * set_total), loss_ref.shape)

    picked = mm(jnp.concatenate(split3(solved_all), axis=0), table[...])
    solved3 = jnp.concatenate(
        [picked.astype(BF16), jnp.zeros((LANES - 3 * REGRESSORS, picked.shape[1]), BF16)], axis=0
    )
    spread = mm(design3, solved3).astype(BF16).astype(F32)
    slopes = (nsig[...] * spread).astype(BF16)
    scale = 1.0 / math.sqrt(paths_all)
    weight_part = mm(slopes, paths, TN) * scale
    wown[...] = weight_part.astype(BF16).reshape(outer, trades, feats)
    weight_z = over_z(4, lambda peer: wown.at[peer], wz)
    wz[z] = wown[z]

    pulled = mm(solved3, tval[...], NT)
    pulled = (
        pulled[:REGRESSORS]
        + pulled[REGRESSORS : 2 * REGRESSORS]
        + pulled[2 * REGRESSORS : 3 * REGRESSORS]
    )
    for i in range(inner):
        eown[i] = pulled[:, i * rows : (i + 1) * rows]
    pull_q = over_q(5, lambda peer: eown.at[peer], eq)
    eq[q] = eown[q]
    basis_part = mm(slopes, weights)
    pown[...] = basis_part.astype(BF16).reshape(inner, rows, feats)
    basis_q = over_q(6, lambda peer: pown.at[peer], pq)
    pq[q] = pown[q]

    fitted = mm(own_triple, stack3(coeffs_all))
    full_thresholds = jnp.concatenate([all_thresholds[i : i + 1] for i in range(inner)], axis=1)
    full_rates = jnp.concatenate([all_rates[i : i + 1] for i in range(inner)], axis=1)
    over = fitted - full_thresholds
    tail = jnp.exp(-jnp.abs(over))
    own_seed = full_rates * (jnp.where(over >= 0.0, 1.0, tail) / (1.0 + tail))
    residual = own_seed - mm(own_triple, stack3(solved_all))
    term = precise(coeffs_all, residual, NT) - precise(solved_all, fitted, NT)
    arrive(pull_q)
    term = term + total(eq, inner)
    padded = jnp.concatenate([term, jnp.zeros((LANES - REGRESSORS, rows), F32)], axis=0)
    turned = pltpu.roll(jnp.transpose(padded), LANES - 1, 1)
    lane = lax.broadcasted_iota(jnp.int32, turned.shape, 1)
    turned = jnp.where(lane < REGRESSORS - 1, turned, 0.0)
    arrive(basis_q)
    basis_ref[...] = total(pq, inner)
    basis_ref[:, :LANES] = basis_ref[:, :LANES] + turned
    arrive(weight_z)
    wadj_ref[...] = total(wz, outer)
    for copy in pending:
        copy.wait_send()


def square(
    paths_all, set_total,
    pb_hbm, w_hbm, not_hbm, set_hbm, tidx_hbm, level_hbm, rate_hbm,
    loss_ref, basis_ref, wadj_ref,
    not_ref, set_ref, tidx_ref, level_ref, rate_ref,
    pall, wall, small, dall, dgrid, dstack, dtri, dturn, table, invert,
    bown, bq, bzsend, bz, csend, cq, ssend, sq, lsend, lq, over_ref,
    by_trades, tval, nsig, slopes, pulls,
    wsend, wvia, wnear, wjoin, wz, psend, pvia, pown, pjoin, pq, esend, evia, ejoin, eq,
    local, send, recv, ready, order,
):
    rows, feats = basis_ref.shape
    trades = wadj_ref.shape[0]
    quarter = set_total // 4
    me = lax.axis_index("paths")
    q, z = lax.rem(me, 4), lax.div(me, 4)
    bits = [lax.rem(lax.div(me, weight), 2) for weight in (1, 2, 4, 8)]
    peers = [me] + [partner(me, step, 16) for step in range(1, 16)]
    low, high = bits[2], bits[3]
    inner = low + high - 2 * low * high
    CORE, SIDE, NEAR, FAR = 1, 2, 4, 8
    MID = NEAR + FAR
    trade_steps = (0, NEAR, SIDE, NEAR + SIDE)
    design_steps = (0, CORE, FAR, CORE + FAR)

    loads = [
        pltpu.make_async_copy(source, target, local.at[i])
        for i, (source, target) in enumerate(
            [
                (pb_hbm, pall.at[pl.ds(0, rows)]),
                (not_hbm, not_ref),
                (w_hbm, wall.at[0]),
                (set_hbm, set_ref),
                (tidx_hbm, tidx_ref),
                (level_hbm, level_ref),
                (rate_hbm, rate_ref),
            ]
        )
    ]
    barrier = pltpu.get_barrier_semaphore()

    def greet(semaphore, step):
        pl.semaphore_signal(
            semaphore, inc=1, device_id={"paths": peers[step]},
            device_id_type=pl.DeviceIdType.MESH,
        )

    for i, step in enumerate((CORE, SIDE, NEAR, FAR)):

        @pl.when(bits[i] == 0)
        def _():
            greet(barrier, step)

    @pl.when(inner * (1 - high) == 1)
    def _():
        greet(barrier, MID)

    for load in loads:
        load.start()

    made, copies, inner_copies, outer_copies = [], [], [], []

    def remote(source, target, step, bag=copies):
        k = len(made)
        copy = pltpu.make_async_remote_copy(
            src_ref=source, dst_ref=target, send_sem=send.at[k], recv_sem=recv.at[k],
            device_id={"paths": peers[step]}, device_id_type=pl.DeviceIdType.MESH,
        )
        made.append(copy)
        bag.append(copy)
        return copy

    def slot(i):
        return pall.at[pl.ds(i * rows, rows)]

    def start(*group):
        for copy in group:
            copy.start()

    def fence():
        pl.semaphore_signal(order, inc=1)
        pl.semaphore_wait(order, 1)

    def arrive(*group):
        for copy in group:
            copy.wait_recv()

    def pieces(source, target, step, extent, bag=copies):
        part = extent // PIECES
        cuts = [pl.ds(p * part, part) for p in range(PIECES)]
        return [remote(source.at[cut], target.at[cut], step, bag) for cut in cuts]

    def grouped(source, target, bits):
        return [remote(source(peers[s]), target, s) for s in bits]

    def place(i):
        design = design_of(pall[i * rows : (i + 1) * rows, :])
        at = slice(i * rows, (i + 1) * rows)
        dtri[at, :] = triple(design)
        turned = jnp.transpose(design)[:REGRESSORS, :].astype(BF16)
        dturn[:, at] = turned
        return turned

    path_core = remote(pb_hbm, slot(1), CORE)
    trade_side = pieces(w_hbm, wall.at[2], SIDE, trades)
    trade_near = pieces(w_hbm, wall.at[1], NEAR, trades)
    path_mid = pieces(pb_hbm, slot(2), MID, rows, inner_copies)
    path_far = pieces(pb_hbm, slot(4), FAR, rows, outer_copies)
    small_side = remote(small.at[0], small.at[2], SIDE)
    small_near = remote(small.at[0], small.at[1], NEAR)

    lower = bits[0] + bits[1] + bits[2] + bits[3] + inner * high

    @pl.when(lower > 0)
    def _():
        pl.semaphore_wait(barrier, lower)

    for i, step in enumerate((CORE, SIDE, NEAR)):

        @pl.when(bits[i] == 1)
        def _():
            greet(ready.at[i], step)

    @pl.when(inner * high == 1)
    def _():
        greet(ready.at[3], FAR)
        greet(ready.at[5], MID)

    def down(i, *group):
        @pl.when(bits[i] == 1)
        def _():
            start(*group)

    def up(i, *group):
        @pl.when(bits[i] == 0)
        def _():
            pl.semaphore_wait(ready.at[i], 1)
            start(*group)

    split = PIECES // 2
    down(2, *trade_near[:split])

    @pl.when(inner * high == 1)
    def _():
        start(*path_mid)

    down(1, *trade_side[:split])
    down(0, path_core)
    loads[0].wait()
    own_turned = place(0)
    loads[1].wait()
    note = jnp.broadcast_to(not_ref[...].astype(F32), (16, trades)).astype(BF16)
    small[0] = jnp.concatenate([own_turned, note], axis=0)
    down(2, small_near, *trade_near[split:])
    down(1, small_side, *trade_side[split:])
    up(0, path_core)
    up(1, small_side, *trade_side)
    up(2, small_near, *trade_near)

    @pl.when((1 - inner) * high == 1)
    def _():
        start(*path_far)

    @pl.when(inner * (1 - high) == 1)
    def _():
        pl.semaphore_wait(ready.at[5], 1)
        start(*path_mid)

    @pl.when((1 - inner) * (1 - high) == 1)
    def _():
        pl.semaphore_wait(ready.at[3], 1)
        start(*path_far)

    loads[2].wait()
    small_pass = remote(small.at[1], small.at[3], SIDE)
    trade_pass = pieces(wall.at[1], wall.at[3], SIDE, trades)
    mid_pass = pieces(slot(2), slot(3), CORE, rows, inner_copies)
    far_pass = pieces(slot(4), slot(5), CORE, rows, inner_copies)
    front = pl.ds(0, REGRESSORS)
    design_core = remote(small.at[:, front], dall.at[0], CORE)
    design_far = remote(small.at[:, front], dall.at[1], FAR)
    design_pass = remote(dall.at[1], dall.at[2], CORE)

    for load in loads[3:]:
        load.wait()
    labels = jnp.concatenate([set_ref[pl.ds(peers[s], 1), :] for s in trade_steps], axis=1)
    table[...] = set_table(labels, set_total)

    def value(top, bottom, left, right):
        paths = pall[top:bottom, :]
        weights = wall[left:right].reshape((right - left) * trades, feats)
        notional = jnp.concatenate(
            [small[s, REGRESSORS:, :].astype(F32)[:1, :] for s in range(left, right)], axis=1
        )
        pre_act = mm(paths, weights, NT)
        fade = jnp.exp(-jnp.abs(pre_act))
        at = (slice(top, bottom), slice(left * trades, right * trades))
        tval[at] = (notional * (jnp.maximum(pre_act, 0.0) + jnp.log1p(fade))).astype(BF16)
        nsig[at] = pre_act

    def sigmoid(top, bottom):
        notional = jnp.concatenate(
            [small[s, REGRESSORS:, :].astype(F32)[:1, :] for s in range(4)], axis=1
        )
        pre_act = nsig[top:bottom, :]
        fade = jnp.exp(-jnp.abs(pre_act))
        nsig[top:bottom, :] = notional * (jnp.where(pre_act >= 0.0, 1.0, fade) / (1.0 + fade))

    pair, head, tail, last = 2 * rows, 4 * rows, 5 * rows, 6 * rows
    arrive(path_core)
    place(1)

    @pl.when(inner == 1)
    def _():
        for copy, onward in zip(path_mid, mid_pass):
            arrive(copy)
            start(onward)

    for p, (copy, onward) in enumerate(zip(trade_near, trade_pass)):
        if p == split:
            arrive(small_near)
            start(small_pass)
        arrive(copy)
        start(onward)
    arrive(*trade_side, small_side)
    value(0, pair, 0, 3)

    @pl.when(inner == 1)
    def _():
        place(2)
        arrive(*mid_pass)
        place(3)
        value(pair, head, 0, 3)
        for copy, onward in zip(path_far, far_pass):
            arrive(copy)
            start(onward)
        greet(ready.at[4], FAR)
        fence()
        place(4)
        value(head, tail, 0, 3)

    arrive(small_pass)
    start(design_core, design_far)
    fence()
    arrive(*trade_pass)

    @pl.when(inner == 0)
    def _():
        value(0, pair, 3, 4)
        by_trades[...] = mm(dturn[:, :pair], tval[:pair, :])

    @pl.when(inner == 1)
    def _():
        value(0, tail, 3, 4)
        by_trades[...] = mm(dturn[:, :tail], tval[:tail, :])
        arrive(*far_pass)
        place(5)
        value(tail, last, 0, 4)
        by_trades[...] = by_trades[...] + mm(dturn[:, tail:], tval[tail:, :])

    by_trade = by_trades[...]
    by_set = mm(jnp.concatenate(split3(by_trade), axis=0), table[...], NT)
    moments = (
        by_set[:REGRESSORS] + by_set[REGRESSORS : 2 * REGRESSORS] + by_set[2 * REGRESSORS :]
    )
    for i in range(4):
        bown[i] = moments[:, i * quarter : (i + 1) * quarter]
    quads = (CORE + SIDE, SIDE, CORE)
    lines = (NEAR + FAR, FAR, NEAR)

    def total(ref, count):
        result = ref[0].astype(F32)
        for i in range(1, count):
            result = result + ref[i].astype(F32)
        return result

    moment_q = grouped(lambda peer: bown.at[lax.rem(peer, 4)], bq.at[q], quads)
    start(*moment_q)
    fence()
    bq[q] = bown[q]

    arrive(design_far)
    start(design_pass)
    fence()
    arrive(design_core, design_pass)
    for s in range(4):
        dgrid[peers[trade_steps[s]]] = small[s, :REGRESSORS, :]
    for k in range(1, 4):
        for s in range(4):
            dgrid[peers[trade_steps[s] + design_steps[k]]] = dall[k - 1, s]
    turned_all = jnp.concatenate([dgrid[i] for i in range(16)], axis=1)
    dstack[...] = jnp.concatenate(
        [turned_all, turned_all, turned_all, jnp.zeros_like(turned_all)], axis=0
    )
    gram = mm(turned_all, turned_all, NT)
    gram = jnp.concatenate([gram, jnp.zeros((REGRESSORS, LANES - REGRESSORS), F32)], axis=1)
    gram_row = lax.broadcasted_iota(jnp.int32, (REGRESSORS, LANES), 0)
    gram_lane = lax.broadcasted_iota(jnp.int32, (REGRESSORS, LANES), 1)
    ridge = jnp.where(gram_row == gram_lane, RIDGE_SCALE * paths_all, 0.0)
    work = eliminate(augmented(gram + ridge), 0, FIRST_STEPS)

    arrive(*moment_q)
    bzsend[...] = total(bq, 4)

    @pl.when(inner == 0)
    def _():
        pl.semaphore_wait(ready.at[4], 1)

    moment_z = grouped(lambda peer: bzsend, bz.at[z], lines)
    start(*moment_z)
    fence()
    bz[z] = bzsend[...]
    work = eliminate(work, FIRST_STEPS, REGRESSORS)
    invert[...] = pltpu.roll(work, LANES - REGRESSORS, 1)
    fence()
    sigmoid(0, pair)

    @pl.when(inner == 1)
    def _():
        sigmoid(pair, last)

    all_levels = tidx_ref[...]
    all_thresholds = jnp.zeros((4, quarter), F32)
    levels = tidx_ref[pl.ds(q, 1), :]
    thresholds = jnp.zeros((1, quarter), F32)
    for i in range(level_ref.shape[0]):
        thresholds = jnp.where(levels == i, level_ref[i], thresholds)
        all_thresholds = jnp.where(all_levels == i, level_ref[i], all_thresholds)
    thresholds = jnp.transpose(jnp.broadcast_to(thresholds, (quarter, quarter)))[:, :1]
    rate = jnp.transpose(
        jnp.broadcast_to(rate_ref[pl.ds(q, 1), :], (quarter, quarter))
    )[:, :1]
    all_rates = rate_ref[...]
    full_thresholds = jnp.concatenate([all_thresholds[i : i + 1] for i in range(4)], axis=1)
    full_rates = jnp.concatenate([all_rates[i : i + 1] for i in range(4)], axis=1)

    arrive(*moment_z)
    inverse = invert[:, :REGRESSORS]
    coeffs = precise(inverse, total(bz, 4))
    csend[...] = coeffs
    coeffs_q = grouped(lambda peer: csend, cq.at[q], quads)
    cq[q] = coeffs
    excess = mm(stack3(coeffs), dstack[...], TN) - thresholds
    over_ref[...] = excess
    fade = jnp.exp(-jnp.abs(excess))
    seed = rate * (jnp.where(excess >= 0.0, 1.0, fade) / (1.0 + fade))
    seed_cut = mm(dstack[:REGRESSORS, :], jnp.concatenate(split3(seed), axis=0), NT)
    seed_sum = (
        seed_cut[:, :quarter] + seed_cut[:, quarter : 2 * quarter] + seed_cut[:, 2 * quarter :]
    )
    solved = precise(inverse, seed_sum)
    ssend[...] = solved
    answer_q = grouped(lambda peer: ssend, sq.at[q], quads)
    start(*answer_q)
    start(*coeffs_q)
    fence()
    sq[q] = solved

    excess = over_ref[...]
    loss = jnp.maximum(excess, 0.0) + jnp.log1p(jnp.exp(-jnp.abs(excess)))
    loss_part = jnp.sum(rate * jnp.sum(loss, axis=1, keepdims=True), axis=0, keepdims=True)
    lsend[...] = jnp.broadcast_to(loss_part, lsend.shape)
    lq[q] = lsend[...]
    loss_q = grouped(lambda peer: lsend, lq.at[q], quads)
    start(*loss_q)
    fence()

    arrive(*answer_q)
    solved_all = jnp.concatenate([sq[i] for i in range(4)], axis=1)
    picked = mm(jnp.concatenate(split3(solved_all), axis=0), table[...])
    solved3 = jnp.concatenate(
        [picked.astype(BF16), jnp.zeros((LANES - 3 * REGRESSORS, picked.shape[1]), BF16)], axis=0
    )

    def slope(top, bottom, left, right):
        at = (slice(top, bottom), slice(left * trades, right * trades))
        spread = mm(dtri[top:bottom, :], solved3[:, at[1]]).astype(BF16).astype(F32)
        slopes[at] = (nsig[at] * spread).astype(BF16)

    scale = 1.0 / math.sqrt(paths_all)

    def basis_part(first, final):
        return mm(slopes[first * rows : final * rows, :], wall[...].reshape(4 * trades, feats))

    def weight_part(left, right, depth):
        cut = slopes[:depth, left * trades : right * trades]
        return mm(cut, pall[:depth, :], TN) * scale

    basis_via = [pieces(psend.at[i], pvia.at[i], CORE, rows, inner_copies) for i in range(2)]
    basis_core = remote(psend.at[2], pq.at[0], CORE)
    basis_far = pieces(pjoin.at[0], pq.at[1], FAR, rows, inner_copies)
    basis_mid = pieces(pjoin.at[1], pq.at[1], MID, rows, inner_copies)
    weight_via = pieces(wsend.at[0], wvia, SIDE, trades)
    weight_side = remote(wsend.at[1], wz.at[0], SIDE)

    def give(i, slot, depth, *group):
        wsend[i] = weight_part(slot, slot + 1, depth).astype(BF16)
        start(*group)
        fence()

    def join(i, onwards):
        for p, (copy, onward) in enumerate(zip(basis_via[i], onwards)):
            cut = slice(p * rows // PIECES, (p + 1) * rows // PIECES)
            arrive(copy)
            pjoin[i, cut, :] = (pown[i, cut, :] + pvia[i, cut, :].astype(F32)).astype(BF16)
            start(onward)
            fence()

    def pull(depth):
        pulled = mm(solved3, tval[:depth, :], NT)
        pulls[:, :depth] = (
            pulled[:REGRESSORS]
            + pulled[REGRESSORS : 2 * REGRESSORS]
            + pulled[2 * REGRESSORS : 3 * REGRESSORS]
        )

    @pl.when(inner == 1)
    def _():
        slope(0, last, 3, 4)
        give(0, 3, last, *weight_via)
        slope(head, last, 0, 3)
        part = basis_part(4, 6)
        psend[0] = part[rows:].astype(BF16)
        start(*basis_via[0])
        fence()
        pown[0] = part[:rows]
        slope(0, head, 0, 3)
        psend[1] = basis_part(3, 4).astype(BF16)
        start(*basis_via[1])
        fence()
        give(1, 2, last, weight_side)
        join(0, basis_far)
        part = basis_part(1, 3)
        pown[1] = part[rows:]
        join(1, basis_mid)
        psend[2] = part[:rows].astype(BF16)
        start(basis_core)
        fence()
        wnear[...] = weight_part(1, 2, last)
        pull(last)

    @pl.when(inner == 0)
    def _():
        slope(0, pair, 3, 4)
        give(0, 3, pair, *weight_via)
        slope(0, pair, 0, 3)
        give(1, 2, pair, weight_side)
        psend[2] = basis_part(1, 2).astype(BF16)
        start(basis_core)
        fence()
        wnear[...] = weight_part(1, 2, pair)
        pull(pair)

    pull_via = [remote(esend.at[i], evia.at[i], CORE, inner_copies) for i in range(2)]
    pull_core = remote(esend.at[2], eq.at[0], CORE)
    pull_far = remote(ejoin.at[0], eq.at[1], FAR, inner_copies)
    pull_mid = remote(ejoin.at[1], eq.at[1], MID, inner_copies)
    esend[2] = pulls[:, rows:pair]
    start(pull_core)
    fence()

    @pl.when(inner == 1)
    def _():
        esend[0] = pulls[:, tail:]
        esend[1] = pulls[:, 3 * rows : head]
        start(*pull_via)
        fence()

    weight_near = pieces(wjoin, wz.at[1], NEAR, trades)
    for p, (copy, onward) in enumerate(zip(weight_via, weight_near)):
        cut = slice(p * trades // PIECES, (p + 1) * trades // PIECES)
        arrive(copy)
        wjoin[cut, :] = (wnear[cut, :] + wvia[cut, :].astype(F32)).astype(BF16)
        start(onward)
        if p == 0:

            @pl.when(inner == 1)
            def _():
                arrive(*pull_via)
                ejoin[0] = pulls[:, head:tail] + evia[0]
                ejoin[1] = pulls[:, pair : 3 * rows] + evia[1]
                start(pull_far, pull_mid)

    fence()

    @pl.when(inner == 1)
    def _():
        wadj_ref[...] = weight_part(0, 1, last)

    @pl.when(inner == 0)
    def _():
        wadj_ref[...] = weight_part(0, 1, pair)

    basis_ref[...] = basis_part(0, 1)

    arrive(*coeffs_q)
    own_triple = dtri[:rows, :]
    coeffs_all = jnp.concatenate([cq[i] for i in range(4)], axis=1)
    fitted = mm(own_triple, stack3(coeffs_all))
    over = fitted - full_thresholds
    fall = jnp.exp(-jnp.abs(over))
    own_seed = full_rates * (jnp.where(over >= 0.0, 1.0, fall) / (1.0 + fall))
    residual = own_seed - mm(own_triple, stack3(solved_all))
    term = precise(coeffs_all, residual, NT) - precise(solved_all, fitted, NT)
    term = term + pulls[:, :rows]
    arrive(*loss_q)
    answers = jnp.concatenate([lq[i] for i in range(4)], axis=1)
    loss_sum = jnp.sum(answers[:1], axis=1, keepdims=True) / quarter
    loss_ref[...] = jnp.broadcast_to(loss_sum / (paths_all * set_total), loss_ref.shape)
    arrive(basis_core)
    basis_ref[...] = basis_ref[...] + pq[0].astype(F32)
    arrive(weight_side)
    wadj_ref[...] = wadj_ref[...] + wz[0].astype(F32)

    @pl.when(inner == 1)
    def _():
        arrive(*basis_mid)

    @pl.when(inner == 0)
    def _():
        arrive(*basis_far)

    basis_ref[...] = basis_ref[...] + pq[1].astype(F32)
    arrive(pull_core)

    @pl.when(inner == 1)
    def _():
        arrive(pull_mid)

    @pl.when(inner == 0)
    def _():
        arrive(pull_far)

    term = term + eq[0] + eq[1]
    padded = jnp.concatenate([term, jnp.zeros((LANES - REGRESSORS, rows), F32)], axis=0)
    turned = pltpu.roll(jnp.transpose(padded), LANES - 1, 1)
    lane = lax.broadcasted_iota(jnp.int32, turned.shape, 1)
    turned = jnp.where(lane < REGRESSORS - 1, turned, 0.0)
    basis_ref[:, :LANES] = basis_ref[:, :LANES] + turned
    for p, copy in enumerate(weight_near):
        cut = slice(p * trades // PIECES, (p + 1) * trades // PIECES)
        arrive(copy)
        wadj_ref[cut, :] = wadj_ref[cut, :] + wz[1, cut, :].astype(F32)
    for copy in copies:
        copy.wait_send()

    @pl.when(inner == 1)
    def _():
        for copy in inner_copies:
            copy.wait_send()

    @pl.when(inner == 0)
    def _():
        for copy in outer_copies:
            copy.wait_send()


def square_scratch(rows, trades, feats, set_total):
    size, quarter = REGRESSORS, set_total // 4
    return [
        pltpu.VMEM((6 * rows, feats), BF16),
        pltpu.VMEM((4, trades, feats), BF16),
        pltpu.VMEM((4, size + 16, trades), BF16),
        pltpu.VMEM((3, 4, size, rows), BF16),
        pltpu.VMEM((16, size, rows), BF16),
        pltpu.VMEM((LANES, 16 * rows), BF16),
        pltpu.VMEM((6 * rows, LANES), BF16),
        pltpu.VMEM((size, 6 * rows), BF16),
        pltpu.VMEM((set_total, 4 * trades), BF16),
        pltpu.VMEM((size, LANES), F32),
        pltpu.VMEM((4, size, quarter), F32),
        pltpu.VMEM((4, size, quarter), F32),
        pltpu.VMEM((size, quarter), F32),
        pltpu.VMEM((4, size, quarter), F32),
        pltpu.VMEM((size, quarter), F32),
        pltpu.VMEM((4, size, quarter), F32),
        pltpu.VMEM((size, quarter), F32),
        pltpu.VMEM((4, size, quarter), F32),
        pltpu.VMEM((8, quarter), F32),
        pltpu.VMEM((4, 8, quarter), F32),
        pltpu.VMEM((quarter, 16 * rows), F32),
        pltpu.VMEM((size, 4 * trades), F32),
        pltpu.VMEM((6 * rows, 4 * trades), BF16),
        pltpu.VMEM((6 * rows, 4 * trades), F32),
        pltpu.VMEM((6 * rows, 4 * trades), BF16),
        pltpu.VMEM((size, 6 * rows), F32),
        pltpu.VMEM((2, trades, feats), BF16),
        pltpu.VMEM((trades, feats), BF16),
        pltpu.VMEM((trades, feats), F32),
        pltpu.VMEM((trades, feats), BF16),
        pltpu.VMEM((2, trades, feats), BF16),
        pltpu.VMEM((3, rows, feats), BF16),
        pltpu.VMEM((2, rows, feats), BF16),
        pltpu.VMEM((2, rows, feats), F32),
        pltpu.VMEM((2, rows, feats), BF16),
        pltpu.VMEM((2, rows, feats), BF16),
        pltpu.VMEM((3, size, rows), F32),
        pltpu.VMEM((2, size, rows), F32),
        pltpu.VMEM((2, size, rows), F32),
        pltpu.VMEM((2, size, rows), F32),
        pltpu.SemaphoreType.DMA((7,)),
        pltpu.SemaphoreType.DMA((COPIES,)),
        pltpu.SemaphoreType.DMA((COPIES,)),
        pltpu.SemaphoreType.REGULAR((6,)),
        pltpu.SemaphoreType.REGULAR,
    ]


def chain_scratch(inner, outer, rows, trades, feats, set_total):
    size, quarter, count = REGRESSORS, set_total // inner, inner * outer
    z_pairs, q_pairs = max(outer - 1, 1), max(inner - 1, 1)
    return [
        pltpu.VMEM((inner, rows, feats), BF16),
        pltpu.VMEM((outer, trades, feats), BF16),
        pltpu.VMEM((outer, 8, trades), F32),
        pltpu.VMEM((8, trades), F32),
        pltpu.VMEM((size, rows), BF16),
        pltpu.VMEM((outer, size, rows), BF16),
        pltpu.VMEM((inner, outer, size, rows), BF16),
        pltpu.VMEM((LANES, count * rows), BF16),
        pltpu.VMEM((set_total, outer * trades), BF16),
        pltpu.VMEM((size, LANES), F32),
        pltpu.VMEM((inner, size, quarter), F32),
        pltpu.VMEM((inner, size, quarter), F32),
        pltpu.VMEM((size, quarter), F32),
        pltpu.VMEM((outer, size, quarter), F32),
        pltpu.VMEM((size, quarter), F32),
        pltpu.VMEM((inner, size, quarter), F32),
        pltpu.VMEM((size + 8, quarter), F32),
        pltpu.VMEM((inner, size + 8, quarter), F32),
        pltpu.VMEM((inner, size, rows), F32),
        pltpu.VMEM((inner, size, rows), F32),
        pltpu.VMEM((outer, trades, feats), BF16),
        pltpu.VMEM((outer, trades, feats), BF16),
        pltpu.VMEM((inner, rows, feats), BF16),
        pltpu.VMEM((inner, rows, feats), BF16),
        pltpu.VMEM((inner * rows, outer * trades), F32),
        pltpu.VMEM((inner * rows, outer * trades), BF16),
        pltpu.SemaphoreType.DMA((7,)),
        pltpu.SemaphoreType.DMA((5, z_pairs)),
        pltpu.SemaphoreType.DMA((5, z_pairs)),
        pltpu.SemaphoreType.DMA((7, q_pairs)),
        pltpu.SemaphoreType.DMA((7, q_pairs)),
    ]


def shards(
    path_basis, proxy_weight, notional, set_of, threshold_index, threshold_levels, loss_rate
):
    count = lax.axis_size("paths")
    inner = math.gcd(4, count)
    outer = count // inner
    rows, feats = path_basis.shape
    trades = proxy_weight.shape[0]
    set_total = loss_rate.shape[0]
    quarter = set_total // inner
    vmem = pl.BlockSpec(memory_space=pltpu.VMEM)
    if count == 16 and rows == trades and rows % (16 * PIECES) == 0:
        body = functools.partial(square, rows * count, set_total)
        scratch = square_scratch(rows, trades, feats, set_total)
    else:
        body = functools.partial(kernel, inner, outer, rows * count, set_total)
        scratch = chain_scratch(inner, outer, rows, trades, feats, set_total)
    loss, basis_adjoint, weight_adjoint = pl.pallas_call(
        body,
        out_shape=(
            jax.ShapeDtypeStruct((1, LANES), F32),
            jax.ShapeDtypeStruct((rows, feats), F32),
            jax.ShapeDtypeStruct((trades, feats), F32),
        ),
        in_specs=[pl.BlockSpec(memory_space=pltpu.HBM)] * 7,
        out_specs=(vmem, vmem, vmem),
        scratch_shapes=[
            pltpu.VMEM((1, trades), BF16),
            pltpu.VMEM((inner * outer, trades), jnp.int32),
            pltpu.VMEM((inner, quarter), jnp.int32),
            pltpu.SMEM(threshold_levels.shape, F32),
            pltpu.VMEM((inner, quarter), F32),
            *scratch,
        ],
        compiler_params=pltpu.CompilerParams(
            collective_id=0, has_side_effects=True, vmem_limit_bytes=48 * 1024 * 1024
        ),
    )(
        *(
            pltpu.with_memory_space_constraint(operand, pltpu.HBM)
            for operand in (
                path_basis,
                proxy_weight,
                notional.reshape(1, trades),
                set_of.reshape(-1, trades),
                threshold_index.reshape(inner, quarter),
                threshold_levels,
                loss_rate.reshape(inner, quarter),
            )
        )
    )
    return loss[0, :1], basis_adjoint, weight_adjoint


def solution(mesh):
    placed = (
        P(("groups", "paths"), None),
        P(("groups", "paths"), None),
        P(("groups", "paths")),
        P("groups"),
        P("groups"),
        P("groups"),
        P("groups"),
    )
    return jax.shard_map(
        shards,
        mesh=mesh,
        in_specs=placed,
        out_specs=(P("groups"), P(("groups", "paths"), None), P(("groups", "paths"), None)),
        check_vma=False,
    )
```

```python
import functools
import math

import jax
import jax.numpy as jnp
from jax import lax
from jax.experimental import pallas as pl
from jax.experimental.pallas import tpu as pltpu
from jax.sharding import PartitionSpec as P

REGRESSORS = 32
RIDGE_SCALE = 0.01
PRECISE = lax.Precision.HIGHEST
LANES = 128
PIECES = 4
SENDS = 19
ARRIVALS = 28
F32 = jnp.float32
BF16 = jnp.bfloat16

NN = (((1,), (0,)), ((), ()))
NT = (((1,), (1,)), ((), ()))
TN = (((0,), (0,)), ((), ()))


def mm(a, b, dims=NN):
    return lax.dot_general(a, b, dims, preferred_element_type=F32)


def precise(a, b, dims=NN):
    return lax.dot_general(a, b, dims, precision=PRECISE, preferred_element_type=F32)


def split3(x):
    hi = x.astype(BF16)
    rest = x - hi.astype(F32)
    mid = rest.astype(BF16)
    lo = (rest - mid.astype(F32)).astype(BF16)
    return hi, mid, lo


def stack3(x):
    hi, mid, lo = split3(x)
    return jnp.concatenate([hi, mid, lo, jnp.zeros_like(hi)], axis=0)


def design_of(basis):
    front = pltpu.roll(basis[:, :LANES].astype(F32), 1, 1)
    lane = lax.broadcasted_iota(jnp.int32, front.shape, 1)
    return jnp.where(lane == 0, 1.0, jnp.where(lane < REGRESSORS, front, 0.0))


def triple(design):
    return (
        design + pltpu.roll(design, REGRESSORS, 1) + pltpu.roll(design, 2 * REGRESSORS, 1)
    ).astype(BF16)


def augmented(gram):
    row = lax.broadcasted_iota(jnp.int32, gram.shape, 0)
    lane = lax.broadcasted_iota(jnp.int32, gram.shape, 1)
    return jnp.where(lane < REGRESSORS, gram, jnp.where(lane == row + REGRESSORS, 1.0, 0.0))


def eliminate(work, first, last):
    row = lax.broadcasted_iota(jnp.int32, work.shape, 0)
    for k in range(first, last):
        column = jnp.broadcast_to(work[:, k : k + 1], work.shape)
        pivot = work[k : k + 1, :] / column[k : k + 1, :]
        work = jnp.where(row == k, pivot, work - column * pivot)
    return work


def spd_inverse(gram):
    work = eliminate(augmented(gram), 0, REGRESSORS)
    return pltpu.roll(work, LANES - REGRESSORS, 1)


def set_table(labels, set_total):
    sets = lax.broadcasted_iota(jnp.int32, (set_total, labels.shape[1]), 0)
    return jnp.where(sets == labels, 1.0, 0.0).astype(BF16)


def partner(index, step, count):
    if count & (count - 1):
        return lax.rem(index + step, count)
    result, weight = 0, 1
    while weight < count:
        bit = lax.rem(lax.div(index, weight), 2)
        result = result + weight * (1 - bit if step & weight else bit)
        weight *= 2
    return result


def kernel(
    inner, outer, paths_all, set_total,
    pb_hbm, w_hbm, not_hbm, set_hbm, tidx_hbm, level_hbm, rate_hbm,
    loss_ref, basis_ref, wadj_ref,
    not_ref, set_ref, tidx_ref, level_ref, rate_ref,
    pall, wall, nall, nsend, gown, gall, gq, dstack, table, invert,
    bown, bq, bzsend, bz, csend, cq, ssend, sq,
    eown, eq, wown, wz, pown, pq, nsig, tval,
    local, zsend, zrecv, qsend, qrecv,
):
    rows, feats = basis_ref.shape
    trades = wadj_ref.shape[0]
    quarter = set_total // inner
    me = lax.axis_index("paths")
    q = lax.rem(me, inner)
    z = lax.div(me, inner)

    loads = [
        pltpu.make_async_copy(source, target, local.at[i])
        for i, (source, target) in enumerate(
            [
                (pb_hbm, pall.at[q]),
                (not_hbm, not_ref),
                (w_hbm, wall.at[z]),
                (set_hbm, set_ref),
                (tidx_hbm, tidx_ref),
                (level_hbm, level_ref),
                (rate_hbm, rate_ref),
            ]
        )
    ]
    for load in loads:
        load.start()

    barrier = pltpu.get_barrier_semaphore()
    for d in range(1, inner):
        pl.semaphore_signal(
            barrier, inc=1, device_id={"paths": z * inner + lax.rem(q + d, inner)},
            device_id_type=pl.DeviceIdType.MESH,
        )
    for d in range(1, outer):
        pl.semaphore_signal(
            barrier, inc=1, device_id={"paths": lax.rem(z + d, outer) * inner + q},
            device_id_type=pl.DeviceIdType.MESH,
        )

    pending = []

    def over_q(which, source, target):
        copies = []
        for d in range(inner - 1, 0, -1):
            peer = partner(q, d, inner)
            copy = pltpu.make_async_remote_copy(
                src_ref=source(peer), dst_ref=target.at[q],
                send_sem=qsend.at[which, d - 1], recv_sem=qrecv.at[which, d - 1],
                device_id={"paths": z * inner + peer},
                device_id_type=pl.DeviceIdType.MESH,
            )
            copy.start()
            copies.append(copy)
        pending.extend(copies)
        return copies

    def over_z(which, source, target):
        copies = []
        for d in range(outer - 1, 0, -1):
            peer = partner(z, d, outer)
            copy = pltpu.make_async_remote_copy(
                src_ref=source(peer), dst_ref=target.at[z],
                send_sem=zsend.at[which, d - 1], recv_sem=zrecv.at[which, d - 1],
                device_id={"paths": peer * inner + q},
                device_id_type=pl.DeviceIdType.MESH,
            )
            copy.start()
            copies.append(copy)
        pending.extend(copies)
        return copies

    def arrive(copies):
        for copy in copies:
            copy.wait_recv()

    def total(ref, count):
        result = ref[0].astype(F32)
        for i in range(1, count):
            result = result + ref[i].astype(F32)
        return result

    loads[0].wait()
    own_design = design_of(pall[q])
    own_triple = triple(own_design)
    own_turned = jnp.transpose(own_design)[:REGRESSORS, :].astype(BF16)
    gown[...] = own_turned
    loads[1].wait()
    nrow = jnp.broadcast_to(not_ref[...].astype(F32), (8, trades))
    nsend[...] = nrow
    loads[2].wait()
    pl.semaphore_wait(barrier, inner + outer - 2)

    gram_z = over_z(0, lambda peer: gown, gall)
    note_z = over_z(1, lambda peer: nsend, nall)
    trade_z = over_z(2, lambda peer: wall.at[z], wall)
    path_q = over_q(0, lambda peer: pall.at[q], pall)
    gall[z] = own_turned
    nall[z] = nrow

    arrive(gram_z)
    gram_q = over_q(1, lambda peer: gall, gq)
    gq[q] = gall[...]

    for load in loads[3:]:
        load.wait()
    all_levels = tidx_ref[...]
    all_thresholds = jnp.zeros((inner, quarter), F32)
    levels = tidx_ref[pl.ds(q, 1), :]
    thresholds = jnp.zeros((1, quarter), F32)
    for i in range(level_ref.shape[0]):
        thresholds = jnp.where(levels == i, level_ref[i], thresholds)
        all_thresholds = jnp.where(all_levels == i, level_ref[i], all_thresholds)
    thresholds = jnp.transpose(jnp.broadcast_to(thresholds, (quarter, quarter)))[:, :1]
    rate = jnp.transpose(
        jnp.broadcast_to(rate_ref[pl.ds(q, 1), :], (quarter, quarter))
    )[:, :1]
    all_rates = rate_ref[...]
    labels = jnp.concatenate(
        [set_ref[pl.ds(i * inner + q, 1), :] for i in range(outer)], axis=1
    )
    table[...] = set_table(labels, set_total)

    arrive(path_q)
    paths = pall[...].reshape(inner * rows, feats)
    design = design_of(paths)
    design3 = triple(design)
    design_t = jnp.transpose(design)[:REGRESSORS, :].astype(BF16)

    arrive(gram_q)
    turned_all = jnp.concatenate(
        [gq[i, j] for i in range(inner) for j in range(outer)], axis=1
    )
    dstack[...] = jnp.concatenate(
        [turned_all, turned_all, turned_all, jnp.zeros_like(turned_all)], axis=0
    )
    gram = mm(turned_all, dstack[...], NT)
    gram_row = lax.broadcasted_iota(jnp.int32, (REGRESSORS, LANES), 0)
    gram_lane = lax.broadcasted_iota(jnp.int32, (REGRESSORS, LANES), 1)
    ridge = jnp.where(gram_row == gram_lane, RIDGE_SCALE * paths_all, 0.0)
    invert[...] = spd_inverse(gram + ridge)

    arrive(note_z)
    notional = jnp.concatenate([nall[i][0:1, :] for i in range(outer)], axis=1)
    arrive(trade_z)
    weights = wall[...].reshape(outer * trades, feats)
    pre_act = mm(paths, weights, NT)
    small = jnp.exp(-jnp.abs(pre_act))
    tval[...] = (notional * (jnp.maximum(pre_act, 0.0) + jnp.log1p(small))).astype(BF16)
    nsig[...] = notional * (jnp.where(pre_act >= 0.0, 1.0, small) / (1.0 + small))

    by_trade = mm(design_t, tval[...])
    by_set = mm(jnp.concatenate(split3(by_trade), axis=0), table[...], NT)
    moments = (
        by_set[:REGRESSORS] + by_set[REGRESSORS : 2 * REGRESSORS] + by_set[2 * REGRESSORS :]
    )
    for i in range(inner):
        bown[i] = moments[:, i * quarter : (i + 1) * quarter]
    moment_q = over_q(2, lambda peer: bown.at[peer], bq)
    bq[q] = bown[q]
    arrive(moment_q)
    moment_mid = total(bq, inner)
    bzsend[...] = moment_mid
    moment_z = over_z(3, lambda peer: bzsend, bz)
    bz[z] = moment_mid
    arrive(moment_z)
    inverse = invert[:, :REGRESSORS]
    coeffs = precise(inverse, total(bz, outer))
    csend[...] = coeffs
    coeffs_q = over_q(3, lambda peer: csend, cq)
    cq[q] = coeffs
    excess = mm(stack3(coeffs), dstack[...], TN) - thresholds
    fade = jnp.exp(-jnp.abs(excess))
    loss = jnp.maximum(excess, 0.0) + jnp.log1p(fade)
    seed = rate * (jnp.where(excess >= 0.0, 1.0, fade) / (1.0 + fade))
    seed_cut = mm(dstack[:REGRESSORS, :], jnp.concatenate(split3(seed), axis=0), NT)
    seed_sum = (
        seed_cut[:, :quarter] + seed_cut[:, quarter : 2 * quarter] + seed_cut[:, 2 * quarter :]
    )
    solved = precise(inverse, seed_sum)
    loss_part = jnp.sum(rate * jnp.sum(loss, axis=1, keepdims=True), axis=0, keepdims=True)
    answer = jnp.concatenate([solved, jnp.broadcast_to(loss_part, (8, quarter))], axis=0)
    ssend[...] = answer
    answer_q = over_q(4, lambda peer: ssend, sq)
    sq[q] = answer
    arrive(coeffs_q)
    coeffs_all = jnp.concatenate([cq[i] for i in range(inner)], axis=1)
    arrive(answer_q)
    answers = jnp.concatenate([sq[i] for i in range(inner)], axis=1)
    solved_all = answers[:REGRESSORS]
    loss_sum = jnp.sum(answers[REGRESSORS : REGRESSORS + 1], axis=1, keepdims=True) / quarter
    loss_ref[...] = jnp.broadcast_to(loss_sum / (paths_all * set_total), loss_ref.shape)

    picked = mm(jnp.concatenate(split3(solved_all), axis=0), table[...])
    solved3 = jnp.concatenate(
        [picked.astype(BF16), jnp.zeros((LANES - 3 * REGRESSORS, picked.shape[1]), BF16)], axis=0
    )
    spread = mm(design3, solved3).astype(BF16).astype(F32)
    slopes = (nsig[...] * spread).astype(BF16)
    scale = 1.0 / math.sqrt(paths_all)
    weight_part = mm(slopes, paths, TN) * scale
    wown[...] = weight_part.astype(BF16).reshape(outer, trades, feats)
    weight_z = over_z(4, lambda peer: wown.at[peer], wz)
    wz[z] = wown[z]

    pulled = mm(solved3, tval[...], NT)
    pulled = (
        pulled[:REGRESSORS]
        + pulled[REGRESSORS : 2 * REGRESSORS]
        + pulled[2 * REGRESSORS : 3 * REGRESSORS]
    )
    for i in range(inner):
        eown[i] = pulled[:, i * rows : (i + 1) * rows]
    pull_q = over_q(5, lambda peer: eown.at[peer], eq)
    eq[q] = eown[q]
    basis_part = mm(slopes, weights)
    pown[...] = basis_part.astype(BF16).reshape(inner, rows, feats)
    basis_q = over_q(6, lambda peer: pown.at[peer], pq)
    pq[q] = pown[q]

    fitted = mm(own_triple, stack3(coeffs_all))
    full_thresholds = jnp.concatenate([all_thresholds[i : i + 1] for i in range(inner)], axis=1)
    full_rates = jnp.concatenate([all_rates[i : i + 1] for i in range(inner)], axis=1)
    over = fitted - full_thresholds
    tail = jnp.exp(-jnp.abs(over))
    own_seed = full_rates * (jnp.where(over >= 0.0, 1.0, tail) / (1.0 + tail))
    residual = own_seed - mm(own_triple, stack3(solved_all))
    term = precise(coeffs_all, residual, NT) - precise(solved_all, fitted, NT)
    arrive(pull_q)
    term = term + total(eq, inner)
    padded = jnp.concatenate([term, jnp.zeros((LANES - REGRESSORS, rows), F32)], axis=0)
    turned = pltpu.roll(jnp.transpose(padded), LANES - 1, 1)
    lane = lax.broadcasted_iota(jnp.int32, turned.shape, 1)
    turned = jnp.where(lane < REGRESSORS - 1, turned, 0.0)
    arrive(basis_q)
    basis_ref[...] = total(pq, inner)
    basis_ref[:, :LANES] = basis_ref[:, :LANES] + turned
    arrive(weight_z)
    wadj_ref[...] = total(wz, outer)
    for copy in pending:
        copy.wait_send()


def pair_inverse(gram):
    work = augmented(gram)
    row = lax.broadcasted_iota(jnp.int32, work.shape, 0)
    for k in range(0, REGRESSORS, 2):
        left = jnp.broadcast_to(work[:, k : k + 1], work.shape)
        right = jnp.broadcast_to(work[:, k + 1 : k + 2], work.shape)
        a, c = left[k : k + 1, :], left[k + 1 : k + 2, :]
        b, d = right[k : k + 1, :], right[k + 1 : k + 2, :]
        above, below = work[k : k + 1, :], work[k + 1 : k + 2, :]
        factor = 1.0 / (a * d - b * c)
        upper = (d * above - b * below) * factor
        lower = (a * below - c * above) * factor
        rest = work - left * upper - right * lower
        work = jnp.where(row == k, upper, jnp.where(row == k + 1, lower, rest))
    return pltpu.roll(work, LANES - REGRESSORS, 1)


def split2(x):
    hi = x.astype(BF16)
    return hi, (x - hi.astype(F32)).astype(BF16)


def square(
    paths_all, set_total,
    pb_hbm, w_hbm, not_hbm, set_hbm, tidx_hbm, level_hbm, rate_hbm,
    loss_ref, basis_ref, wadj_ref,
    not_ref, set_ref, tidx_ref, level_ref, rate_ref,
    pall, wall, small, dall, dgrid, dstack, dtri, dturn, table, invert,
    bown, bq, bzsend, bz, csend, cq, ssend, sq, lsend, lq, over_ref,
    by_trades, tval, nsig, slopes, pulls,
    wsend, wvia, wnear, wjoin, wz, psend, pvia, pown, pjoin, pq, esend, evia, ejoin, eq,
    local, send, recv, ready, order,
):
    rows, feats = basis_ref.shape
    trades = wadj_ref.shape[0]
    quarter = set_total // 4
    me = lax.axis_index("paths")
    q, z = lax.rem(me, 4), lax.div(me, 4)
    bits = [lax.rem(lax.div(me, weight), 2) for weight in (1, 2, 4, 8)]
    peers = [me] + [partner(me, step, 16) for step in range(1, 16)]
    low, high = bits[2], bits[3]
    inner = low + high - 2 * low * high
    CORE, SIDE, NEAR, FAR = 1, 2, 4, 8
    MID = NEAR + FAR
    trade_steps = (0, NEAR, SIDE, NEAR + SIDE)
    design_steps = (0, CORE, FAR, CORE + FAR)

    loads = [
        pltpu.make_async_copy(source, target, local.at[i])
        for i, (source, target) in enumerate(
            [
                (pb_hbm, pall.at[pl.ds(0, rows)]),
                (not_hbm, not_ref),
                (w_hbm, wall.at[0]),
                (set_hbm, set_ref),
                (tidx_hbm, tidx_ref),
                (level_hbm, level_ref),
                (rate_hbm, rate_ref),
            ]
        )
    ]
    barrier = pltpu.get_barrier_semaphore()

    def greet(semaphore, step):
        pl.semaphore_signal(
            semaphore, inc=1, device_id={"paths": peers[step]},
            device_id_type=pl.DeviceIdType.MESH,
        )

    for i, step in enumerate((CORE, SIDE, NEAR, FAR)):

        @pl.when(bits[i] == 0)
        def _():
            greet(barrier, step)

    @pl.when(inner * (1 - high) == 1)
    def _():
        greet(barrier, MID)

    for load in loads:
        load.start()

    copies, inner_copies, outer_copies = [], [], []
    free_send, free_recv = list(range(SENDS)), list(range(ARRIVALS))

    def wire(source, target, step, s, r):
        return pltpu.make_async_remote_copy(
            src_ref=source, dst_ref=target, send_sem=send.at[s], recv_sem=recv.at[r],
            device_id={"paths": peers[step]}, device_id_type=pl.DeviceIdType.MESH,
        )

    def remote(source, target, step, bag=copies):
        s, r = free_send.pop(0), free_recv.pop(0)
        copy = wire(source, target, step, s, r)
        bag.append((copy, s))
        return copy

    def slot(i):
        return pall.at[pl.ds(i * rows, rows)]

    def start(*group):
        for copy in group:
            copy.start()

    def fence():
        pl.semaphore_signal(order, inc=1)
        pl.semaphore_wait(order, 1)

    def drain(*keep):
        kept = [id(copy) for copy in keep]

        def settle(bag):
            for copy, s in bag:
                if id(copy) not in kept:
                    copy.wait_send()
                    free_send.append(s)
            bag[:] = [pair for pair in bag if id(pair[0]) in kept]

        settle(copies)

        @pl.when(inner == 1)
        def _():
            settle(inner_copies)

        @pl.when(inner == 0)
        def _():
            settle(outer_copies)

    def arrive(*group):
        for copy in group:
            copy.wait_recv()

    def cuts(extent):
        part = extent // PIECES
        return [pl.ds(p * part, part) for p in range(PIECES)]

    def pieces(source, target, step, extent, bag=copies):
        s = free_send.pop(0)
        rs = [free_recv.pop(0) for _ in range(PIECES)]
        bag.append((wire(source, target, step, s, rs[0]), s))
        return [
            wire(source.at[cut], target.at[cut], step, s, r) for cut, r in zip(cuts(extent), rs)
        ]

    def parcel(source, target, step, extent, bag=copies):
        s, r = free_send.pop(0), free_recv.pop(0)
        whole = wire(source, target, step, s, r)
        bag.append((whole, s))
        parts = [wire(source.at[cut], target.at[cut], step, s, r) for cut in cuts(extent)]
        return parts, whole

    def grouped(source, target, place, steps):
        s, r = free_send.pop(0), free_recv.pop(0)
        three = target.at[pl.ds(0, 3)]
        whole = wire(three, three, steps[0], s, r)
        copies.append((whole, s))
        return [wire(source(peers[t]), target.at[place], t, s, r) for t in steps], whole

    def place(i):
        design = design_of(pall[i * rows : (i + 1) * rows, :])
        at = slice(i * rows, (i + 1) * rows)
        dtri[at, :] = triple(design)
        turned = jnp.transpose(design)[:REGRESSORS, :].astype(BF16)
        dturn[:, at] = turned
        return turned

    path_core = remote(pb_hbm, slot(1), CORE)
    trade_side, side_all = parcel(w_hbm, wall.at[2], SIDE, trades)
    trade_near = pieces(w_hbm, wall.at[1], NEAR, trades)
    path_mid = pieces(pb_hbm, slot(2), MID, rows, inner_copies)
    path_far = pieces(pb_hbm, slot(4), FAR, rows, outer_copies)
    small_side = remote(small.at[0], small.at[2], SIDE)
    small_near = remote(small.at[0], small.at[1], NEAR)

    lower = bits[0] + bits[1] + bits[2] + bits[3] + inner * high

    @pl.when(lower > 0)
    def _():
        pl.semaphore_wait(barrier, lower)

    for i, step in enumerate((CORE, SIDE, NEAR)):

        @pl.when(bits[i] == 1)
        def _():
            greet(ready.at[i], step)

    @pl.when(inner * high == 1)
    def _():
        greet(ready.at[3], FAR)
        greet(ready.at[5], MID)

    def down(i, *group):
        @pl.when(bits[i] == 1)
        def _():
            start(*group)

    def up(i, *group):
        @pl.when(bits[i] == 0)
        def _():
            pl.semaphore_wait(ready.at[i], 1)
            start(*group)

    split = PIECES // 2
    down(2, *trade_near[:split])

    @pl.when(inner * high == 1)
    def _():
        start(*path_mid)

    down(1, *trade_side[:split])
    down(0, path_core)
    loads[0].wait()
    own_turned = place(0)
    loads[1].wait()
    note = jnp.broadcast_to(not_ref[...].astype(F32), (16, trades)).astype(BF16)
    small[0] = jnp.concatenate([own_turned, note], axis=0)
    down(2, small_near, *trade_near[split:])
    down(1, small_side, *trade_side[split:])
    up(0, path_core)
    up(1, small_side, *trade_side)
    up(2, small_near, *trade_near)

    @pl.when((1 - inner) * high == 1)
    def _():
        start(*path_far)

    @pl.when(inner * (1 - high) == 1)
    def _():
        pl.semaphore_wait(ready.at[5], 1)
        start(*path_mid)

    @pl.when((1 - inner) * (1 - high) == 1)
    def _():
        pl.semaphore_wait(ready.at[3], 1)
        start(*path_far)

    loads[2].wait()
    small_pass = remote(small.at[1], small.at[3], SIDE)
    trade_pass, pass_all = parcel(wall.at[1], wall.at[3], SIDE, trades)
    mid_pass, mid_all = parcel(slot(2), slot(3), CORE, rows, inner_copies)
    far_pass, far_all = parcel(slot(4), slot(5), CORE, rows, inner_copies)
    used = [r for r in range(ARRIVALS) if r not in free_recv]
    front = pl.ds(0, REGRESSORS)
    design_core = remote(small.at[:, front], dall.at[0], CORE)
    design_far = remote(small.at[:, front], dall.at[1], FAR)
    design_pass = remote(dall.at[1], dall.at[2], CORE)

    for load in loads[3:]:
        load.wait()
    labels = jnp.concatenate([set_ref[pl.ds(peers[s], 1), :] for s in trade_steps], axis=1)
    table[...] = set_table(labels, set_total)

    def value(top, bottom, left, right):
        paths = pall[top:bottom, :]
        weights = wall[left:right].reshape((right - left) * trades, feats)
        notional = jnp.concatenate(
            [small[s, REGRESSORS:, :].astype(F32)[:1, :] for s in range(left, right)], axis=1
        )
        pre_act = mm(paths, weights, NT)
        fade = jnp.exp(-jnp.abs(pre_act))
        at = (slice(top, bottom), slice(left * trades, right * trades))
        tval[at] = (notional * (jnp.maximum(pre_act, 0.0) + jnp.log1p(fade))).astype(BF16)
        nsig[at] = pre_act

    def sigmoid(top, bottom):
        notional = jnp.concatenate(
            [small[s, REGRESSORS:, :].astype(F32)[:1, :] for s in range(4)], axis=1
        )
        pre_act = nsig[top:bottom, :]
        fade = jnp.exp(-jnp.abs(pre_act))
        nsig[top:bottom, :] = notional * (jnp.where(pre_act >= 0.0, 1.0, fade) / (1.0 + fade))

    pair, head, tail, last = 2 * rows, 4 * rows, 5 * rows, 6 * rows
    arrive(path_core)
    place(1)

    @pl.when(inner == 1)
    def _():
        for copy, onward in zip(path_mid, mid_pass):
            arrive(copy)
            start(onward)

    for p, (copy, onward) in enumerate(zip(trade_near, trade_pass)):
        if p == split:
            arrive(small_near)
            start(small_pass)
        arrive(copy)
        start(onward)
    arrive(side_all, small_side)
    value(0, pair, 0, 3)

    @pl.when(inner == 1)
    def _():
        place(2)
        arrive(mid_all)
        place(3)
        value(pair, head, 0, 3)
        for copy, onward in zip(path_far, far_pass):
            arrive(copy)
            start(onward)
        greet(ready.at[4], FAR)
        fence()
        place(4)
        value(head, tail, 0, 3)

    arrive(small_pass)
    start(design_core, design_far)
    fence()
    arrive(pass_all)

    @pl.when(inner == 0)
    def _():
        value(0, pair, 3, 4)
        by_trades[...] = mm(dturn[:, :pair], tval[:pair, :])

    @pl.when(inner == 1)
    def _():
        value(0, tail, 3, 4)
        by_trades[...] = mm(dturn[:, :tail], tval[:tail, :])
        arrive(far_all)
        place(5)
        value(tail, last, 0, 4)
        by_trades[...] = by_trades[...] + mm(dturn[:, tail:], tval[tail:, :])

    by_trade = by_trades[...]
    by_set = mm(jnp.concatenate(split3(by_trade), axis=0), table[...], NT)
    moments = (
        by_set[:REGRESSORS] + by_set[REGRESSORS : 2 * REGRESSORS] + by_set[2 * REGRESSORS :]
    )
    for i in range(4):
        bown[i] = moments[:, i * quarter : (i + 1) * quarter]
    quads = (CORE + SIDE, SIDE, CORE)
    lines = (NEAR + FAR, FAR, NEAR)

    def total(ref, count):
        result = ref[0].astype(F32)
        for i in range(1, count):
            result = result + ref[i].astype(F32)
        return result

    moment_q, moment_all = grouped(lambda peer: bown.at[lax.rem(peer, 4)], bq, q, quads)
    start(*moment_q)
    fence()
    bq[q] = bown[q]

    @pl.when(inner == 1)
    def _():
        arrive(design_far)
        start(design_pass)

    arrive(moment_all)
    bzsend[...] = total(bq, 4)

    @pl.when(inner == 0)
    def _():
        pl.semaphore_wait(ready.at[4], 1)

    moment_z, moment_all = grouped(lambda peer: bzsend, bz, z, lines)
    start(*moment_z)
    fence()
    bz[z] = bzsend[...]
    @pl.when(inner == 0)
    def _():
        arrive(design_far)
        start(design_pass)

    fence()
    arrive(design_core, design_pass)
    for s in range(4):
        dgrid[peers[trade_steps[s]]] = small[s, :REGRESSORS, :]
    for k in range(1, 4):
        for s in range(4):
            dgrid[peers[trade_steps[s] + design_steps[k]]] = dall[k - 1, s]
    turned_all = jnp.concatenate([dgrid[i] for i in range(16)], axis=1)
    dstack[...] = jnp.concatenate(
        [turned_all, turned_all, turned_all, jnp.zeros_like(turned_all)], axis=0
    )
    gram = mm(turned_all, turned_all, NT)
    gram = jnp.concatenate([gram, jnp.zeros((REGRESSORS, LANES - REGRESSORS), F32)], axis=1)
    gram_row = lax.broadcasted_iota(jnp.int32, (REGRESSORS, LANES), 0)
    gram_lane = lax.broadcasted_iota(jnp.int32, (REGRESSORS, LANES), 1)
    ridge = jnp.where(gram_row == gram_lane, RIDGE_SCALE * paths_all, 0.0)
    invert[...] = pair_inverse(gram + ridge)
    fence()
    sigmoid(0, pair)

    @pl.when(inner == 1)
    def _():
        sigmoid(pair, last)

    all_levels = tidx_ref[...]
    all_thresholds = jnp.zeros((4, quarter), F32)
    levels = tidx_ref[pl.ds(q, 1), :]
    thresholds = jnp.zeros((1, quarter), F32)
    for i in range(level_ref.shape[0]):
        thresholds = jnp.where(levels == i, level_ref[i], thresholds)
        all_thresholds = jnp.where(all_levels == i, level_ref[i], all_thresholds)
    thresholds = jnp.transpose(jnp.broadcast_to(thresholds, (quarter, quarter)))[:, :1]
    rate = jnp.transpose(
        jnp.broadcast_to(rate_ref[pl.ds(q, 1), :], (quarter, quarter))
    )[:, :1]
    all_rates = rate_ref[...]
    full_thresholds = jnp.concatenate([all_thresholds[i : i + 1] for i in range(4)], axis=1)
    full_rates = jnp.concatenate([all_rates[i : i + 1] for i in range(4)], axis=1)

    arrive(moment_all)
    inverse = invert[:, :REGRESSORS]
    coeffs = precise(inverse, total(bz, 4))
    csend[...] = coeffs
    coeffs_q, coeffs_all_sent = grouped(lambda peer: csend, cq, q, quads)
    cq[q] = coeffs
    excess = mm(stack3(coeffs), dstack[...], TN) - thresholds
    over_ref[...] = excess
    fade = jnp.exp(-jnp.abs(excess))
    seed = rate * (jnp.where(excess >= 0.0, 1.0, fade) / (1.0 + fade))
    seed_cut = mm(dstack[:REGRESSORS, :], jnp.concatenate(split2(seed), axis=0), NT)
    seed_sum = seed_cut[:, :quarter] + seed_cut[:, quarter:]
    solved = precise(inverse, seed_sum)
    ssend[...] = solved
    answer_q, answer_all = grouped(lambda peer: ssend, sq, q, quads)
    start(*answer_q)
    start(*coeffs_q)
    fence()
    sq[q] = solved

    excess = over_ref[...]
    loss = jnp.maximum(excess, 0.0) + jnp.log1p(jnp.exp(-jnp.abs(excess)))
    loss_part = jnp.sum(rate * jnp.sum(loss, axis=1, keepdims=True), axis=0, keepdims=True)
    lsend[...] = jnp.broadcast_to(loss_part, lsend.shape)
    lq[q] = lsend[...]
    loss_q, loss_all = grouped(lambda peer: lsend, lq, q, quads)
    start(*loss_q)
    fence()

    drain(answer_all, coeffs_all_sent, loss_all)
    arrive(answer_all)
    solved_all = jnp.concatenate([sq[i] for i in range(4)], axis=1)
    picked = mm(jnp.concatenate(split3(solved_all), axis=0), table[...])
    solved3 = jnp.concatenate(
        [picked.astype(BF16), jnp.zeros((LANES - 3 * REGRESSORS, picked.shape[1]), BF16)], axis=0
    )

    def slope(top, bottom, left, right):
        at = (slice(top, bottom), slice(left * trades, right * trades))
        spread = mm(dtri[top:bottom, :], solved3[:, at[1]]).astype(BF16).astype(F32)
        slopes[at] = (nsig[at] * spread).astype(BF16)

    scale = 1.0 / math.sqrt(paths_all)

    def basis_part(first, final):
        return mm(slopes[first * rows : final * rows, :], wall[...].reshape(4 * trades, feats))

    def weight_part(left, right, depth):
        cut = slopes[:depth, left * trades : right * trades]
        return mm(cut, pall[:depth, :], TN) * scale

    free_recv.extend(used)
    basis_via = [remote(psend.at[i], pvia.at[i], CORE, inner_copies) for i in range(2)]
    basis_core = remote(psend.at[2], pq.at[0], CORE)
    basis_far = remote(pjoin.at[0], pq.at[1], FAR, inner_copies)
    basis_mid = remote(pjoin.at[1], pq.at[1], MID, inner_copies)
    pull_via = [remote(esend.at[i], evia.at[i], CORE, inner_copies) for i in range(2)]
    pull_core = remote(esend.at[2], eq.at[0], CORE)
    pull_far = remote(ejoin.at[0], eq.at[1], FAR, inner_copies)
    pull_mid = remote(ejoin.at[1], eq.at[1], MID, inner_copies)
    weight_via = pieces(wsend.at[0], wvia, SIDE, trades)
    weight_side = remote(wsend.at[1], wz.at[0], SIDE)

    def give(i, slot, depth, *group):
        wsend[i] = weight_part(slot, slot + 1, depth).astype(BF16)
        start(*group)
        fence()

    def join(i, onward):
        arrive(basis_via[i])
        pjoin[i] = (pown[i] + pvia[i].astype(F32)).astype(BF16)
        start(onward)
        fence()

    def pull(depth):
        pulled = mm(solved3, tval[:depth, :], NT)
        pulls[:, :depth] = (
            pulled[:REGRESSORS]
            + pulled[REGRESSORS : 2 * REGRESSORS]
            + pulled[2 * REGRESSORS : 3 * REGRESSORS]
        )

    @pl.when(inner == 1)
    def _():
        slope(0, last, 3, 4)
        give(0, 3, last, *weight_via)
        slope(head, last, 0, 3)
        part = basis_part(4, 6)
        psend[0] = part[rows:].astype(BF16)
        start(basis_via[0])
        fence()
        pown[0] = part[:rows]
        slope(0, head, 0, 3)
        psend[1] = basis_part(3, 4).astype(BF16)
        start(basis_via[1])
        fence()
        give(1, 2, last, weight_side)
        join(0, basis_far)
        pull(last)
        esend[0] = pulls[:, tail:]
        esend[1] = pulls[:, 3 * rows : head]
        esend[2] = pulls[:, rows:pair]
        start(*pull_via, pull_core)
        fence()
        part = basis_part(1, 3)
        pown[1] = part[rows:]
        psend[2] = part[:rows].astype(BF16)
        start(basis_core)
        fence()
        arrive(*pull_via)
        ejoin[0] = pulls[:, head:tail] + evia[0]
        ejoin[1] = pulls[:, pair : 3 * rows] + evia[1]
        start(pull_far, pull_mid)
        fence()
        join(1, basis_mid)
        wnear[...] = weight_part(1, 2, last)

    @pl.when(inner == 0)
    def _():
        slope(0, pair, 3, 4)
        give(0, 3, pair, *weight_via)
        slope(0, pair, 0, 3)
        give(1, 2, pair, weight_side)
        psend[2] = basis_part(1, 2).astype(BF16)
        start(basis_core)
        fence()
        wnear[...] = weight_part(1, 2, pair)
        pull(pair)
        esend[2] = pulls[:, rows:pair]
        start(pull_core)
        fence()

    weight_near = pieces(wjoin, wz.at[1], NEAR, trades)
    near_all = copies[-1][0]
    for p, (copy, onward) in enumerate(zip(weight_via, weight_near)):
        cut = slice(p * trades // PIECES, (p + 1) * trades // PIECES)
        arrive(copy)
        wjoin[cut, :] = (wnear[cut, :] + wvia[cut, :].astype(F32)).astype(BF16)
        start(onward)

    fence()

    @pl.when(inner == 1)
    def _():
        wadj_ref[...] = weight_part(0, 1, last)

    @pl.when(inner == 0)
    def _():
        wadj_ref[...] = weight_part(0, 1, pair)

    basis_ref[...] = basis_part(0, 1)

    arrive(coeffs_all_sent)
    own_triple = dtri[:rows, :]
    coeffs_all = jnp.concatenate([cq[i] for i in range(4)], axis=1)
    fitted = mm(own_triple, stack3(coeffs_all))
    over = fitted - full_thresholds
    fall = jnp.exp(-jnp.abs(over))
    own_seed = full_rates * (jnp.where(over >= 0.0, 1.0, fall) / (1.0 + fall))
    residual = own_seed - mm(own_triple, stack3(solved_all))
    term = precise(coeffs_all, residual, NT) - precise(solved_all, fitted, NT)
    term = term + pulls[:, :rows]
    arrive(loss_all)
    answers = jnp.concatenate([lq[i] for i in range(4)], axis=1)
    loss_sum = jnp.sum(answers[:1], axis=1, keepdims=True) / quarter
    loss_ref[...] = jnp.broadcast_to(loss_sum / (paths_all * set_total), loss_ref.shape)
    arrive(basis_core)
    basis_ref[...] = basis_ref[...] + pq[0].astype(F32)
    arrive(weight_side)
    wadj_ref[...] = wadj_ref[...] + wz[0].astype(F32)

    @pl.when(inner == 1)
    def _():
        arrive(basis_mid)

    @pl.when(inner == 0)
    def _():
        arrive(basis_far)

    basis_ref[...] = basis_ref[...] + pq[1].astype(F32)
    drain(near_all, basis_mid, pull_far, pull_mid)
    arrive(pull_core)

    @pl.when(inner == 1)
    def _():
        arrive(pull_mid)

    @pl.when(inner == 0)
    def _():
        arrive(pull_far)

    term = term + eq[0] + eq[1]
    padded = jnp.concatenate([term, jnp.zeros((LANES - REGRESSORS, rows), F32)], axis=0)
    turned = pltpu.roll(jnp.transpose(padded), LANES - 1, 1)
    lane = lax.broadcasted_iota(jnp.int32, turned.shape, 1)
    turned = jnp.where(lane < REGRESSORS - 1, turned, 0.0)
    basis_ref[:, :LANES] = basis_ref[:, :LANES] + turned
    for p, copy in enumerate(weight_near):
        cut = slice(p * trades // PIECES, (p + 1) * trades // PIECES)
        arrive(copy)
        wadj_ref[cut, :] = wadj_ref[cut, :] + wz[1, cut, :].astype(F32)
    drain()


def square_scratch(rows, trades, feats, set_total):
    size, quarter = REGRESSORS, set_total // 4
    return [
        pltpu.VMEM((6 * rows, feats), BF16),
        pltpu.VMEM((4, trades, feats), BF16),
        pltpu.VMEM((4, size + 16, trades), BF16),
        pltpu.VMEM((3, 4, size, rows), BF16),
        pltpu.VMEM((16, size, rows), BF16),
        pltpu.VMEM((LANES, 16 * rows), BF16),
        pltpu.VMEM((6 * rows, LANES), BF16),
        pltpu.VMEM((size, 6 * rows), BF16),
        pltpu.VMEM((set_total, 4 * trades), BF16),
        pltpu.VMEM((size, LANES), F32),
        pltpu.VMEM((4, size, quarter), F32),
        pltpu.VMEM((4, size, quarter), F32),
        pltpu.VMEM((size, quarter), F32),
        pltpu.VMEM((4, size, quarter), F32),
        pltpu.VMEM((size, quarter), F32),
        pltpu.VMEM((4, size, quarter), F32),
        pltpu.VMEM((size, quarter), F32),
        pltpu.VMEM((4, size, quarter), F32),
        pltpu.VMEM((8, quarter), F32),
        pltpu.VMEM((4, 8, quarter), F32),
        pltpu.VMEM((quarter, 16 * rows), F32),
        pltpu.VMEM((size, 4 * trades), F32),
        pltpu.VMEM((6 * rows, 4 * trades), BF16),
        pltpu.VMEM((6 * rows, 4 * trades), F32),
        pltpu.VMEM((6 * rows, 4 * trades), BF16),
        pltpu.VMEM((size, 6 * rows), F32),
        pltpu.VMEM((2, trades, feats), BF16),
        pltpu.VMEM((trades, feats), BF16),
        pltpu.VMEM((trades, feats), F32),
        pltpu.VMEM((trades, feats), BF16),
        pltpu.VMEM((2, trades, feats), BF16),
        pltpu.VMEM((3, rows, feats), BF16),
        pltpu.VMEM((2, rows, feats), BF16),
        pltpu.VMEM((2, rows, feats), F32),
        pltpu.VMEM((2, rows, feats), BF16),
        pltpu.VMEM((2, rows, feats), BF16),
        pltpu.VMEM((3, size, rows), F32),
        pltpu.VMEM((2, size, rows), F32),
        pltpu.VMEM((2, size, rows), F32),
        pltpu.VMEM((2, size, rows), F32),
        pltpu.SemaphoreType.DMA((7,)),
        pltpu.SemaphoreType.DMA((SENDS,)),
        pltpu.SemaphoreType.DMA((ARRIVALS,)),
        pltpu.SemaphoreType.REGULAR((6,)),
        pltpu.SemaphoreType.REGULAR,
    ]


def chain_scratch(inner, outer, rows, trades, feats, set_total):
    size, quarter, count = REGRESSORS, set_total // inner, inner * outer
    z_pairs, q_pairs = max(outer - 1, 1), max(inner - 1, 1)
    return [
        pltpu.VMEM((inner, rows, feats), BF16),
        pltpu.VMEM((outer, trades, feats), BF16),
        pltpu.VMEM((outer, 8, trades), F32),
        pltpu.VMEM((8, trades), F32),
        pltpu.VMEM((size, rows), BF16),
        pltpu.VMEM((outer, size, rows), BF16),
        pltpu.VMEM((inner, outer, size, rows), BF16),
        pltpu.VMEM((LANES, count * rows), BF16),
        pltpu.VMEM((set_total, outer * trades), BF16),
        pltpu.VMEM((size, LANES), F32),
        pltpu.VMEM((inner, size, quarter), F32),
        pltpu.VMEM((inner, size, quarter), F32),
        pltpu.VMEM((size, quarter), F32),
        pltpu.VMEM((outer, size, quarter), F32),
        pltpu.VMEM((size, quarter), F32),
        pltpu.VMEM((inner, size, quarter), F32),
        pltpu.VMEM((size + 8, quarter), F32),
        pltpu.VMEM((inner, size + 8, quarter), F32),
        pltpu.VMEM((inner, size, rows), F32),
        pltpu.VMEM((inner, size, rows), F32),
        pltpu.VMEM((outer, trades, feats), BF16),
        pltpu.VMEM((outer, trades, feats), BF16),
        pltpu.VMEM((inner, rows, feats), BF16),
        pltpu.VMEM((inner, rows, feats), BF16),
        pltpu.VMEM((inner * rows, outer * trades), F32),
        pltpu.VMEM((inner * rows, outer * trades), BF16),
        pltpu.SemaphoreType.DMA((7,)),
        pltpu.SemaphoreType.DMA((5, z_pairs)),
        pltpu.SemaphoreType.DMA((5, z_pairs)),
        pltpu.SemaphoreType.DMA((7, q_pairs)),
        pltpu.SemaphoreType.DMA((7, q_pairs)),
    ]


def shards(
    path_basis, proxy_weight, notional, set_of, threshold_index, threshold_levels, loss_rate
):
    count = lax.axis_size("paths")
    inner = math.gcd(4, count)
    outer = count // inner
    rows, feats = path_basis.shape
    trades = proxy_weight.shape[0]
    set_total = loss_rate.shape[0]
    quarter = set_total // inner
    vmem = pl.BlockSpec(memory_space=pltpu.VMEM)
    if count == 16 and rows == trades and rows % (16 * PIECES) == 0:
        body = functools.partial(square, rows * count, set_total)
        scratch = square_scratch(rows, trades, feats, set_total)
    else:
        body = functools.partial(kernel, inner, outer, rows * count, set_total)
        scratch = chain_scratch(inner, outer, rows, trades, feats, set_total)
    loss, basis_adjoint, weight_adjoint = pl.pallas_call(
        body,
        out_shape=(
            jax.ShapeDtypeStruct((1, LANES), F32),
            jax.ShapeDtypeStruct((rows, feats), F32),
            jax.ShapeDtypeStruct((trades, feats), F32),
        ),
        in_specs=[pl.BlockSpec(memory_space=pltpu.HBM)] * 7,
        out_specs=(vmem, vmem, vmem),
        scratch_shapes=[
            pltpu.VMEM((1, trades), BF16),
            pltpu.VMEM((inner * outer, trades), jnp.int32),
            pltpu.VMEM((inner, quarter), jnp.int32),
            pltpu.SMEM(threshold_levels.shape, F32),
            pltpu.VMEM((inner, quarter), F32),
            *scratch,
        ],
        compiler_params=pltpu.CompilerParams(
            collective_id=0, has_side_effects=True, vmem_limit_bytes=48 * 1024 * 1024
        ),
    )(
        *(
            pltpu.with_memory_space_constraint(operand, pltpu.HBM)
            for operand in (
                path_basis,
                proxy_weight,
                notional.reshape(1, trades),
                set_of.reshape(-1, trades),
                threshold_index.reshape(inner, quarter),
                threshold_levels,
                loss_rate.reshape(inner, quarter),
            )
        )
    )
    return loss[0, :1], basis_adjoint, weight_adjoint


def solution(mesh):
    placed = (
        P(("groups", "paths"), None),
        P(("groups", "paths"), None),
        P(("groups", "paths")),
        P("groups"),
        P("groups"),
        P("groups"),
        P("groups"),
    )
    return jax.shard_map(
        shards,
        mesh=mesh,
        in_specs=placed,
        out_specs=(P("groups"), P(("groups", "paths"), None), P(("groups", "paths"), None)),
        check_vma=False,
    )
```

```python
import functools
import math

import jax
import jax.numpy as jnp
from jax import lax
from jax.experimental import pallas as pl
from jax.experimental.pallas import tpu as pltpu
from jax.sharding import PartitionSpec as P

REGRESSORS = 32
RIDGE_SCALE = 0.01
PRECISE = lax.Precision.HIGHEST
LANES = 128
PIECES = 4
SENDS = 19
ARRIVALS = 28
F32 = jnp.float32
BF16 = jnp.bfloat16

NN = (((1,), (0,)), ((), ()))
NT = (((1,), (1,)), ((), ()))
TN = (((0,), (0,)), ((), ()))


def mm(a, b, dims=NN):
    return lax.dot_general(a, b, dims, preferred_element_type=F32)


def precise(a, b, dims=NN):
    return lax.dot_general(a, b, dims, precision=PRECISE, preferred_element_type=F32)


def split3(x):
    hi = x.astype(BF16)
    rest = x - hi.astype(F32)
    mid = rest.astype(BF16)
    lo = (rest - mid.astype(F32)).astype(BF16)
    return hi, mid, lo


def stack3(x):
    hi, mid, lo = split3(x)
    return jnp.concatenate([hi, mid, lo, jnp.zeros_like(hi)], axis=0)


def design_of(basis):
    front = pltpu.roll(basis[:, :LANES].astype(F32), 1, 1)
    lane = lax.broadcasted_iota(jnp.int32, front.shape, 1)
    return jnp.where(lane == 0, 1.0, jnp.where(lane < REGRESSORS, front, 0.0))


def triple(design):
    return (
        design + pltpu.roll(design, REGRESSORS, 1) + pltpu.roll(design, 2 * REGRESSORS, 1)
    ).astype(BF16)


def augmented(gram):
    row = lax.broadcasted_iota(jnp.int32, gram.shape, 0)
    lane = lax.broadcasted_iota(jnp.int32, gram.shape, 1)
    return jnp.where(lane < REGRESSORS, gram, jnp.where(lane == row + REGRESSORS, 1.0, 0.0))


def eliminate(work, first, last):
    row = lax.broadcasted_iota(jnp.int32, work.shape, 0)
    for k in range(first, last):
        column = jnp.broadcast_to(work[:, k : k + 1], work.shape)
        pivot = work[k : k + 1, :] / column[k : k + 1, :]
        work = jnp.where(row == k, pivot, work - column * pivot)
    return work


def spd_inverse(gram):
    work = eliminate(augmented(gram), 0, REGRESSORS)
    return pltpu.roll(work, LANES - REGRESSORS, 1)


def set_table(labels, set_total):
    sets = lax.broadcasted_iota(jnp.int32, (set_total, labels.shape[1]), 0)
    return jnp.where(sets == labels, 1.0, 0.0).astype(BF16)


def partner(index, step, count):
    if count & (count - 1):
        return lax.rem(index + step, count)
    result, weight = 0, 1
    while weight < count:
        bit = lax.rem(lax.div(index, weight), 2)
        result = result + weight * (1 - bit if step & weight else bit)
        weight *= 2
    return result


def kernel(
    inner, outer, paths_all, set_total,
    pb_hbm, w_hbm, not_hbm, set_hbm, tidx_hbm, level_hbm, rate_hbm,
    loss_ref, basis_ref, wadj_ref,
    not_ref, set_ref, tidx_ref, level_ref, rate_ref,
    pall, wall, nall, nsend, gown, gall, gq, dstack, table, invert,
    bown, bq, bzsend, bz, csend, cq, ssend, sq,
    eown, eq, wown, wz, pown, pq, nsig, tval,
    local, zsend, zrecv, qsend, qrecv,
):
    rows, feats = basis_ref.shape
    trades = wadj_ref.shape[0]
    quarter = set_total // inner
    me = lax.axis_index("paths")
    q = lax.rem(me, inner)
    z = lax.div(me, inner)

    loads = [
        pltpu.make_async_copy(source, target, local.at[i])
        for i, (source, target) in enumerate(
            [
                (pb_hbm, pall.at[q]),
                (not_hbm, not_ref),
                (w_hbm, wall.at[z]),
                (set_hbm, set_ref),
                (tidx_hbm, tidx_ref),
                (level_hbm, level_ref),
                (rate_hbm, rate_ref),
            ]
        )
    ]
    for load in loads:
        load.start()

    barrier = pltpu.get_barrier_semaphore()
    for d in range(1, inner):
        pl.semaphore_signal(
            barrier, inc=1, device_id={"paths": z * inner + lax.rem(q + d, inner)},
            device_id_type=pl.DeviceIdType.MESH,
        )
    for d in range(1, outer):
        pl.semaphore_signal(
            barrier, inc=1, device_id={"paths": lax.rem(z + d, outer) * inner + q},
            device_id_type=pl.DeviceIdType.MESH,
        )

    pending = []

    def over_q(which, source, target):
        copies = []
        for d in range(inner - 1, 0, -1):
            peer = partner(q, d, inner)
            copy = pltpu.make_async_remote_copy(
                src_ref=source(peer), dst_ref=target.at[q],
                send_sem=qsend.at[which, d - 1], recv_sem=qrecv.at[which, d - 1],
                device_id={"paths": z * inner + peer},
                device_id_type=pl.DeviceIdType.MESH,
            )
            copy.start()
            copies.append(copy)
        pending.extend(copies)
        return copies

    def over_z(which, source, target):
        copies = []
        for d in range(outer - 1, 0, -1):
            peer = partner(z, d, outer)
            copy = pltpu.make_async_remote_copy(
                src_ref=source(peer), dst_ref=target.at[z],
                send_sem=zsend.at[which, d - 1], recv_sem=zrecv.at[which, d - 1],
                device_id={"paths": peer * inner + q},
                device_id_type=pl.DeviceIdType.MESH,
            )
            copy.start()
            copies.append(copy)
        pending.extend(copies)
        return copies

    def arrive(copies):
        for copy in copies:
            copy.wait_recv()

    def total(ref, count):
        result = ref[0].astype(F32)
        for i in range(1, count):
            result = result + ref[i].astype(F32)
        return result

    loads[0].wait()
    own_design = design_of(pall[q])
    own_triple = triple(own_design)
    own_turned = jnp.transpose(own_design)[:REGRESSORS, :].astype(BF16)
    gown[...] = own_turned
    loads[1].wait()
    nrow = jnp.broadcast_to(not_ref[...].astype(F32), (8, trades))
    nsend[...] = nrow
    loads[2].wait()
    pl.semaphore_wait(barrier, inner + outer - 2)

    gram_z = over_z(0, lambda peer: gown, gall)
    note_z = over_z(1, lambda peer: nsend, nall)
    trade_z = over_z(2, lambda peer: wall.at[z], wall)
    path_q = over_q(0, lambda peer: pall.at[q], pall)
    gall[z] = own_turned
    nall[z] = nrow

    arrive(gram_z)
    gram_q = over_q(1, lambda peer: gall, gq)
    gq[q] = gall[...]

    for load in loads[3:]:
        load.wait()
    all_levels = tidx_ref[...]
    all_thresholds = jnp.zeros((inner, quarter), F32)
    levels = tidx_ref[pl.ds(q, 1), :]
    thresholds = jnp.zeros((1, quarter), F32)
    for i in range(level_ref.shape[0]):
        thresholds = jnp.where(levels == i, level_ref[i], thresholds)
        all_thresholds = jnp.where(all_levels == i, level_ref[i], all_thresholds)
    thresholds = jnp.transpose(jnp.broadcast_to(thresholds, (quarter, quarter)))[:, :1]
    rate = jnp.transpose(
        jnp.broadcast_to(rate_ref[pl.ds(q, 1), :], (quarter, quarter))
    )[:, :1]
    all_rates = rate_ref[...]
    labels = jnp.concatenate(
        [set_ref[pl.ds(i * inner + q, 1), :] for i in range(outer)], axis=1
    )
    table[...] = set_table(labels, set_total)

    arrive(path_q)
    paths = pall[...].reshape(inner * rows, feats)
    design = design_of(paths)
    design3 = triple(design)
    design_t = jnp.transpose(design)[:REGRESSORS, :].astype(BF16)

    arrive(gram_q)
    turned_all = jnp.concatenate(
        [gq[i, j] for i in range(inner) for j in range(outer)], axis=1
    )
    dstack[...] = jnp.concatenate(
        [turned_all, turned_all, turned_all, jnp.zeros_like(turned_all)], axis=0
    )
    gram = mm(turned_all, dstack[...], NT)
    gram_row = lax.broadcasted_iota(jnp.int32, (REGRESSORS, LANES), 0)
    gram_lane = lax.broadcasted_iota(jnp.int32, (REGRESSORS, LANES), 1)
    ridge = jnp.where(gram_row == gram_lane, RIDGE_SCALE * paths_all, 0.0)
    invert[...] = spd_inverse(gram + ridge)

    arrive(note_z)
    notional = jnp.concatenate([nall[i][0:1, :] for i in range(outer)], axis=1)
    arrive(trade_z)
    weights = wall[...].reshape(outer * trades, feats)
    pre_act = mm(paths, weights, NT)
    small = jnp.exp(-jnp.abs(pre_act))
    tval[...] = (notional * (jnp.maximum(pre_act, 0.0) + jnp.log1p(small))).astype(BF16)
    nsig[...] = notional * (jnp.where(pre_act >= 0.0, 1.0, small) / (1.0 + small))

    by_trade = mm(design_t, tval[...])
    by_set = mm(jnp.concatenate(split3(by_trade), axis=0), table[...], NT)
    moments = (
        by_set[:REGRESSORS] + by_set[REGRESSORS : 2 * REGRESSORS] + by_set[2 * REGRESSORS :]
    )
    for i in range(inner):
        bown[i] = moments[:, i * quarter : (i + 1) * quarter]
    moment_q = over_q(2, lambda peer: bown.at[peer], bq)
    bq[q] = bown[q]
    arrive(moment_q)
    moment_mid = total(bq, inner)
    bzsend[...] = moment_mid
    moment_z = over_z(3, lambda peer: bzsend, bz)
    bz[z] = moment_mid
    arrive(moment_z)
    inverse = invert[:, :REGRESSORS]
    coeffs = precise(inverse, total(bz, outer))
    csend[...] = coeffs
    coeffs_q = over_q(3, lambda peer: csend, cq)
    cq[q] = coeffs
    excess = mm(stack3(coeffs), dstack[...], TN) - thresholds
    fade = jnp.exp(-jnp.abs(excess))
    loss = jnp.maximum(excess, 0.0) + jnp.log1p(fade)
    seed = rate * (jnp.where(excess >= 0.0, 1.0, fade) / (1.0 + fade))
    seed_cut = mm(dstack[:REGRESSORS, :], jnp.concatenate(split3(seed), axis=0), NT)
    seed_sum = (
        seed_cut[:, :quarter] + seed_cut[:, quarter : 2 * quarter] + seed_cut[:, 2 * quarter :]
    )
    solved = precise(inverse, seed_sum)
    loss_part = jnp.sum(rate * jnp.sum(loss, axis=1, keepdims=True), axis=0, keepdims=True)
    answer = jnp.concatenate([solved, jnp.broadcast_to(loss_part, (8, quarter))], axis=0)
    ssend[...] = answer
    answer_q = over_q(4, lambda peer: ssend, sq)
    sq[q] = answer
    arrive(coeffs_q)
    coeffs_all = jnp.concatenate([cq[i] for i in range(inner)], axis=1)
    arrive(answer_q)
    answers = jnp.concatenate([sq[i] for i in range(inner)], axis=1)
    solved_all = answers[:REGRESSORS]
    loss_sum = jnp.sum(answers[REGRESSORS : REGRESSORS + 1], axis=1, keepdims=True) / quarter
    loss_ref[...] = jnp.broadcast_to(loss_sum / (paths_all * set_total), loss_ref.shape)

    picked = mm(jnp.concatenate(split3(solved_all), axis=0), table[...])
    solved3 = jnp.concatenate(
        [picked.astype(BF16), jnp.zeros((LANES - 3 * REGRESSORS, picked.shape[1]), BF16)], axis=0
    )
    spread = mm(design3, solved3).astype(BF16).astype(F32)
    slopes = (nsig[...] * spread).astype(BF16)
    scale = 1.0 / math.sqrt(paths_all)
    weight_part = mm(slopes, paths, TN) * scale
    wown[...] = weight_part.astype(BF16).reshape(outer, trades, feats)
    weight_z = over_z(4, lambda peer: wown.at[peer], wz)
    wz[z] = wown[z]

    pulled = mm(solved3, tval[...], NT)
    pulled = (
        pulled[:REGRESSORS]
        + pulled[REGRESSORS : 2 * REGRESSORS]
        + pulled[2 * REGRESSORS : 3 * REGRESSORS]
    )
    for i in range(inner):
        eown[i] = pulled[:, i * rows : (i + 1) * rows]
    pull_q = over_q(5, lambda peer: eown.at[peer], eq)
    eq[q] = eown[q]
    basis_part = mm(slopes, weights)
    pown[...] = basis_part.astype(BF16).reshape(inner, rows, feats)
    basis_q = over_q(6, lambda peer: pown.at[peer], pq)
    pq[q] = pown[q]

    fitted = mm(own_triple, stack3(coeffs_all))
    full_thresholds = jnp.concatenate([all_thresholds[i : i + 1] for i in range(inner)], axis=1)
    full_rates = jnp.concatenate([all_rates[i : i + 1] for i in range(inner)], axis=1)
    over = fitted - full_thresholds
    tail = jnp.exp(-jnp.abs(over))
    own_seed = full_rates * (jnp.where(over >= 0.0, 1.0, tail) / (1.0 + tail))
    residual = own_seed - mm(own_triple, stack3(solved_all))
    term = precise(coeffs_all, residual, NT) - precise(solved_all, fitted, NT)
    arrive(pull_q)
    term = term + total(eq, inner)
    padded = jnp.concatenate([term, jnp.zeros((LANES - REGRESSORS, rows), F32)], axis=0)
    turned = pltpu.roll(jnp.transpose(padded), LANES - 1, 1)
    lane = lax.broadcasted_iota(jnp.int32, turned.shape, 1)
    turned = jnp.where(lane < REGRESSORS - 1, turned, 0.0)
    arrive(basis_q)
    basis_ref[...] = total(pq, inner)
    basis_ref[:, :LANES] = basis_ref[:, :LANES] + turned
    arrive(weight_z)
    wadj_ref[...] = total(wz, outer)
    for copy in pending:
        copy.wait_send()


def pair_inverse(gram):
    work = augmented(gram)
    row = lax.broadcasted_iota(jnp.int32, work.shape, 0)
    for k in range(0, REGRESSORS, 2):
        left = jnp.broadcast_to(work[:, k : k + 1], work.shape)
        right = jnp.broadcast_to(work[:, k + 1 : k + 2], work.shape)
        a, c = left[k : k + 1, :], left[k + 1 : k + 2, :]
        b, d = right[k : k + 1, :], right[k + 1 : k + 2, :]
        above, below = work[k : k + 1, :], work[k + 1 : k + 2, :]
        factor = 1.0 / (a * d - b * c)
        upper = (d * above - b * below) * factor
        lower = (a * below - c * above) * factor
        rest = work - left * upper - right * lower
        work = jnp.where(row == k, upper, jnp.where(row == k + 1, lower, rest))
    return pltpu.roll(work, LANES - REGRESSORS, 1)


def split2(x):
    hi = x.astype(BF16)
    return hi, (x - hi.astype(F32)).astype(BF16)


def square(
    paths_all, set_total,
    pb_hbm, w_hbm, not_hbm, set_hbm, tidx_hbm, level_hbm, rate_hbm,
    loss_ref, basis_ref, wadj_ref,
    not_ref, set_ref, tidx_ref, level_ref, rate_ref,
    pall, wall, small, dall, dgrid, dstack, dtri, dturn, table, invert,
    bown, bq, bzsend, bz, csend, cq, ssend, sq, lsend, lq, over_ref,
    by_trades, tval, nsig, slopes, pulls,
    wsend, wvia, wnear, wjoin, wz, psend, pvia, pown, pjoin, pq, esend, evia, ejoin, eq,
    local, send, recv, ready, order,
):
    rows, feats = basis_ref.shape
    trades = wadj_ref.shape[0]
    quarter = set_total // 4
    me = lax.axis_index("paths")
    q, z = lax.rem(me, 4), lax.div(me, 4)
    bits = [lax.rem(lax.div(me, weight), 2) for weight in (1, 2, 4, 8)]
    peers = [me] + [partner(me, step, 16) for step in range(1, 16)]
    low, high = bits[2], bits[3]
    inner = low + high - 2 * low * high
    CORE, SIDE, NEAR, FAR = 1, 2, 4, 8
    MID = NEAR + FAR
    trade_steps = (0, NEAR, SIDE, NEAR + SIDE)
    design_steps = (0, CORE, FAR, CORE + FAR)

    loads = [
        pltpu.make_async_copy(source, target, local.at[i])
        for i, (source, target) in enumerate(
            [
                (pb_hbm, pall.at[pl.ds(0, rows)]),
                (not_hbm, not_ref),
                (w_hbm, wall.at[0]),
                (set_hbm, set_ref),
                (tidx_hbm, tidx_ref),
                (level_hbm, level_ref),
                (rate_hbm, rate_ref),
            ]
        )
    ]
    barrier = pltpu.get_barrier_semaphore()

    def greet(semaphore, step):
        pl.semaphore_signal(
            semaphore, inc=1, device_id={"paths": peers[step]},
            device_id_type=pl.DeviceIdType.MESH,
        )

    for i, step in enumerate((CORE, SIDE, NEAR, FAR)):

        @pl.when(bits[i] == 0)
        def _():
            greet(barrier, step)

    @pl.when(inner * (1 - high) == 1)
    def _():
        greet(barrier, MID)

    for load in loads:
        load.start()

    copies, inner_copies, outer_copies = [], [], []
    free_send, free_recv = list(range(SENDS)), list(range(ARRIVALS))

    def wire(source, target, step, s, r):
        return pltpu.make_async_remote_copy(
            src_ref=source, dst_ref=target, send_sem=send.at[s], recv_sem=recv.at[r],
            device_id={"paths": peers[step]}, device_id_type=pl.DeviceIdType.MESH,
        )

    def remote(source, target, step, bag=copies):
        s, r = free_send.pop(0), free_recv.pop(0)
        copy = wire(source, target, step, s, r)
        bag.append((copy, s))
        return copy

    def slot(i):
        return pall.at[pl.ds(i * rows, rows)]

    def start(*group):
        for copy in group:
            copy.start()

    def fence():
        pl.semaphore_signal(order, inc=1)
        pl.semaphore_wait(order, 1)

    def drain(*keep):
        kept = [id(copy) for copy in keep]

        def settle(bag):
            for copy, s in bag:
                if id(copy) not in kept:
                    copy.wait_send()
                    free_send.append(s)
            bag[:] = [pair for pair in bag if id(pair[0]) in kept]

        settle(copies)

        @pl.when(inner == 1)
        def _():
            settle(inner_copies)

        @pl.when(inner == 0)
        def _():
            settle(outer_copies)

    def arrive(*group):
        for copy in group:
            copy.wait_recv()

    def cuts(extent):
        part = extent // PIECES
        return [pl.ds(p * part, part) for p in range(PIECES)]

    def pieces(source, target, step, extent, bag=copies):
        s = free_send.pop(0)
        rs = [free_recv.pop(0) for _ in range(PIECES)]
        bag.append((wire(source, target, step, s, rs[0]), s))
        return [
            wire(source.at[cut], target.at[cut], step, s, r) for cut, r in zip(cuts(extent), rs)
        ]

    def parcel(source, target, step, extent, bag=copies):
        s, r = free_send.pop(0), free_recv.pop(0)
        whole = wire(source, target, step, s, r)
        bag.append((whole, s))
        parts = [wire(source.at[cut], target.at[cut], step, s, r) for cut in cuts(extent)]
        return parts, whole

    def grouped(source, target, place, steps):
        s, r = free_send.pop(0), free_recv.pop(0)
        three = target.at[pl.ds(0, 3)]
        whole = wire(three, three, steps[0], s, r)
        copies.append((whole, s))
        return [wire(source(peers[t]), target.at[place], t, s, r) for t in steps], whole

    def place(i):
        design = design_of(pall[i * rows : (i + 1) * rows, :])
        at = slice(i * rows, (i + 1) * rows)
        dtri[at, :] = triple(design)
        turned = jnp.transpose(design)[:REGRESSORS, :].astype(BF16)
        dturn[:, at] = turned
        return turned

    path_core = remote(pb_hbm, slot(1), CORE)
    trade_side, side_all = parcel(w_hbm, wall.at[2], SIDE, trades)
    trade_near = pieces(w_hbm, wall.at[1], NEAR, trades)
    path_mid = pieces(pb_hbm, slot(2), MID, rows, inner_copies)
    path_far = pieces(pb_hbm, slot(4), FAR, rows, outer_copies)
    small_side = remote(small.at[0], small.at[2], SIDE)
    small_near = remote(small.at[0], small.at[1], NEAR)

    lower = bits[0] + bits[1] + bits[2] + bits[3] + inner * high

    @pl.when(lower > 0)
    def _():
        pl.semaphore_wait(barrier, lower)

    for i, step in enumerate((CORE, SIDE, NEAR)):

        @pl.when(bits[i] == 1)
        def _():
            greet(ready.at[i], step)

    @pl.when(inner * high == 1)
    def _():
        greet(ready.at[3], FAR)
        greet(ready.at[5], MID)

    def down(i, *group):
        @pl.when(bits[i] == 1)
        def _():
            start(*group)

    def up(i, *group):
        @pl.when(bits[i] == 0)
        def _():
            pl.semaphore_wait(ready.at[i], 1)
            start(*group)

    split = PIECES // 2
    down(2, *trade_near[:split])

    @pl.when(inner * high == 1)
    def _():
        start(*path_mid)

    down(1, *trade_side[:split])
    down(0, path_core)
    loads[0].wait()
    own_turned = place(0)
    loads[1].wait()
    note = jnp.broadcast_to(not_ref[...].astype(F32), (16, trades)).astype(BF16)
    small[0] = jnp.concatenate([own_turned, note], axis=0)
    down(2, small_near, *trade_near[split:])
    down(1, small_side, *trade_side[split:])
    up(0, path_core)
    up(1, small_side, *trade_side)
    up(2, small_near, *trade_near)

    @pl.when((1 - inner) * high == 1)
    def _():
        start(*path_far)

    @pl.when(inner * (1 - high) == 1)
    def _():
        pl.semaphore_wait(ready.at[5], 1)
        start(*path_mid)

    @pl.when((1 - inner) * (1 - high) == 1)
    def _():
        pl.semaphore_wait(ready.at[3], 1)
        start(*path_far)

    loads[2].wait()
    small_pass = remote(small.at[1], small.at[3], SIDE)
    trade_pass, pass_all = parcel(wall.at[1], wall.at[3], SIDE, trades)
    mid_pass, mid_all = parcel(slot(2), slot(3), CORE, rows, inner_copies)
    far_pass, far_all = parcel(slot(4), slot(5), CORE, rows, inner_copies)
    used = [r for r in range(ARRIVALS) if r not in free_recv]
    front = pl.ds(0, REGRESSORS)
    design_core = remote(small.at[:, front], dall.at[0], CORE)
    design_far = remote(small.at[:, front], dall.at[1], FAR)
    design_pass = remote(dall.at[1], dall.at[2], CORE)

    for load in loads[3:]:
        load.wait()
    labels = jnp.concatenate([set_ref[pl.ds(peers[s], 1), :] for s in trade_steps], axis=1)
    table[...] = set_table(labels, set_total)

    def value(top, bottom, left, right):
        paths = pall[top:bottom, :]
        weights = wall[left:right].reshape((right - left) * trades, feats)
        notional = jnp.concatenate(
            [small[s, REGRESSORS:, :].astype(F32)[:1, :] for s in range(left, right)], axis=1
        )
        pre_act = mm(paths, weights, NT)
        fade = jnp.exp(-jnp.abs(pre_act))
        at = (slice(top, bottom), slice(left * trades, right * trades))
        tval[at] = (notional * (jnp.maximum(pre_act, 0.0) + jnp.log1p(fade))).astype(BF16)
        nsig[at] = pre_act

    def sigmoid(top, bottom):
        notional = jnp.concatenate(
            [small[s, REGRESSORS:, :].astype(F32)[:1, :] for s in range(4)], axis=1
        )
        pre_act = nsig[top:bottom, :]
        fade = jnp.exp(-jnp.abs(pre_act))
        nsig[top:bottom, :] = notional * (jnp.where(pre_act >= 0.0, 1.0, fade) / (1.0 + fade))

    pair, head, tail, last = 2 * rows, 4 * rows, 5 * rows, 6 * rows
    arrive(path_core)
    place(1)

    @pl.when(inner == 1)
    def _():
        for copy, onward in zip(path_mid, mid_pass):
            arrive(copy)
            start(onward)

    for p, (copy, onward) in enumerate(zip(trade_near, trade_pass)):
        if p == split:
            arrive(small_near)
            start(small_pass)
        arrive(copy)
        start(onward)
    arrive(side_all, small_side)
    value(0, pair, 0, 3)

    @pl.when(inner == 1)
    def _():
        place(2)
        arrive(mid_all)
        place(3)
        value(pair, head, 0, 3)
        for copy, onward in zip(path_far, far_pass):
            arrive(copy)
            start(onward)
        greet(ready.at[4], FAR)
        fence()
        place(4)
        value(head, tail, 0, 3)

    arrive(small_pass)
    start(design_core, design_far)
    fence()

    @pl.when(inner == 0)
    def _():
        arrive(pass_all)
        value(0, pair, 3, 4)
        by_trades[...] = mm(dturn[:, :pair], tval[:pair, :])

    @pl.when(inner == 1)
    def _():
        arrive(far_all)
        place(5)
        value(tail, last, 0, 3)
        arrive(pass_all)
        value(0, last, 3, 4)
        by_trades[...] = mm(dturn[...], tval[...])

    by_trade = by_trades[...]
    by_set = mm(jnp.concatenate(split3(by_trade), axis=0), table[...], NT)
    moments = (
        by_set[:REGRESSORS] + by_set[REGRESSORS : 2 * REGRESSORS] + by_set[2 * REGRESSORS :]
    )
    for i in range(4):
        bown[i] = moments[:, i * quarter : (i + 1) * quarter]
    quads = (CORE + SIDE, SIDE, CORE)
    lines = (NEAR + FAR, FAR, NEAR)

    def total(ref, count):
        result = ref[0].astype(F32)
        for i in range(1, count):
            result = result + ref[i].astype(F32)
        return result

    moment_q, moment_all = grouped(lambda peer: bown.at[lax.rem(peer, 4)], bq, q, quads)
    start(*moment_q)
    fence()
    bq[q] = bown[q]

    @pl.when(inner == 1)
    def _():
        arrive(design_far)
        start(design_pass)

    arrive(moment_all)
    bzsend[...] = total(bq, 4)

    @pl.when(inner == 0)
    def _():
        pl.semaphore_wait(ready.at[4], 1)

    moment_z, moment_all = grouped(lambda peer: bzsend, bz, z, lines)
    start(*moment_z)
    fence()
    bz[z] = bzsend[...]
    @pl.when(inner == 0)
    def _():
        arrive(design_far)
        start(design_pass)

    fence()
    arrive(design_core, design_pass)
    for s in range(4):
        dgrid[peers[trade_steps[s]]] = small[s, :REGRESSORS, :]
    for k in range(1, 4):
        for s in range(4):
            dgrid[peers[trade_steps[s] + design_steps[k]]] = dall[k - 1, s]
    turned_all = jnp.concatenate([dgrid[i] for i in range(16)], axis=1)
    dstack[...] = jnp.concatenate(
        [turned_all, turned_all, turned_all, jnp.zeros_like(turned_all)], axis=0
    )
    gram = mm(turned_all, turned_all, NT)
    gram = jnp.concatenate([gram, jnp.zeros((REGRESSORS, LANES - REGRESSORS), F32)], axis=1)
    gram_row = lax.broadcasted_iota(jnp.int32, (REGRESSORS, LANES), 0)
    gram_lane = lax.broadcasted_iota(jnp.int32, (REGRESSORS, LANES), 1)
    ridge = jnp.where(gram_row == gram_lane, RIDGE_SCALE * paths_all, 0.0)
    invert[...] = pair_inverse(gram + ridge)
    fence()
    sigmoid(0, pair)

    @pl.when(inner == 1)
    def _():
        sigmoid(pair, last)

    all_levels = tidx_ref[...]
    all_thresholds = jnp.zeros((4, quarter), F32)
    levels = tidx_ref[pl.ds(q, 1), :]
    thresholds = jnp.zeros((1, quarter), F32)
    for i in range(level_ref.shape[0]):
        thresholds = jnp.where(levels == i, level_ref[i], thresholds)
        all_thresholds = jnp.where(all_levels == i, level_ref[i], all_thresholds)
    thresholds = jnp.transpose(jnp.broadcast_to(thresholds, (quarter, quarter)))[:, :1]
    rate = jnp.transpose(
        jnp.broadcast_to(rate_ref[pl.ds(q, 1), :], (quarter, quarter))
    )[:, :1]
    all_rates = rate_ref[...]
    full_thresholds = jnp.concatenate([all_thresholds[i : i + 1] for i in range(4)], axis=1)
    full_rates = jnp.concatenate([all_rates[i : i + 1] for i in range(4)], axis=1)

    arrive(moment_all)
    inverse = invert[:, :REGRESSORS]
    coeffs = precise(inverse, total(bz, 4))
    csend[...] = coeffs
    coeffs_q, coeffs_all_sent = grouped(lambda peer: csend, cq, q, quads)
    cq[q] = coeffs
    excess = mm(stack3(coeffs), dstack[...], TN) - thresholds
    over_ref[...] = excess
    fade = jnp.exp(-jnp.abs(excess))
    seed = jnp.where(excess >= 0.0, 1.0, fade) / (1.0 + fade)
    seed_cut = mm(dstack[:REGRESSORS, :], jnp.concatenate(split2(seed), axis=0), NT)
    seed_sum = (seed_cut[:, :quarter] + seed_cut[:, quarter:]) * rate_ref[pl.ds(q, 1), :]
    solved = precise(inverse, seed_sum)
    ssend[...] = solved
    answer_q, answer_all = grouped(lambda peer: ssend, sq, q, quads)
    start(*answer_q)
    start(*coeffs_q)
    fence()
    sq[q] = solved

    excess = over_ref[...]
    loss = jnp.maximum(excess, 0.0) + jnp.log1p(jnp.exp(-jnp.abs(excess)))
    loss_part = jnp.sum(rate * jnp.sum(loss, axis=1, keepdims=True), axis=0, keepdims=True)
    lsend[...] = jnp.broadcast_to(loss_part, lsend.shape)
    lq[q] = lsend[...]
    loss_q, loss_all = grouped(lambda peer: lsend, lq, q, quads)
    start(*loss_q)
    fence()

    drain(answer_all, coeffs_all_sent, loss_all)
    arrive(answer_all)
    solved_all = jnp.concatenate([sq[i] for i in range(4)], axis=1)
    picked = mm(jnp.concatenate(split3(solved_all), axis=0), table[...])
    solved3 = jnp.concatenate(
        [picked.astype(BF16), jnp.zeros((LANES - 3 * REGRESSORS, picked.shape[1]), BF16)], axis=0
    )

    def slope(top, bottom, left, right):
        at = (slice(top, bottom), slice(left * trades, right * trades))
        spread = mm(dtri[top:bottom, :], solved3[:, at[1]]).astype(BF16).astype(F32)
        slopes[at] = (nsig[at] * spread).astype(BF16)

    scale = 1.0 / math.sqrt(paths_all)

    def basis_part(first, final):
        return mm(slopes[first * rows : final * rows, :], wall[...].reshape(4 * trades, feats))

    def weight_part(left, right, depth):
        cut = slopes[:depth, left * trades : right * trades]
        return mm(cut, pall[:depth, :], TN) * scale

    free_recv.extend(used)
    basis_via = [remote(psend.at[i], pvia.at[i], CORE, inner_copies) for i in range(2)]
    basis_core = remote(psend.at[2], pq.at[0], CORE)
    basis_far = remote(pjoin.at[0], pq.at[1], FAR, inner_copies)
    basis_mid = remote(pjoin.at[1], pq.at[1], MID, inner_copies)
    pull_via = [remote(esend.at[i], evia.at[i], CORE, inner_copies) for i in range(2)]
    pull_core = remote(esend.at[2], eq.at[0], CORE)
    pull_far = remote(ejoin.at[0], eq.at[1], FAR, inner_copies)
    pull_mid = remote(ejoin.at[1], eq.at[1], MID, inner_copies)
    weight_via = pieces(wsend.at[0], wvia, SIDE, trades)
    weight_side = remote(wsend.at[1], wz.at[0], SIDE)

    def give(i, slot, depth, *group):
        wsend[i] = weight_part(slot, slot + 1, depth).astype(BF16)
        start(*group)
        fence()

    def join(i, onward):
        arrive(basis_via[i])
        pjoin[i] = (pown[i] + pvia[i].astype(F32)).astype(BF16)
        start(onward)
        fence()

    def pull(depth):
        pulled = mm(solved3, tval[:depth, :], NT)
        pulls[:, :depth] = (
            pulled[:REGRESSORS]
            + pulled[REGRESSORS : 2 * REGRESSORS]
            + pulled[2 * REGRESSORS : 3 * REGRESSORS]
        )

    @pl.when(inner == 1)
    def _():
        slope(head, last, 0, 4)
        part = basis_part(4, 6)
        psend[0] = part[rows:].astype(BF16)
        start(basis_via[0])
        fence()
        pown[0] = part[:rows]
        slope(0, head, 3, 4)
        give(0, 3, last, *weight_via)
        slope(0, head, 0, 3)
        psend[1] = basis_part(3, 4).astype(BF16)
        start(basis_via[1])
        fence()
        join(0, basis_far)
        give(1, 2, last, weight_side)
        pull(last)
        esend[0] = pulls[:, tail:]
        esend[1] = pulls[:, 3 * rows : head]
        esend[2] = pulls[:, rows:pair]
        start(*pull_via, pull_core)
        fence()
        part = basis_part(1, 3)
        pown[1] = part[rows:]
        psend[2] = part[:rows].astype(BF16)
        start(basis_core)
        fence()
        arrive(*pull_via)
        ejoin[0] = pulls[:, head:tail] + evia[0]
        ejoin[1] = pulls[:, pair : 3 * rows] + evia[1]
        start(pull_far, pull_mid)
        fence()
        join(1, basis_mid)
        wnear[...] = weight_part(1, 2, last)

    @pl.when(inner == 0)
    def _():
        slope(0, pair, 3, 4)
        give(0, 3, pair, *weight_via)
        slope(0, pair, 0, 3)
        give(1, 2, pair, weight_side)
        psend[2] = basis_part(1, 2).astype(BF16)
        start(basis_core)
        fence()
        wnear[...] = weight_part(1, 2, pair)
        pull(pair)
        esend[2] = pulls[:, rows:pair]
        start(pull_core)
        fence()

    weight_near = pieces(wjoin, wz.at[1], NEAR, trades)
    near_all = copies[-1][0]
    for p, (copy, onward) in enumerate(zip(weight_via, weight_near)):
        cut = slice(p * trades // PIECES, (p + 1) * trades // PIECES)
        arrive(copy)
        wjoin[cut, :] = (wnear[cut, :] + wvia[cut, :].astype(F32)).astype(BF16)
        start(onward)

    fence()

    @pl.when(inner == 1)
    def _():
        wadj_ref[...] = weight_part(0, 1, last)

    @pl.when(inner == 0)
    def _():
        wadj_ref[...] = weight_part(0, 1, pair)

    basis_ref[...] = basis_part(0, 1)

    arrive(coeffs_all_sent)
    own_triple = dtri[:rows, :]
    coeffs_all = jnp.concatenate([cq[i] for i in range(4)], axis=1)
    fitted = mm(own_triple, stack3(coeffs_all))
    over = fitted - full_thresholds
    fall = jnp.exp(-jnp.abs(over))
    own_seed = full_rates * (jnp.where(over >= 0.0, 1.0, fall) / (1.0 + fall))
    residual = own_seed - mm(own_triple, stack3(solved_all))
    term = precise(coeffs_all, residual, NT) - precise(solved_all, fitted, NT)
    term = term + pulls[:, :rows]
    arrive(loss_all)
    answers = jnp.concatenate([lq[i] for i in range(4)], axis=1)
    loss_sum = jnp.sum(answers[:1], axis=1, keepdims=True) / quarter
    loss_ref[...] = jnp.broadcast_to(loss_sum / (paths_all * set_total), loss_ref.shape)
    arrive(basis_core)
    basis_ref[...] = basis_ref[...] + pq[0].astype(F32)
    arrive(weight_side)
    wadj_ref[...] = wadj_ref[...] + wz[0].astype(F32)

    @pl.when(inner == 1)
    def _():
        arrive(basis_mid)

    @pl.when(inner == 0)
    def _():
        arrive(basis_far)

    basis_ref[...] = basis_ref[...] + pq[1].astype(F32)
    drain(near_all, basis_mid, pull_far, pull_mid)
    arrive(pull_core)

    @pl.when(inner == 1)
    def _():
        arrive(pull_mid)

    @pl.when(inner == 0)
    def _():
        arrive(pull_far)

    term = term + eq[0] + eq[1]
    padded = jnp.concatenate([term, jnp.zeros((LANES - REGRESSORS, rows), F32)], axis=0)
    turned = pltpu.roll(jnp.transpose(padded), LANES - 1, 1)
    lane = lax.broadcasted_iota(jnp.int32, turned.shape, 1)
    turned = jnp.where(lane < REGRESSORS - 1, turned, 0.0)
    basis_ref[:, :LANES] = basis_ref[:, :LANES] + turned
    for p, copy in enumerate(weight_near):
        cut = slice(p * trades // PIECES, (p + 1) * trades // PIECES)
        arrive(copy)
        wadj_ref[cut, :] = wadj_ref[cut, :] + wz[1, cut, :].astype(F32)
    drain()


def square_scratch(rows, trades, feats, set_total):
    size, quarter = REGRESSORS, set_total // 4
    return [
        pltpu.VMEM((6 * rows, feats), BF16),
        pltpu.VMEM((4, trades, feats), BF16),
        pltpu.VMEM((4, size + 16, trades), BF16),
        pltpu.VMEM((3, 4, size, rows), BF16),
        pltpu.VMEM((16, size, rows), BF16),
        pltpu.VMEM((LANES, 16 * rows), BF16),
        pltpu.VMEM((6 * rows, LANES), BF16),
        pltpu.VMEM((size, 6 * rows), BF16),
        pltpu.VMEM((set_total, 4 * trades), BF16),
        pltpu.VMEM((size, LANES), F32),
        pltpu.VMEM((4, size, quarter), F32),
        pltpu.VMEM((4, size, quarter), F32),
        pltpu.VMEM((size, quarter), F32),
        pltpu.VMEM((4, size, quarter), F32),
        pltpu.VMEM((size, quarter), F32),
        pltpu.VMEM((4, size, quarter), F32),
        pltpu.VMEM((size, quarter), F32),
        pltpu.VMEM((4, size, quarter), F32),
        pltpu.VMEM((8, quarter), F32),
        pltpu.VMEM((4, 8, quarter), F32),
        pltpu.VMEM((quarter, 16 * rows), F32),
        pltpu.VMEM((size, 4 * trades), F32),
        pltpu.VMEM((6 * rows, 4 * trades), BF16),
        pltpu.VMEM((6 * rows, 4 * trades), F32),
        pltpu.VMEM((6 * rows, 4 * trades), BF16),
        pltpu.VMEM((size, 6 * rows), F32),
        pltpu.VMEM((2, trades, feats), BF16),
        pltpu.VMEM((trades, feats), BF16),
        pltpu.VMEM((trades, feats), F32),
        pltpu.VMEM((trades, feats), BF16),
        pltpu.VMEM((2, trades, feats), BF16),
        pltpu.VMEM((3, rows, feats), BF16),
        pltpu.VMEM((2, rows, feats), BF16),
        pltpu.VMEM((2, rows, feats), F32),
        pltpu.VMEM((2, rows, feats), BF16),
        pltpu.VMEM((2, rows, feats), BF16),
        pltpu.VMEM((3, size, rows), F32),
        pltpu.VMEM((2, size, rows), F32),
        pltpu.VMEM((2, size, rows), F32),
        pltpu.VMEM((2, size, rows), F32),
        pltpu.SemaphoreType.DMA((7,)),
        pltpu.SemaphoreType.DMA((SENDS,)),
        pltpu.SemaphoreType.DMA((ARRIVALS,)),
        pltpu.SemaphoreType.REGULAR((6,)),
        pltpu.SemaphoreType.REGULAR,
    ]


def chain_scratch(inner, outer, rows, trades, feats, set_total):
    size, quarter, count = REGRESSORS, set_total // inner, inner * outer
    z_pairs, q_pairs = max(outer - 1, 1), max(inner - 1, 1)
    return [
        pltpu.VMEM((inner, rows, feats), BF16),
        pltpu.VMEM((outer, trades, feats), BF16),
        pltpu.VMEM((outer, 8, trades), F32),
        pltpu.VMEM((8, trades), F32),
        pltpu.VMEM((size, rows), BF16),
        pltpu.VMEM((outer, size, rows), BF16),
        pltpu.VMEM((inner, outer, size, rows), BF16),
        pltpu.VMEM((LANES, count * rows), BF16),
        pltpu.VMEM((set_total, outer * trades), BF16),
        pltpu.VMEM((size, LANES), F32),
        pltpu.VMEM((inner, size, quarter), F32),
        pltpu.VMEM((inner, size, quarter), F32),
        pltpu.VMEM((size, quarter), F32),
        pltpu.VMEM((outer, size, quarter), F32),
        pltpu.VMEM((size, quarter), F32),
        pltpu.VMEM((inner, size, quarter), F32),
        pltpu.VMEM((size + 8, quarter), F32),
        pltpu.VMEM((inner, size + 8, quarter), F32),
        pltpu.VMEM((inner, size, rows), F32),
        pltpu.VMEM((inner, size, rows), F32),
        pltpu.VMEM((outer, trades, feats), BF16),
        pltpu.VMEM((outer, trades, feats), BF16),
        pltpu.VMEM((inner, rows, feats), BF16),
        pltpu.VMEM((inner, rows, feats), BF16),
        pltpu.VMEM((inner * rows, outer * trades), F32),
        pltpu.VMEM((inner * rows, outer * trades), BF16),
        pltpu.SemaphoreType.DMA((7,)),
        pltpu.SemaphoreType.DMA((5, z_pairs)),
        pltpu.SemaphoreType.DMA((5, z_pairs)),
        pltpu.SemaphoreType.DMA((7, q_pairs)),
        pltpu.SemaphoreType.DMA((7, q_pairs)),
    ]


def publish(*refs):
    sources, targets, done = refs[:3], refs[3:6], refs[6]
    copies = [
        pltpu.make_async_copy(source, target, done.at[i])
        for i, (source, target) in enumerate(zip(sources, targets))
    ]
    for copy in copies:
        copy.start()
    for copy in copies:
        copy.wait()


def shards(
    path_basis, proxy_weight, notional, set_of, threshold_index, threshold_levels, loss_rate
):
    count = lax.axis_size("paths")
    inner = math.gcd(4, count)
    outer = count // inner
    rows, feats = path_basis.shape
    trades = proxy_weight.shape[0]
    set_total = loss_rate.shape[0]
    quarter = set_total // inner
    vmem = pl.BlockSpec(memory_space=pltpu.VMEM)
    if count == 16 and rows == trades and rows % (16 * PIECES) == 0:
        body = functools.partial(square, rows * count, set_total)
        scratch = square_scratch(rows, trades, feats, set_total)
    else:
        body = functools.partial(kernel, inner, outer, rows * count, set_total)
        scratch = chain_scratch(inner, outer, rows, trades, feats, set_total)
    loss, basis_adjoint, weight_adjoint = pl.pallas_call(
        body,
        out_shape=(
            jax.ShapeDtypeStruct((1, LANES), F32),
            jax.ShapeDtypeStruct((rows, feats), F32),
            jax.ShapeDtypeStruct((trades, feats), F32),
        ),
        in_specs=[pl.BlockSpec(memory_space=pltpu.HBM)] * 7,
        out_specs=(vmem, vmem, vmem),
        scratch_shapes=[
            pltpu.VMEM((1, trades), BF16),
            pltpu.VMEM((inner * outer, trades), jnp.int32),
            pltpu.VMEM((inner, quarter), jnp.int32),
            pltpu.SMEM(threshold_levels.shape, F32),
            pltpu.VMEM((inner, quarter), F32),
            *scratch,
        ],
        compiler_params=pltpu.CompilerParams(
            collective_id=0, has_side_effects=True, vmem_limit_bytes=48 * 1024 * 1024
        ),
    )(
        *(
            pltpu.with_memory_space_constraint(operand, pltpu.HBM)
            for operand in (
                path_basis,
                proxy_weight,
                notional.reshape(1, trades),
                set_of.reshape(-1, trades),
                threshold_index.reshape(inner, quarter),
                threshold_levels,
                loss_rate.reshape(inner, quarter),
            )
        )
    )
    results = (loss, basis_adjoint, weight_adjoint)
    loss, basis_adjoint, weight_adjoint = pl.pallas_call(
        publish,
        out_shape=[jax.ShapeDtypeStruct(result.shape, result.dtype) for result in results],
        in_specs=[pl.BlockSpec(memory_space=pl.ANY)] * 3,
        out_specs=[pl.BlockSpec(memory_space=pl.ANY)] * 3,
        scratch_shapes=[pltpu.SemaphoreType.DMA((3,))],
        compiler_params=pltpu.CompilerParams(vmem_limit_bytes=1024 * 1024),
    )(*results)
    return loss[0, :1], basis_adjoint, weight_adjoint


def solution(mesh):
    placed = (
        P(("groups", "paths"), None),
        P(("groups", "paths"), None),
        P(("groups", "paths")),
        P("groups"),
        P("groups"),
        P("groups"),
        P("groups"),
    )
    return jax.shard_map(
        shards,
        mesh=mesh,
        in_specs=placed,
        out_specs=(P("groups"), P(("groups", "paths"), None), P(("groups", "paths"), None)),
        check_vma=False,
    )
```

```python
import functools
import math

import jax
import jax.numpy as jnp
from jax import lax
from jax.experimental import pallas as pl
from jax.experimental.pallas import tpu as pltpu
from jax.sharding import PartitionSpec as P

REGRESSORS = 32
RIDGE_SCALE = 0.01
PRECISE = lax.Precision.HIGHEST
LANES = 128
PIECES = 4
SENDS = 19
ARRIVALS = 28
F32 = jnp.float32
BF16 = jnp.bfloat16

NN = (((1,), (0,)), ((), ()))
NT = (((1,), (1,)), ((), ()))
TN = (((0,), (0,)), ((), ()))


def mm(a, b, dims=NN):
    return lax.dot_general(a, b, dims, preferred_element_type=F32)


def precise(a, b, dims=NN):
    return lax.dot_general(a, b, dims, precision=PRECISE, preferred_element_type=F32)


def split3(x):
    hi = x.astype(BF16)
    rest = x - hi.astype(F32)
    mid = rest.astype(BF16)
    lo = (rest - mid.astype(F32)).astype(BF16)
    return hi, mid, lo


def stack3(x):
    hi, mid, lo = split3(x)
    return jnp.concatenate([hi, mid, lo, jnp.zeros_like(hi)], axis=0)


def design_of(basis):
    front = pltpu.roll(basis[:, :LANES].astype(F32), 1, 1)
    lane = lax.broadcasted_iota(jnp.int32, front.shape, 1)
    return jnp.where(lane == 0, 1.0, jnp.where(lane < REGRESSORS, front, 0.0))


def triple(design):
    return (
        design + pltpu.roll(design, REGRESSORS, 1) + pltpu.roll(design, 2 * REGRESSORS, 1)
    ).astype(BF16)


def augmented(gram):
    row = lax.broadcasted_iota(jnp.int32, gram.shape, 0)
    lane = lax.broadcasted_iota(jnp.int32, gram.shape, 1)
    return jnp.where(lane < REGRESSORS, gram, jnp.where(lane == row + REGRESSORS, 1.0, 0.0))


def eliminate(work, first, last):
    row = lax.broadcasted_iota(jnp.int32, work.shape, 0)
    for k in range(first, last):
        column = jnp.broadcast_to(work[:, k : k + 1], work.shape)
        pivot = work[k : k + 1, :] / column[k : k + 1, :]
        work = jnp.where(row == k, pivot, work - column * pivot)
    return work


def spd_inverse(gram):
    work = eliminate(augmented(gram), 0, REGRESSORS)
    return pltpu.roll(work, LANES - REGRESSORS, 1)


def set_table(labels, set_total):
    sets = lax.broadcasted_iota(jnp.int32, (set_total, labels.shape[1]), 0)
    return jnp.where(sets == labels, 1.0, 0.0).astype(BF16)


def partner(index, step, count):
    if count & (count - 1):
        return lax.rem(index + step, count)
    result, weight = 0, 1
    while weight < count:
        bit = lax.rem(lax.div(index, weight), 2)
        result = result + weight * (1 - bit if step & weight else bit)
        weight *= 2
    return result


def kernel(
    inner, outer, paths_all, set_total,
    pb_hbm, w_hbm, not_hbm, set_hbm, tidx_hbm, level_hbm, rate_hbm,
    loss_ref, basis_ref, wadj_ref,
    not_ref, set_ref, tidx_ref, level_ref, rate_ref,
    pall, wall, nall, nsend, gown, gall, gq, dstack, table, invert,
    bown, bq, bzsend, bz, csend, cq, ssend, sq,
    eown, eq, wown, wz, pown, pq, nsig, tval,
    local, zsend, zrecv, qsend, qrecv,
):
    rows, feats = basis_ref.shape
    trades = wadj_ref.shape[0]
    quarter = set_total // inner
    me = lax.axis_index("paths")
    q = lax.rem(me, inner)
    z = lax.div(me, inner)

    loads = [
        pltpu.make_async_copy(source, target, local.at[i])
        for i, (source, target) in enumerate(
            [
                (pb_hbm, pall.at[q]),
                (not_hbm, not_ref),
                (w_hbm, wall.at[z]),
                (set_hbm, set_ref),
                (tidx_hbm, tidx_ref),
                (level_hbm, level_ref),
                (rate_hbm, rate_ref),
            ]
        )
    ]
    for load in loads:
        load.start()

    barrier = pltpu.get_barrier_semaphore()
    for d in range(1, inner):
        pl.semaphore_signal(
            barrier, inc=1, device_id={"paths": z * inner + lax.rem(q + d, inner)},
            device_id_type=pl.DeviceIdType.MESH,
        )
    for d in range(1, outer):
        pl.semaphore_signal(
            barrier, inc=1, device_id={"paths": lax.rem(z + d, outer) * inner + q},
            device_id_type=pl.DeviceIdType.MESH,
        )

    pending = []

    def over_q(which, source, target):
        copies = []
        for d in range(inner - 1, 0, -1):
            peer = partner(q, d, inner)
            copy = pltpu.make_async_remote_copy(
                src_ref=source(peer), dst_ref=target.at[q],
                send_sem=qsend.at[which, d - 1], recv_sem=qrecv.at[which, d - 1],
                device_id={"paths": z * inner + peer},
                device_id_type=pl.DeviceIdType.MESH,
            )
            copy.start()
            copies.append(copy)
        pending.extend(copies)
        return copies

    def over_z(which, source, target):
        copies = []
        for d in range(outer - 1, 0, -1):
            peer = partner(z, d, outer)
            copy = pltpu.make_async_remote_copy(
                src_ref=source(peer), dst_ref=target.at[z],
                send_sem=zsend.at[which, d - 1], recv_sem=zrecv.at[which, d - 1],
                device_id={"paths": peer * inner + q},
                device_id_type=pl.DeviceIdType.MESH,
            )
            copy.start()
            copies.append(copy)
        pending.extend(copies)
        return copies

    def arrive(copies):
        for copy in copies:
            copy.wait_recv()

    def total(ref, count):
        result = ref[0].astype(F32)
        for i in range(1, count):
            result = result + ref[i].astype(F32)
        return result

    loads[0].wait()
    own_design = design_of(pall[q])
    own_triple = triple(own_design)
    own_turned = jnp.transpose(own_design)[:REGRESSORS, :].astype(BF16)
    gown[...] = own_turned
    loads[1].wait()
    nrow = jnp.broadcast_to(not_ref[...].astype(F32), (8, trades))
    nsend[...] = nrow
    loads[2].wait()
    pl.semaphore_wait(barrier, inner + outer - 2)

    gram_z = over_z(0, lambda peer: gown, gall)
    note_z = over_z(1, lambda peer: nsend, nall)
    trade_z = over_z(2, lambda peer: wall.at[z], wall)
    path_q = over_q(0, lambda peer: pall.at[q], pall)
    gall[z] = own_turned
    nall[z] = nrow

    arrive(gram_z)
    gram_q = over_q(1, lambda peer: gall, gq)
    gq[q] = gall[...]

    for load in loads[3:]:
        load.wait()
    all_levels = tidx_ref[...]
    all_thresholds = jnp.zeros((inner, quarter), F32)
    levels = tidx_ref[pl.ds(q, 1), :]
    thresholds = jnp.zeros((1, quarter), F32)
    for i in range(level_ref.shape[0]):
        thresholds = jnp.where(levels == i, level_ref[i], thresholds)
        all_thresholds = jnp.where(all_levels == i, level_ref[i], all_thresholds)
    thresholds = jnp.transpose(jnp.broadcast_to(thresholds, (quarter, quarter)))[:, :1]
    rate = jnp.transpose(
        jnp.broadcast_to(rate_ref[pl.ds(q, 1), :], (quarter, quarter))
    )[:, :1]
    all_rates = rate_ref[...]
    labels = jnp.concatenate(
        [set_ref[pl.ds(i * inner + q, 1), :] for i in range(outer)], axis=1
    )
    table[...] = set_table(labels, set_total)

    arrive(path_q)
    paths = pall[...].reshape(inner * rows, feats)
    design = design_of(paths)
    design3 = triple(design)
    design_t = jnp.transpose(design)[:REGRESSORS, :].astype(BF16)

    arrive(gram_q)
    turned_all = jnp.concatenate(
        [gq[i, j] for i in range(inner) for j in range(outer)], axis=1
    )
    dstack[...] = jnp.concatenate(
        [turned_all, turned_all, turned_all, jnp.zeros_like(turned_all)], axis=0
    )
    gram = mm(turned_all, dstack[...], NT)
    gram_row = lax.broadcasted_iota(jnp.int32, (REGRESSORS, LANES), 0)
    gram_lane = lax.broadcasted_iota(jnp.int32, (REGRESSORS, LANES), 1)
    ridge = jnp.where(gram_row == gram_lane, RIDGE_SCALE * paths_all, 0.0)
    invert[...] = spd_inverse(gram + ridge)

    arrive(note_z)
    notional = jnp.concatenate([nall[i][0:1, :] for i in range(outer)], axis=1)
    arrive(trade_z)
    weights = wall[...].reshape(outer * trades, feats)
    pre_act = mm(paths, weights, NT)
    small = jnp.exp(-jnp.abs(pre_act))
    tval[...] = (notional * (jnp.maximum(pre_act, 0.0) + jnp.log1p(small))).astype(BF16)
    nsig[...] = notional * (jnp.where(pre_act >= 0.0, 1.0, small) / (1.0 + small))

    by_trade = mm(design_t, tval[...])
    by_set = mm(jnp.concatenate(split3(by_trade), axis=0), table[...], NT)
    moments = (
        by_set[:REGRESSORS] + by_set[REGRESSORS : 2 * REGRESSORS] + by_set[2 * REGRESSORS :]
    )
    for i in range(inner):
        bown[i] = moments[:, i * quarter : (i + 1) * quarter]
    moment_q = over_q(2, lambda peer: bown.at[peer], bq)
    bq[q] = bown[q]
    arrive(moment_q)
    moment_mid = total(bq, inner)
    bzsend[...] = moment_mid
    moment_z = over_z(3, lambda peer: bzsend, bz)
    bz[z] = moment_mid
    arrive(moment_z)
    inverse = invert[:, :REGRESSORS]
    coeffs = precise(inverse, total(bz, outer))
    csend[...] = coeffs
    coeffs_q = over_q(3, lambda peer: csend, cq)
    cq[q] = coeffs
    excess = mm(stack3(coeffs), dstack[...], TN) - thresholds
    fade = jnp.exp(-jnp.abs(excess))
    loss = jnp.maximum(excess, 0.0) + jnp.log1p(fade)
    seed = rate * (jnp.where(excess >= 0.0, 1.0, fade) / (1.0 + fade))
    seed_cut = mm(dstack[:REGRESSORS, :], jnp.concatenate(split3(seed), axis=0), NT)
    seed_sum = (
        seed_cut[:, :quarter] + seed_cut[:, quarter : 2 * quarter] + seed_cut[:, 2 * quarter :]
    )
    solved = precise(inverse, seed_sum)
    loss_part = jnp.sum(rate * jnp.sum(loss, axis=1, keepdims=True), axis=0, keepdims=True)
    answer = jnp.concatenate([solved, jnp.broadcast_to(loss_part, (8, quarter))], axis=0)
    ssend[...] = answer
    answer_q = over_q(4, lambda peer: ssend, sq)
    sq[q] = answer
    arrive(coeffs_q)
    coeffs_all = jnp.concatenate([cq[i] for i in range(inner)], axis=1)
    arrive(answer_q)
    answers = jnp.concatenate([sq[i] for i in range(inner)], axis=1)
    solved_all = answers[:REGRESSORS]
    loss_sum = jnp.sum(answers[REGRESSORS : REGRESSORS + 1], axis=1, keepdims=True) / quarter
    loss_ref[...] = jnp.broadcast_to(loss_sum / (paths_all * set_total), loss_ref.shape)

    picked = mm(jnp.concatenate(split3(solved_all), axis=0), table[...])
    solved3 = jnp.concatenate(
        [picked.astype(BF16), jnp.zeros((LANES - 3 * REGRESSORS, picked.shape[1]), BF16)], axis=0
    )
    spread = mm(design3, solved3).astype(BF16).astype(F32)
    slopes = (nsig[...] * spread).astype(BF16)
    scale = 1.0 / math.sqrt(paths_all)
    weight_part = mm(slopes, paths, TN) * scale
    wown[...] = weight_part.astype(BF16).reshape(outer, trades, feats)
    weight_z = over_z(4, lambda peer: wown.at[peer], wz)
    wz[z] = wown[z]

    pulled = mm(solved3, tval[...], NT)
    pulled = (
        pulled[:REGRESSORS]
        + pulled[REGRESSORS : 2 * REGRESSORS]
        + pulled[2 * REGRESSORS : 3 * REGRESSORS]
    )
    for i in range(inner):
        eown[i] = pulled[:, i * rows : (i + 1) * rows]
    pull_q = over_q(5, lambda peer: eown.at[peer], eq)
    eq[q] = eown[q]
    basis_part = mm(slopes, weights)
    pown[...] = basis_part.astype(BF16).reshape(inner, rows, feats)
    basis_q = over_q(6, lambda peer: pown.at[peer], pq)
    pq[q] = pown[q]

    fitted = mm(own_triple, stack3(coeffs_all))
    full_thresholds = jnp.concatenate([all_thresholds[i : i + 1] for i in range(inner)], axis=1)
    full_rates = jnp.concatenate([all_rates[i : i + 1] for i in range(inner)], axis=1)
    over = fitted - full_thresholds
    tail = jnp.exp(-jnp.abs(over))
    own_seed = full_rates * (jnp.where(over >= 0.0, 1.0, tail) / (1.0 + tail))
    residual = own_seed - mm(own_triple, stack3(solved_all))
    term = precise(coeffs_all, residual, NT) - precise(solved_all, fitted, NT)
    arrive(pull_q)
    term = term + total(eq, inner)
    padded = jnp.concatenate([term, jnp.zeros((LANES - REGRESSORS, rows), F32)], axis=0)
    turned = pltpu.roll(jnp.transpose(padded), LANES - 1, 1)
    lane = lax.broadcasted_iota(jnp.int32, turned.shape, 1)
    turned = jnp.where(lane < REGRESSORS - 1, turned, 0.0)
    arrive(basis_q)
    basis_ref[...] = total(pq, inner)
    basis_ref[:, :LANES] = basis_ref[:, :LANES] + turned
    arrive(weight_z)
    wadj_ref[...] = total(wz, outer)
    for copy in pending:
        copy.wait_send()


def pair_inverse(gram):
    work = augmented(gram)
    row = lax.broadcasted_iota(jnp.int32, work.shape, 0)
    for k in range(0, REGRESSORS, 2):
        left = jnp.broadcast_to(work[:, k : k + 1], work.shape)
        right = jnp.broadcast_to(work[:, k + 1 : k + 2], work.shape)
        a, c = left[k : k + 1, :], left[k + 1 : k + 2, :]
        b, d = right[k : k + 1, :], right[k + 1 : k + 2, :]
        above, below = work[k : k + 1, :], work[k + 1 : k + 2, :]
        factor = 1.0 / (a * d - b * c)
        upper = (d * above - b * below) * factor
        lower = (a * below - c * above) * factor
        rest = work - left * upper - right * lower
        work = jnp.where(row == k, upper, jnp.where(row == k + 1, lower, rest))
    return pltpu.roll(work, LANES - REGRESSORS, 1)


def split2(x):
    hi = x.astype(BF16)
    return hi, (x - hi.astype(F32)).astype(BF16)


def square(
    paths_all, set_total,
    pb_hbm, w_hbm, not_hbm, set_hbm, tidx_hbm, level_hbm, rate_hbm,
    loss_ref, basis_ref, wadj_ref,
    not_ref, set_ref, tidx_ref, level_ref, rate_ref,
    pall, wall, small, dall, dgrid, dstack, dtri, dturn, table, invert,
    bown, bq, bzsend, bz, csend, cq, ssend, sq, lsend, lq, over_ref,
    by_trades, tval, nsig, slopes, pulls,
    wsend, wvia, wnear, wjoin, wz, psend, pvia, pown, pjoin, pq, esend, evia, ejoin, eq,
    local, send, recv, ready, order,
):
    rows, feats = basis_ref.shape
    trades = wadj_ref.shape[0]
    quarter = set_total // 4
    me = lax.axis_index("paths")
    q, z = lax.rem(me, 4), lax.div(me, 4)
    bits = [lax.rem(lax.div(me, weight), 2) for weight in (1, 2, 4, 8)]
    peers = [me] + [partner(me, step, 16) for step in range(1, 16)]
    low, high = bits[2], bits[3]
    inner = low + high - 2 * low * high
    CORE, SIDE, NEAR, FAR = 1, 2, 4, 8
    MID = NEAR + FAR
    trade_steps = (0, NEAR, SIDE, NEAR + SIDE)
    design_steps = (0, CORE, FAR, CORE + FAR)

    loads = [
        pltpu.make_async_copy(source, target, local.at[i])
        for i, (source, target) in enumerate(
            [
                (pb_hbm, pall.at[pl.ds(0, rows)]),
                (not_hbm, not_ref),
                (w_hbm, wall.at[0]),
                (set_hbm, set_ref),
                (tidx_hbm, tidx_ref),
                (level_hbm, level_ref),
                (rate_hbm, rate_ref),
            ]
        )
    ]
    barrier = pltpu.get_barrier_semaphore()

    def greet(semaphore, step):
        pl.semaphore_signal(
            semaphore, inc=1, device_id={"paths": peers[step]},
            device_id_type=pl.DeviceIdType.MESH,
        )

    for i, step in enumerate((CORE, SIDE, NEAR, FAR)):

        @pl.when(bits[i] == 0)
        def _():
            greet(barrier, step)

    @pl.when(inner * (1 - high) == 1)
    def _():
        greet(barrier, MID)

    for load in loads:
        load.start()

    copies, inner_copies, outer_copies = [], [], []
    free_send, free_recv = list(range(SENDS)), list(range(ARRIVALS))

    def wire(source, target, step, s, r):
        return pltpu.make_async_remote_copy(
            src_ref=source, dst_ref=target, send_sem=send.at[s], recv_sem=recv.at[r],
            device_id={"paths": peers[step]}, device_id_type=pl.DeviceIdType.MESH,
        )

    def remote(source, target, step, bag=copies):
        s, r = free_send.pop(0), free_recv.pop(0)
        copy = wire(source, target, step, s, r)
        bag.append((copy, s))
        return copy

    def slot(i):
        return pall.at[pl.ds(i * rows, rows)]

    def start(*group):
        for copy in group:
            copy.start()

    def fence():
        pl.semaphore_signal(order, inc=1)
        pl.semaphore_wait(order, 1)

    def drain(*keep):
        kept = [id(copy) for copy in keep]

        def settle(bag):
            for copy, s in bag:
                if id(copy) not in kept:
                    copy.wait_send()
                    free_send.append(s)
            bag[:] = [pair for pair in bag if id(pair[0]) in kept]

        settle(copies)

        @pl.when(inner == 1)
        def _():
            settle(inner_copies)

        @pl.when(inner == 0)
        def _():
            settle(outer_copies)

    def arrive(*group):
        for copy in group:
            copy.wait_recv()

    def cuts(extent):
        part = extent // PIECES
        return [pl.ds(p * part, part) for p in range(PIECES)]

    def pieces(source, target, step, extent, bag=copies):
        s = free_send.pop(0)
        rs = [free_recv.pop(0) for _ in range(PIECES)]
        bag.append((wire(source, target, step, s, rs[0]), s))
        return [
            wire(source.at[cut], target.at[cut], step, s, r) for cut, r in zip(cuts(extent), rs)
        ]

    def parcel(source, target, step, extent, bag=copies):
        s, r = free_send.pop(0), free_recv.pop(0)
        whole = wire(source, target, step, s, r)
        bag.append((whole, s))
        parts = [wire(source.at[cut], target.at[cut], step, s, r) for cut in cuts(extent)]
        return parts, whole

    def grouped(source, target, place, steps):
        s, r = free_send.pop(0), free_recv.pop(0)
        three = target.at[pl.ds(0, 3)]
        whole = wire(three, three, steps[0], s, r)
        copies.append((whole, s))
        return [wire(source(peers[t]), target.at[place], t, s, r) for t in steps], whole

    def place(i):
        design = design_of(pall[i * rows : (i + 1) * rows, :])
        at = slice(i * rows, (i + 1) * rows)
        dtri[at, :] = triple(design)
        turned = jnp.transpose(design)[:REGRESSORS, :].astype(BF16)
        dturn[:, at] = turned
        return turned

    path_core = remote(pb_hbm, slot(1), CORE)
    trade_side, side_all = parcel(w_hbm, wall.at[2], SIDE, trades)
    trade_near = pieces(w_hbm, wall.at[1], NEAR, trades)
    path_mid = pieces(pb_hbm, slot(2), MID, rows, inner_copies)
    path_far = pieces(pb_hbm, slot(4), FAR, rows, outer_copies)
    small_side = remote(small.at[0], small.at[2], SIDE)
    small_near = remote(small.at[0], small.at[1], NEAR)

    lower = bits[0] + bits[1] + bits[2] + bits[3] + inner * high

    @pl.when(lower > 0)
    def _():
        pl.semaphore_wait(barrier, lower)

    for i, step in enumerate((CORE, SIDE, NEAR)):

        @pl.when(bits[i] == 1)
        def _():
            greet(ready.at[i], step)

    @pl.when(inner * high == 1)
    def _():
        greet(ready.at[3], FAR)
        greet(ready.at[5], MID)

    def down(i, *group):
        @pl.when(bits[i] == 1)
        def _():
            start(*group)

    def up(i, *group):
        @pl.when(bits[i] == 0)
        def _():
            pl.semaphore_wait(ready.at[i], 1)
            start(*group)

    split = PIECES // 2
    down(2, *trade_near[:split])

    @pl.when(inner * high == 1)
    def _():
        start(*path_mid)

    down(1, *trade_side[:split])
    down(0, path_core)
    loads[0].wait()
    own_turned = place(0)
    loads[1].wait()
    note = jnp.broadcast_to(not_ref[...].astype(F32), (16, trades)).astype(BF16)
    small[0] = jnp.concatenate([own_turned, note], axis=0)
    down(2, small_near, *trade_near[split:])
    down(1, small_side, *trade_side[split:])
    up(0, path_core)
    up(1, small_side, *trade_side)
    up(2, small_near, *trade_near)

    @pl.when((1 - inner) * high == 1)
    def _():
        start(*path_far)

    @pl.when(inner * (1 - high) == 1)
    def _():
        pl.semaphore_wait(ready.at[5], 1)
        start(*path_mid)

    @pl.when((1 - inner) * (1 - high) == 1)
    def _():
        pl.semaphore_wait(ready.at[3], 1)
        start(*path_far)

    loads[2].wait()
    small_pass = remote(small.at[1], small.at[3], SIDE)
    trade_pass, pass_all = parcel(wall.at[1], wall.at[3], SIDE, trades)
    mid_pass, mid_all = parcel(slot(2), slot(3), CORE, rows, inner_copies)
    far_pass, far_all = parcel(slot(4), slot(5), CORE, rows, inner_copies)
    used = [r for r in range(ARRIVALS) if r not in free_recv]
    front = pl.ds(0, REGRESSORS)
    design_core = remote(small.at[:, front], dall.at[0], CORE)
    design_far = remote(small.at[:, front], dall.at[1], FAR)
    design_pass = remote(dall.at[1], dall.at[2], CORE)

    for load in loads[3:]:
        load.wait()
    labels = jnp.concatenate([set_ref[pl.ds(peers[s], 1), :] for s in trade_steps], axis=1)
    table[...] = set_table(labels, set_total)

    def value(top, bottom, left, right):
        paths = pall[top:bottom, :]
        weights = wall[left:right].reshape((right - left) * trades, feats)
        notional = jnp.concatenate(
            [small[s, REGRESSORS:, :].astype(F32)[:1, :] for s in range(left, right)], axis=1
        )
        pre_act = mm(paths, weights, NT)
        fade = jnp.exp(-jnp.abs(pre_act))
        at = (slice(top, bottom), slice(left * trades, right * trades))
        tval[at] = (notional * (jnp.maximum(pre_act, 0.0) + jnp.log1p(fade))).astype(BF16)
        nsig[at] = pre_act

    def sigmoid(top, bottom):
        notional = jnp.concatenate(
            [small[s, REGRESSORS:, :].astype(F32)[:1, :] for s in range(4)], axis=1
        )
        pre_act = nsig[top:bottom, :]
        fade = jnp.exp(-jnp.abs(pre_act))
        nsig[top:bottom, :] = notional * (jnp.where(pre_act >= 0.0, 1.0, fade) / (1.0 + fade))

    pair, head, tail, last = 2 * rows, 4 * rows, 5 * rows, 6 * rows
    arrive(path_core)
    place(1)

    for p, (copy, onward) in enumerate(zip(trade_near, trade_pass)):
        if p == split:
            arrive(small_near)
            start(small_pass)
        arrive(copy)
        start(onward)
    @pl.when(inner == 1)
    def _():
        for copy, onward in zip(path_mid, mid_pass):
            arrive(copy)
            start(onward)

    arrive(side_all, small_side)
    value(0, pair, 0, 3)

    @pl.when(inner == 1)
    def _():
        place(2)
        arrive(mid_all)
        place(3)
        value(pair, head, 0, 3)
        for copy, onward in zip(path_far, far_pass):
            arrive(copy)
            start(onward)
        greet(ready.at[4], FAR)
        fence()
        place(4)
        value(head, tail, 0, 3)

    arrive(small_pass)
    start(design_core, design_far)
    fence()

    @pl.when(inner == 0)
    def _():
        arrive(pass_all)
        value(0, pair, 3, 4)
        by_trades[...] = mm(dturn[:, :pair], tval[:pair, :])

    @pl.when(inner == 1)
    def _():
        arrive(far_all)
        place(5)
        value(tail, last, 0, 3)
        arrive(pass_all)
        value(0, last, 3, 4)
        by_trades[...] = mm(dturn[...], tval[...])

    by_trade = by_trades[...]
    by_set = mm(jnp.concatenate(split3(by_trade), axis=0), table[...], NT)
    moments = (
        by_set[:REGRESSORS] + by_set[REGRESSORS : 2 * REGRESSORS] + by_set[2 * REGRESSORS :]
    )
    for i in range(4):
        bown[i] = moments[:, i * quarter : (i + 1) * quarter]
    quads = (CORE + SIDE, SIDE, CORE)
    lines = (NEAR + FAR, FAR, NEAR)

    def total(ref, count):
        result = ref[0].astype(F32)
        for i in range(1, count):
            result = result + ref[i].astype(F32)
        return result

    moment_q, moment_all = grouped(lambda peer: bown.at[lax.rem(peer, 4)], bq, q, quads)
    start(*moment_q)
    fence()
    bq[q] = bown[q]

    @pl.when(inner == 1)
    def _():
        arrive(design_far)
        start(design_pass)

    arrive(moment_all)
    bzsend[...] = total(bq, 4)

    @pl.when(inner == 0)
    def _():
        pl.semaphore_wait(ready.at[4], 1)

    moment_z, moment_all = grouped(lambda peer: bzsend, bz, z, lines)
    start(*moment_z)
    fence()
    bz[z] = bzsend[...]
    @pl.when(inner == 0)
    def _():
        arrive(design_far)
        start(design_pass)

    fence()
    arrive(design_core, design_pass)
    for s in range(4):
        dgrid[peers[trade_steps[s]]] = small[s, :REGRESSORS, :]
    for k in range(1, 4):
        for s in range(4):
            dgrid[peers[trade_steps[s] + design_steps[k]]] = dall[k - 1, s]
    turned_all = jnp.concatenate([dgrid[i] for i in range(16)], axis=1)
    dstack[...] = jnp.concatenate(
        [turned_all, turned_all, turned_all, jnp.zeros_like(turned_all)], axis=0
    )
    gram = mm(turned_all, turned_all, NT)
    gram = jnp.concatenate([gram, jnp.zeros((REGRESSORS, LANES - REGRESSORS), F32)], axis=1)
    gram_row = lax.broadcasted_iota(jnp.int32, (REGRESSORS, LANES), 0)
    gram_lane = lax.broadcasted_iota(jnp.int32, (REGRESSORS, LANES), 1)
    ridge = jnp.where(gram_row == gram_lane, RIDGE_SCALE * paths_all, 0.0)
    invert[...] = pair_inverse(gram + ridge)
    fence()
    sigmoid(0, pair)

    @pl.when(inner == 1)
    def _():
        sigmoid(pair, last)

    all_levels = tidx_ref[...]
    all_thresholds = jnp.zeros((4, quarter), F32)
    levels = tidx_ref[pl.ds(q, 1), :]
    thresholds = jnp.zeros((1, quarter), F32)
    for i in range(level_ref.shape[0]):
        thresholds = jnp.where(levels == i, level_ref[i], thresholds)
        all_thresholds = jnp.where(all_levels == i, level_ref[i], all_thresholds)
    thresholds = jnp.transpose(jnp.broadcast_to(thresholds, (quarter, quarter)))[:, :1]
    rate = jnp.transpose(
        jnp.broadcast_to(rate_ref[pl.ds(q, 1), :], (quarter, quarter))
    )[:, :1]
    all_rates = rate_ref[...]
    full_thresholds = jnp.concatenate([all_thresholds[i : i + 1] for i in range(4)], axis=1)
    full_rates = jnp.concatenate([all_rates[i : i + 1] for i in range(4)], axis=1)

    arrive(moment_all)
    inverse = invert[:, :REGRESSORS]
    coeffs = precise(inverse, total(bz, 4))
    csend[...] = coeffs
    coeffs_q, coeffs_all_sent = grouped(lambda peer: csend, cq, q, quads)
    cq[q] = coeffs
    excess = mm(stack3(coeffs), dstack[...], TN) - thresholds
    over_ref[...] = excess
    fade = jnp.exp(-jnp.abs(excess))
    seed = jnp.where(excess >= 0.0, 1.0, fade) / (1.0 + fade)
    seed_cut = mm(dstack[:REGRESSORS, :], jnp.concatenate(split2(seed), axis=0), NT)
    seed_sum = (seed_cut[:, :quarter] + seed_cut[:, quarter:]) * rate_ref[pl.ds(q, 1), :]
    solved = precise(inverse, seed_sum)
    ssend[...] = solved
    answer_q, answer_all = grouped(lambda peer: ssend, sq, q, quads)
    start(*answer_q)
    start(*coeffs_q)
    fence()
    sq[q] = solved

    excess = over_ref[...]
    loss = jnp.maximum(excess, 0.0) + jnp.log1p(jnp.exp(-jnp.abs(excess)))
    loss_part = jnp.sum(rate * jnp.sum(loss, axis=1, keepdims=True), axis=0, keepdims=True)
    lsend[...] = jnp.broadcast_to(loss_part, lsend.shape)
    lq[q] = lsend[...]
    loss_q, loss_all = grouped(lambda peer: lsend, lq, q, quads)
    start(*loss_q)
    fence()

    drain(answer_all, coeffs_all_sent, loss_all)
    arrive(answer_all)
    solved_all = jnp.concatenate([sq[i] for i in range(4)], axis=1)
    picked = mm(jnp.concatenate(split3(solved_all), axis=0), table[...])
    solved3 = jnp.concatenate(
        [picked.astype(BF16), jnp.zeros((LANES - 3 * REGRESSORS, picked.shape[1]), BF16)], axis=0
    )

    def slope(top, bottom, left, right):
        at = (slice(top, bottom), slice(left * trades, right * trades))
        spread = mm(dtri[top:bottom, :], solved3[:, at[1]]).astype(BF16).astype(F32)
        slopes[at] = (nsig[at] * spread).astype(BF16)

    scale = 1.0 / math.sqrt(paths_all)

    def basis_part(first, final):
        return mm(slopes[first * rows : final * rows, :], wall[...].reshape(4 * trades, feats))

    def weight_part(left, right, depth):
        cut = slopes[:depth, left * trades : right * trades]
        return mm(cut, pall[:depth, :], TN) * scale

    free_recv.extend(used)
    basis_via = [remote(psend.at[i], pvia.at[i], CORE, inner_copies) for i in range(2)]
    basis_core = remote(psend.at[2], pq.at[0], CORE)
    basis_far = remote(pjoin.at[0], pq.at[1], FAR, inner_copies)
    basis_mid = remote(pjoin.at[1], pq.at[1], MID, inner_copies)
    pull_via = [remote(esend.at[i], evia.at[i], CORE, inner_copies) for i in range(2)]
    pull_core = remote(esend.at[2], eq.at[0], CORE)
    pull_far = remote(ejoin.at[0], eq.at[1], FAR, inner_copies)
    pull_mid = remote(ejoin.at[1], eq.at[1], MID, inner_copies)
    weight_via = pieces(wsend.at[0], wvia, SIDE, trades)
    weight_side = remote(wsend.at[1], wz.at[0], SIDE)

    def give(i, slot, depth, *group):
        wsend[i] = weight_part(slot, slot + 1, depth).astype(BF16)
        start(*group)
        fence()

    def join(i, onward):
        arrive(basis_via[i])
        pjoin[i] = (pown[i] + pvia[i].astype(F32)).astype(BF16)
        start(onward)
        fence()

    def pull(depth):
        pulled = mm(solved3, tval[:depth, :], NT)
        pulls[:, :depth] = (
            pulled[:REGRESSORS]
            + pulled[REGRESSORS : 2 * REGRESSORS]
            + pulled[2 * REGRESSORS : 3 * REGRESSORS]
        )

    @pl.when(inner == 1)
    def _():
        slope(head, last, 0, 4)
        part = basis_part(4, 6)
        psend[0] = part[rows:].astype(BF16)
        start(basis_via[0])
        fence()
        pown[0] = part[:rows]
        slope(0, head, 3, 4)
        give(0, 3, last, *weight_via)
        slope(0, head, 0, 3)
        psend[1] = basis_part(3, 4).astype(BF16)
        start(basis_via[1])
        fence()
        join(0, basis_far)
        give(1, 2, last, weight_side)
        pull(last)
        esend[0] = pulls[:, tail:]
        esend[1] = pulls[:, 3 * rows : head]
        esend[2] = pulls[:, rows:pair]
        start(*pull_via, pull_core)
        fence()
        part = basis_part(1, 3)
        pown[1] = part[rows:]
        psend[2] = part[:rows].astype(BF16)
        start(basis_core)
        fence()
        arrive(*pull_via)
        ejoin[0] = pulls[:, head:tail] + evia[0]
        ejoin[1] = pulls[:, pair : 3 * rows] + evia[1]
        start(pull_far, pull_mid)
        fence()
        join(1, basis_mid)
        wnear[...] = weight_part(1, 2, last)

    @pl.when(inner == 0)
    def _():
        slope(0, pair, 3, 4)
        give(0, 3, pair, *weight_via)
        slope(0, pair, 0, 3)
        give(1, 2, pair, weight_side)
        psend[2] = basis_part(1, 2).astype(BF16)
        start(basis_core)
        fence()
        wnear[...] = weight_part(1, 2, pair)
        pull(pair)
        esend[2] = pulls[:, rows:pair]
        start(pull_core)
        fence()

    weight_near = pieces(wjoin, wz.at[1], NEAR, trades)
    near_all = copies[-1][0]
    for p, (copy, onward) in enumerate(zip(weight_via, weight_near)):
        cut = slice(p * trades // PIECES, (p + 1) * trades // PIECES)
        arrive(copy)
        wjoin[cut, :] = (wnear[cut, :] + wvia[cut, :].astype(F32)).astype(BF16)
        start(onward)

    fence()

    @pl.when(inner == 1)
    def _():
        wadj_ref[...] = weight_part(0, 1, last)

    @pl.when(inner == 0)
    def _():
        wadj_ref[...] = weight_part(0, 1, pair)

    basis_ref[...] = basis_part(0, 1)

    arrive(coeffs_all_sent)
    own_triple = dtri[:rows, :]
    coeffs_all = jnp.concatenate([cq[i] for i in range(4)], axis=1)
    fitted = mm(own_triple, stack3(coeffs_all))
    over = fitted - full_thresholds
    fall = jnp.exp(-jnp.abs(over))
    own_seed = full_rates * (jnp.where(over >= 0.0, 1.0, fall) / (1.0 + fall))
    residual = own_seed - mm(own_triple, stack3(solved_all))
    term = precise(coeffs_all, residual, NT) - precise(solved_all, fitted, NT)
    term = term + pulls[:, :rows]
    arrive(loss_all)
    answers = jnp.concatenate([lq[i] for i in range(4)], axis=1)
    loss_sum = jnp.sum(answers[:1], axis=1, keepdims=True) / quarter
    loss_ref[...] = jnp.broadcast_to(loss_sum / (paths_all * set_total), loss_ref.shape)
    arrive(basis_core)
    basis_ref[...] = basis_ref[...] + pq[0].astype(F32)
    arrive(weight_side)
    wadj_ref[...] = wadj_ref[...] + wz[0].astype(F32)

    @pl.when(inner == 1)
    def _():
        arrive(basis_mid)

    @pl.when(inner == 0)
    def _():
        arrive(basis_far)

    basis_ref[...] = basis_ref[...] + pq[1].astype(F32)
    drain(near_all, basis_mid, pull_far, pull_mid)
    arrive(pull_core)

    @pl.when(inner == 1)
    def _():
        arrive(pull_mid)

    @pl.when(inner == 0)
    def _():
        arrive(pull_far)

    term = term + eq[0] + eq[1]
    padded = jnp.concatenate([term, jnp.zeros((LANES - REGRESSORS, rows), F32)], axis=0)
    turned = pltpu.roll(jnp.transpose(padded), LANES - 1, 1)
    lane = lax.broadcasted_iota(jnp.int32, turned.shape, 1)
    turned = jnp.where(lane < REGRESSORS - 1, turned, 0.0)
    basis_ref[:, :LANES] = basis_ref[:, :LANES] + turned
    for p, copy in enumerate(weight_near):
        cut = slice(p * trades // PIECES, (p + 1) * trades // PIECES)
        arrive(copy)
        wadj_ref[cut, :] = wadj_ref[cut, :] + wz[1, cut, :].astype(F32)
    drain()


def square_scratch(rows, trades, feats, set_total):
    size, quarter = REGRESSORS, set_total // 4
    return [
        pltpu.VMEM((6 * rows, feats), BF16),
        pltpu.VMEM((4, trades, feats), BF16),
        pltpu.VMEM((4, size + 16, trades), BF16),
        pltpu.VMEM((3, 4, size, rows), BF16),
        pltpu.VMEM((16, size, rows), BF16),
        pltpu.VMEM((LANES, 16 * rows), BF16),
        pltpu.VMEM((6 * rows, LANES), BF16),
        pltpu.VMEM((size, 6 * rows), BF16),
        pltpu.VMEM((set_total, 4 * trades), BF16),
        pltpu.VMEM((size, LANES), F32),
        pltpu.VMEM((4, size, quarter), F32),
        pltpu.VMEM((4, size, quarter), F32),
        pltpu.VMEM((size, quarter), F32),
        pltpu.VMEM((4, size, quarter), F32),
        pltpu.VMEM((size, quarter), F32),
        pltpu.VMEM((4, size, quarter), F32),
        pltpu.VMEM((size, quarter), F32),
        pltpu.VMEM((4, size, quarter), F32),
        pltpu.VMEM((8, quarter), F32),
        pltpu.VMEM((4, 8, quarter), F32),
        pltpu.VMEM((quarter, 16 * rows), F32),
        pltpu.VMEM((size, 4 * trades), F32),
        pltpu.VMEM((6 * rows, 4 * trades), BF16),
        pltpu.VMEM((6 * rows, 4 * trades), F32),
        pltpu.VMEM((6 * rows, 4 * trades), BF16),
        pltpu.VMEM((size, 6 * rows), F32),
        pltpu.VMEM((2, trades, feats), BF16),
        pltpu.VMEM((trades, feats), BF16),
        pltpu.VMEM((trades, feats), F32),
        pltpu.VMEM((trades, feats), BF16),
        pltpu.VMEM((2, trades, feats), BF16),
        pltpu.VMEM((3, rows, feats), BF16),
        pltpu.VMEM((2, rows, feats), BF16),
        pltpu.VMEM((2, rows, feats), F32),
        pltpu.VMEM((2, rows, feats), BF16),
        pltpu.VMEM((2, rows, feats), BF16),
        pltpu.VMEM((3, size, rows), F32),
        pltpu.VMEM((2, size, rows), F32),
        pltpu.VMEM((2, size, rows), F32),
        pltpu.VMEM((2, size, rows), F32),
        pltpu.SemaphoreType.DMA((7,)),
        pltpu.SemaphoreType.DMA((SENDS,)),
        pltpu.SemaphoreType.DMA((ARRIVALS,)),
        pltpu.SemaphoreType.REGULAR((6,)),
        pltpu.SemaphoreType.REGULAR,
    ]


def chain_scratch(inner, outer, rows, trades, feats, set_total):
    size, quarter, count = REGRESSORS, set_total // inner, inner * outer
    z_pairs, q_pairs = max(outer - 1, 1), max(inner - 1, 1)
    return [
        pltpu.VMEM((inner, rows, feats), BF16),
        pltpu.VMEM((outer, trades, feats), BF16),
        pltpu.VMEM((outer, 8, trades), F32),
        pltpu.VMEM((8, trades), F32),
        pltpu.VMEM((size, rows), BF16),
        pltpu.VMEM((outer, size, rows), BF16),
        pltpu.VMEM((inner, outer, size, rows), BF16),
        pltpu.VMEM((LANES, count * rows), BF16),
        pltpu.VMEM((set_total, outer * trades), BF16),
        pltpu.VMEM((size, LANES), F32),
        pltpu.VMEM((inner, size, quarter), F32),
        pltpu.VMEM((inner, size, quarter), F32),
        pltpu.VMEM((size, quarter), F32),
        pltpu.VMEM((outer, size, quarter), F32),
        pltpu.VMEM((size, quarter), F32),
        pltpu.VMEM((inner, size, quarter), F32),
        pltpu.VMEM((size + 8, quarter), F32),
        pltpu.VMEM((inner, size + 8, quarter), F32),
        pltpu.VMEM((inner, size, rows), F32),
        pltpu.VMEM((inner, size, rows), F32),
        pltpu.VMEM((outer, trades, feats), BF16),
        pltpu.VMEM((outer, trades, feats), BF16),
        pltpu.VMEM((inner, rows, feats), BF16),
        pltpu.VMEM((inner, rows, feats), BF16),
        pltpu.VMEM((inner * rows, outer * trades), F32),
        pltpu.VMEM((inner * rows, outer * trades), BF16),
        pltpu.SemaphoreType.DMA((7,)),
        pltpu.SemaphoreType.DMA((5, z_pairs)),
        pltpu.SemaphoreType.DMA((5, z_pairs)),
        pltpu.SemaphoreType.DMA((7, q_pairs)),
        pltpu.SemaphoreType.DMA((7, q_pairs)),
    ]


def publish(*refs):
    sources, targets, done = refs[:3], refs[3:6], refs[6]
    copies = [
        pltpu.make_async_copy(source, target, done.at[i])
        for i, (source, target) in enumerate(zip(sources, targets))
    ]
    for copy in copies:
        copy.start()
    for copy in copies:
        copy.wait()


def shards(
    path_basis, proxy_weight, notional, set_of, threshold_index, threshold_levels, loss_rate
):
    count = lax.axis_size("paths")
    inner = math.gcd(4, count)
    outer = count // inner
    rows, feats = path_basis.shape
    trades = proxy_weight.shape[0]
    set_total = loss_rate.shape[0]
    quarter = set_total // inner
    vmem = pl.BlockSpec(memory_space=pltpu.VMEM)
    if count == 16 and rows == trades and rows % (16 * PIECES) == 0:
        body = functools.partial(square, rows * count, set_total)
        scratch = square_scratch(rows, trades, feats, set_total)
    else:
        body = functools.partial(kernel, inner, outer, rows * count, set_total)
        scratch = chain_scratch(inner, outer, rows, trades, feats, set_total)
    loss, basis_adjoint, weight_adjoint = pl.pallas_call(
        body,
        out_shape=(
            jax.ShapeDtypeStruct((1, LANES), F32),
            jax.ShapeDtypeStruct((rows, feats), F32),
            jax.ShapeDtypeStruct((trades, feats), F32),
        ),
        in_specs=[pl.BlockSpec(memory_space=pltpu.HBM)] * 7,
        out_specs=(vmem, vmem, vmem),
        scratch_shapes=[
            pltpu.VMEM((1, trades), BF16),
            pltpu.VMEM((inner * outer, trades), jnp.int32),
            pltpu.VMEM((inner, quarter), jnp.int32),
            pltpu.SMEM(threshold_levels.shape, F32),
            pltpu.VMEM((inner, quarter), F32),
            *scratch,
        ],
        compiler_params=pltpu.CompilerParams(
            collective_id=0, has_side_effects=True, vmem_limit_bytes=48 * 1024 * 1024
        ),
    )(
        *(
            pltpu.with_memory_space_constraint(operand, pltpu.HBM)
            for operand in (
                path_basis,
                proxy_weight,
                notional.reshape(1, trades),
                set_of.reshape(-1, trades),
                threshold_index.reshape(inner, quarter),
                threshold_levels,
                loss_rate.reshape(inner, quarter),
            )
        )
    )
    results = (loss, basis_adjoint, weight_adjoint)
    loss, basis_adjoint, weight_adjoint = pl.pallas_call(
        publish,
        out_shape=[jax.ShapeDtypeStruct(result.shape, result.dtype) for result in results],
        in_specs=[pl.BlockSpec(memory_space=pl.ANY)] * 3,
        out_specs=[pl.BlockSpec(memory_space=pl.ANY)] * 3,
        scratch_shapes=[pltpu.SemaphoreType.DMA((3,))],
        compiler_params=pltpu.CompilerParams(vmem_limit_bytes=1024 * 1024),
    )(*results)
    return loss[0, :1], basis_adjoint, weight_adjoint


def solution(mesh):
    placed = (
        P(("groups", "paths"), None),
        P(("groups", "paths"), None),
        P(("groups", "paths")),
        P("groups"),
        P("groups"),
        P("groups"),
        P("groups"),
    )
    return jax.shard_map(
        shards,
        mesh=mesh,
        in_specs=placed,
        out_specs=(P("groups"), P(("groups", "paths"), None), P(("groups", "paths"), None)),
        check_vma=False,
    )
```

```python
import functools
import math

import jax
import jax.numpy as jnp
from jax import lax
from jax.experimental import pallas as pl
from jax.experimental.pallas import tpu as pltpu
from jax.sharding import PartitionSpec as P

REGRESSORS = 32
RIDGE_SCALE = 0.01
PRECISE = lax.Precision.HIGHEST
LANES = 128
PIECES = 4
SENDS = 19
ARRIVALS = 28
F32 = jnp.float32
BF16 = jnp.bfloat16

NN = (((1,), (0,)), ((), ()))
NT = (((1,), (1,)), ((), ()))
TN = (((0,), (0,)), ((), ()))


def mm(a, b, dims=NN):
    return lax.dot_general(a, b, dims, preferred_element_type=F32)


def precise(a, b, dims=NN):
    return lax.dot_general(a, b, dims, precision=PRECISE, preferred_element_type=F32)


def split3(x):
    hi = x.astype(BF16)
    rest = x - hi.astype(F32)
    mid = rest.astype(BF16)
    lo = (rest - mid.astype(F32)).astype(BF16)
    return hi, mid, lo


def stack3(x):
    hi, mid, lo = split3(x)
    return jnp.concatenate([hi, mid, lo, jnp.zeros_like(hi)], axis=0)


def design_of(basis):
    front = pltpu.roll(basis[:, :LANES].astype(F32), 1, 1)
    lane = lax.broadcasted_iota(jnp.int32, front.shape, 1)
    return jnp.where(lane == 0, 1.0, jnp.where(lane < REGRESSORS, front, 0.0))


def triple(design):
    return (
        design + pltpu.roll(design, REGRESSORS, 1) + pltpu.roll(design, 2 * REGRESSORS, 1)
    ).astype(BF16)


def augmented(gram):
    row = lax.broadcasted_iota(jnp.int32, gram.shape, 0)
    lane = lax.broadcasted_iota(jnp.int32, gram.shape, 1)
    return jnp.where(lane < REGRESSORS, gram, jnp.where(lane == row + REGRESSORS, 1.0, 0.0))


def eliminate(work, first, last):
    row = lax.broadcasted_iota(jnp.int32, work.shape, 0)
    for k in range(first, last):
        column = jnp.broadcast_to(work[:, k : k + 1], work.shape)
        pivot = work[k : k + 1, :] / column[k : k + 1, :]
        work = jnp.where(row == k, pivot, work - column * pivot)
    return work


def spd_inverse(gram):
    work = eliminate(augmented(gram), 0, REGRESSORS)
    return pltpu.roll(work, LANES - REGRESSORS, 1)


def set_table(labels, set_total):
    sets = lax.broadcasted_iota(jnp.int32, (set_total, labels.shape[1]), 0)
    return jnp.where(sets == labels, 1.0, 0.0).astype(BF16)


def partner(index, step, count):
    if count & (count - 1):
        return lax.rem(index + step, count)
    result, weight = 0, 1
    while weight < count:
        bit = lax.rem(lax.div(index, weight), 2)
        result = result + weight * (1 - bit if step & weight else bit)
        weight *= 2
    return result


def kernel(
    inner, outer, paths_all, set_total,
    pb_hbm, w_hbm, not_hbm, set_hbm, tidx_hbm, level_hbm, rate_hbm,
    loss_ref, basis_ref, wadj_ref,
    not_ref, set_ref, tidx_ref, level_ref, rate_ref,
    pall, wall, nall, nsend, gown, gall, gq, dstack, table, invert,
    bown, bq, bzsend, bz, csend, cq, ssend, sq,
    eown, eq, wown, wz, pown, pq, nsig, tval,
    local, zsend, zrecv, qsend, qrecv,
):
    rows, feats = basis_ref.shape
    trades = wadj_ref.shape[0]
    quarter = set_total // inner
    me = lax.axis_index("paths")
    q = lax.rem(me, inner)
    z = lax.div(me, inner)

    loads = [
        pltpu.make_async_copy(source, target, local.at[i])
        for i, (source, target) in enumerate(
            [
                (pb_hbm, pall.at[q]),
                (not_hbm, not_ref),
                (w_hbm, wall.at[z]),
                (set_hbm, set_ref),
                (tidx_hbm, tidx_ref),
                (level_hbm, level_ref),
                (rate_hbm, rate_ref),
            ]
        )
    ]
    for load in loads:
        load.start()

    barrier = pltpu.get_barrier_semaphore()
    for d in range(1, inner):
        pl.semaphore_signal(
            barrier, inc=1, device_id={"paths": z * inner + lax.rem(q + d, inner)},
            device_id_type=pl.DeviceIdType.MESH,
        )
    for d in range(1, outer):
        pl.semaphore_signal(
            barrier, inc=1, device_id={"paths": lax.rem(z + d, outer) * inner + q},
            device_id_type=pl.DeviceIdType.MESH,
        )

    pending = []

    def over_q(which, source, target):
        copies = []
        for d in range(inner - 1, 0, -1):
            peer = partner(q, d, inner)
            copy = pltpu.make_async_remote_copy(
                src_ref=source(peer), dst_ref=target.at[q],
                send_sem=qsend.at[which, d - 1], recv_sem=qrecv.at[which, d - 1],
                device_id={"paths": z * inner + peer},
                device_id_type=pl.DeviceIdType.MESH,
            )
            copy.start()
            copies.append(copy)
        pending.extend(copies)
        return copies

    def over_z(which, source, target):
        copies = []
        for d in range(outer - 1, 0, -1):
            peer = partner(z, d, outer)
            copy = pltpu.make_async_remote_copy(
                src_ref=source(peer), dst_ref=target.at[z],
                send_sem=zsend.at[which, d - 1], recv_sem=zrecv.at[which, d - 1],
                device_id={"paths": peer * inner + q},
                device_id_type=pl.DeviceIdType.MESH,
            )
            copy.start()
            copies.append(copy)
        pending.extend(copies)
        return copies

    def arrive(copies):
        for copy in copies:
            copy.wait_recv()

    def total(ref, count):
        result = ref[0].astype(F32)
        for i in range(1, count):
            result = result + ref[i].astype(F32)
        return result

    loads[0].wait()
    own_design = design_of(pall[q])
    own_triple = triple(own_design)
    own_turned = jnp.transpose(own_design)[:REGRESSORS, :].astype(BF16)
    gown[...] = own_turned
    loads[1].wait()
    nrow = jnp.broadcast_to(not_ref[...].astype(F32), (8, trades))
    nsend[...] = nrow
    loads[2].wait()
    pl.semaphore_wait(barrier, inner + outer - 2)

    gram_z = over_z(0, lambda peer: gown, gall)
    note_z = over_z(1, lambda peer: nsend, nall)
    trade_z = over_z(2, lambda peer: wall.at[z], wall)
    path_q = over_q(0, lambda peer: pall.at[q], pall)
    gall[z] = own_turned
    nall[z] = nrow

    arrive(gram_z)
    gram_q = over_q(1, lambda peer: gall, gq)
    gq[q] = gall[...]

    for load in loads[3:]:
        load.wait()
    all_levels = tidx_ref[...]
    all_thresholds = jnp.zeros((inner, quarter), F32)
    levels = tidx_ref[pl.ds(q, 1), :]
    thresholds = jnp.zeros((1, quarter), F32)
    for i in range(level_ref.shape[0]):
        thresholds = jnp.where(levels == i, level_ref[i], thresholds)
        all_thresholds = jnp.where(all_levels == i, level_ref[i], all_thresholds)
    thresholds = jnp.transpose(jnp.broadcast_to(thresholds, (quarter, quarter)))[:, :1]
    rate = jnp.transpose(
        jnp.broadcast_to(rate_ref[pl.ds(q, 1), :], (quarter, quarter))
    )[:, :1]
    all_rates = rate_ref[...]
    labels = jnp.concatenate(
        [set_ref[pl.ds(i * inner + q, 1), :] for i in range(outer)], axis=1
    )
    table[...] = set_table(labels, set_total)

    arrive(path_q)
    paths = pall[...].reshape(inner * rows, feats)
    design = design_of(paths)
    design3 = triple(design)
    design_t = jnp.transpose(design)[:REGRESSORS, :].astype(BF16)

    arrive(gram_q)
    turned_all = jnp.concatenate(
        [gq[i, j] for i in range(inner) for j in range(outer)], axis=1
    )
    dstack[...] = jnp.concatenate(
        [turned_all, turned_all, turned_all, jnp.zeros_like(turned_all)], axis=0
    )
    gram = mm(turned_all, dstack[...], NT)
    gram_row = lax.broadcasted_iota(jnp.int32, (REGRESSORS, LANES), 0)
    gram_lane = lax.broadcasted_iota(jnp.int32, (REGRESSORS, LANES), 1)
    ridge = jnp.where(gram_row == gram_lane, RIDGE_SCALE * paths_all, 0.0)
    invert[...] = spd_inverse(gram + ridge)

    arrive(note_z)
    notional = jnp.concatenate([nall[i][0:1, :] for i in range(outer)], axis=1)
    arrive(trade_z)
    weights = wall[...].reshape(outer * trades, feats)
    pre_act = mm(paths, weights, NT)
    small = jnp.exp(-jnp.abs(pre_act))
    tval[...] = (notional * (jnp.maximum(pre_act, 0.0) + jnp.log1p(small))).astype(BF16)
    nsig[...] = notional * (jnp.where(pre_act >= 0.0, 1.0, small) / (1.0 + small))

    by_trade = mm(design_t, tval[...])
    by_set = mm(jnp.concatenate(split3(by_trade), axis=0), table[...], NT)
    moments = (
        by_set[:REGRESSORS] + by_set[REGRESSORS : 2 * REGRESSORS] + by_set[2 * REGRESSORS :]
    )
    for i in range(inner):
        bown[i] = moments[:, i * quarter : (i + 1) * quarter]
    moment_q = over_q(2, lambda peer: bown.at[peer], bq)
    bq[q] = bown[q]
    arrive(moment_q)
    moment_mid = total(bq, inner)
    bzsend[...] = moment_mid
    moment_z = over_z(3, lambda peer: bzsend, bz)
    bz[z] = moment_mid
    arrive(moment_z)
    inverse = invert[:, :REGRESSORS]
    coeffs = precise(inverse, total(bz, outer))
    csend[...] = coeffs
    coeffs_q = over_q(3, lambda peer: csend, cq)
    cq[q] = coeffs
    excess = mm(stack3(coeffs), dstack[...], TN) - thresholds
    fade = jnp.exp(-jnp.abs(excess))
    loss = jnp.maximum(excess, 0.0) + jnp.log1p(fade)
    seed = rate * (jnp.where(excess >= 0.0, 1.0, fade) / (1.0 + fade))
    seed_cut = mm(dstack[:REGRESSORS, :], jnp.concatenate(split3(seed), axis=0), NT)
    seed_sum = (
        seed_cut[:, :quarter] + seed_cut[:, quarter : 2 * quarter] + seed_cut[:, 2 * quarter :]
    )
    solved = precise(inverse, seed_sum)
    loss_part = jnp.sum(rate * jnp.sum(loss, axis=1, keepdims=True), axis=0, keepdims=True)
    answer = jnp.concatenate([solved, jnp.broadcast_to(loss_part, (8, quarter))], axis=0)
    ssend[...] = answer
    answer_q = over_q(4, lambda peer: ssend, sq)
    sq[q] = answer
    arrive(coeffs_q)
    coeffs_all = jnp.concatenate([cq[i] for i in range(inner)], axis=1)
    arrive(answer_q)
    answers = jnp.concatenate([sq[i] for i in range(inner)], axis=1)
    solved_all = answers[:REGRESSORS]
    loss_sum = jnp.sum(answers[REGRESSORS : REGRESSORS + 1], axis=1, keepdims=True) / quarter
    loss_ref[...] = jnp.broadcast_to(loss_sum / (paths_all * set_total), loss_ref.shape)

    picked = mm(jnp.concatenate(split3(solved_all), axis=0), table[...])
    solved3 = jnp.concatenate(
        [picked.astype(BF16), jnp.zeros((LANES - 3 * REGRESSORS, picked.shape[1]), BF16)], axis=0
    )
    spread = mm(design3, solved3).astype(BF16).astype(F32)
    slopes = (nsig[...] * spread).astype(BF16)
    scale = 1.0 / math.sqrt(paths_all)
    weight_part = mm(slopes, paths, TN) * scale
    wown[...] = weight_part.astype(BF16).reshape(outer, trades, feats)
    weight_z = over_z(4, lambda peer: wown.at[peer], wz)
    wz[z] = wown[z]

    pulled = mm(solved3, tval[...], NT)
    pulled = (
        pulled[:REGRESSORS]
        + pulled[REGRESSORS : 2 * REGRESSORS]
        + pulled[2 * REGRESSORS : 3 * REGRESSORS]
    )
    for i in range(inner):
        eown[i] = pulled[:, i * rows : (i + 1) * rows]
    pull_q = over_q(5, lambda peer: eown.at[peer], eq)
    eq[q] = eown[q]
    basis_part = mm(slopes, weights)
    pown[...] = basis_part.astype(BF16).reshape(inner, rows, feats)
    basis_q = over_q(6, lambda peer: pown.at[peer], pq)
    pq[q] = pown[q]

    fitted = mm(own_triple, stack3(coeffs_all))
    full_thresholds = jnp.concatenate([all_thresholds[i : i + 1] for i in range(inner)], axis=1)
    full_rates = jnp.concatenate([all_rates[i : i + 1] for i in range(inner)], axis=1)
    over = fitted - full_thresholds
    tail = jnp.exp(-jnp.abs(over))
    own_seed = full_rates * (jnp.where(over >= 0.0, 1.0, tail) / (1.0 + tail))
    residual = own_seed - mm(own_triple, stack3(solved_all))
    term = precise(coeffs_all, residual, NT) - precise(solved_all, fitted, NT)
    arrive(pull_q)
    term = term + total(eq, inner)
    padded = jnp.concatenate([term, jnp.zeros((LANES - REGRESSORS, rows), F32)], axis=0)
    turned = pltpu.roll(jnp.transpose(padded), LANES - 1, 1)
    lane = lax.broadcasted_iota(jnp.int32, turned.shape, 1)
    turned = jnp.where(lane < REGRESSORS - 1, turned, 0.0)
    arrive(basis_q)
    basis_ref[...] = total(pq, inner)
    basis_ref[:, :LANES] = basis_ref[:, :LANES] + turned
    arrive(weight_z)
    wadj_ref[...] = total(wz, outer)
    for copy in pending:
        copy.wait_send()


def pair_inverse(gram):
    work = augmented(gram)
    row = lax.broadcasted_iota(jnp.int32, work.shape, 0)
    for k in range(0, REGRESSORS, 2):
        left = jnp.broadcast_to(work[:, k : k + 1], work.shape)
        right = jnp.broadcast_to(work[:, k + 1 : k + 2], work.shape)
        a, c = left[k : k + 1, :], left[k + 1 : k + 2, :]
        b, d = right[k : k + 1, :], right[k + 1 : k + 2, :]
        above, below = work[k : k + 1, :], work[k + 1 : k + 2, :]
        factor = 1.0 / (a * d - b * c)
        upper = (d * above - b * below) * factor
        lower = (a * below - c * above) * factor
        rest = work - left * upper - right * lower
        work = jnp.where(row == k, upper, jnp.where(row == k + 1, lower, rest))
    return pltpu.roll(work, LANES - REGRESSORS, 1)


def split2(x):
    hi = x.astype(BF16)
    return hi, (x - hi.astype(F32)).astype(BF16)


def square(
    paths_all, set_total,
    pb_hbm, w_hbm, not_hbm, set_hbm, tidx_hbm, level_hbm, rate_hbm,
    loss_ref, basis_ref, wadj_ref,
    not_ref, set_ref, tidx_ref, level_ref, rate_ref,
    pall, wall, small, dall, dgrid, dstack, dtri, dturn, table, invert,
    bown, bq, bzsend, bz, csend, cq, ssend, sq, lsend, lq, over_ref,
    partial, tval, nsig, slopes, pulls,
    wsend, wvia, wnear, wjoin, wz, psend, pvia, pown, pjoin, pq, esend, evia, ejoin, eq,
    local, send, recv, ready, order,
):
    rows, feats = basis_ref.shape
    trades = wadj_ref.shape[0]
    quarter = set_total // 4
    me = lax.axis_index("paths")
    q, z = lax.rem(me, 4), lax.div(me, 4)
    bits = [lax.rem(lax.div(me, weight), 2) for weight in (1, 2, 4, 8)]
    peers = [me] + [partner(me, step, 16) for step in range(1, 16)]
    low, high = bits[2], bits[3]
    inner = low + high - 2 * low * high
    CORE, SIDE, NEAR, FAR = 1, 2, 4, 8
    MID = NEAR + FAR
    trade_steps = (0, NEAR, SIDE, NEAR + SIDE)
    design_steps = (0, CORE, FAR, CORE + FAR)

    loads = [
        pltpu.make_async_copy(source, target, local.at[i])
        for i, (source, target) in enumerate(
            [
                (pb_hbm, pall.at[pl.ds(0, rows)]),
                (not_hbm, not_ref),
                (w_hbm, wall.at[0]),
                (set_hbm, set_ref),
                (tidx_hbm, tidx_ref),
                (level_hbm, level_ref),
                (rate_hbm, rate_ref),
            ]
        )
    ]
    barrier = pltpu.get_barrier_semaphore()

    def greet(semaphore, step):
        pl.semaphore_signal(
            semaphore, inc=1, device_id={"paths": peers[step]},
            device_id_type=pl.DeviceIdType.MESH,
        )

    for i, step in enumerate((CORE, SIDE, NEAR, FAR)):

        @pl.when(bits[i] == 0)
        def _():
            greet(barrier, step)

    @pl.when(inner * (1 - high) == 1)
    def _():
        greet(barrier, MID)

    for load in loads:
        load.start()

    copies, inner_copies, outer_copies = [], [], []
    free_send, free_recv = list(range(SENDS)), list(range(ARRIVALS))

    def wire(source, target, step, s, r):
        return pltpu.make_async_remote_copy(
            src_ref=source, dst_ref=target, send_sem=send.at[s], recv_sem=recv.at[r],
            device_id={"paths": peers[step]}, device_id_type=pl.DeviceIdType.MESH,
        )

    def remote(source, target, step, bag=copies):
        s, r = free_send.pop(0), free_recv.pop(0)
        copy = wire(source, target, step, s, r)
        bag.append((copy, s))
        return copy

    def slot(i):
        return pall.at[pl.ds(i * rows, rows)]

    def start(*group):
        for copy in group:
            copy.start()

    def fence():
        pl.semaphore_signal(order, inc=1)
        pl.semaphore_wait(order, 1)

    def drain(*keep):
        kept = [id(copy) for copy in keep]

        def settle(bag):
            for copy, s in bag:
                if id(copy) not in kept:
                    copy.wait_send()
                    free_send.append(s)
            bag[:] = [pair for pair in bag if id(pair[0]) in kept]

        settle(copies)

        @pl.when(inner == 1)
        def _():
            settle(inner_copies)

        @pl.when(inner == 0)
        def _():
            settle(outer_copies)

    def arrive(*group):
        for copy in group:
            copy.wait_recv()

    def cuts(extent):
        part = extent // PIECES
        return [pl.ds(p * part, part) for p in range(PIECES)]

    def pieces(source, target, step, extent, bag=copies):
        s = free_send.pop(0)
        rs = [free_recv.pop(0) for _ in range(PIECES)]
        bag.append((wire(source, target, step, s, rs[0]), s))
        return [
            wire(source.at[cut], target.at[cut], step, s, r) for cut, r in zip(cuts(extent), rs)
        ]

    def parcel(source, target, step, extent, bag=copies):
        s, r = free_send.pop(0), free_recv.pop(0)
        whole = wire(source, target, step, s, r)
        bag.append((whole, s))
        parts = [wire(source.at[cut], target.at[cut], step, s, r) for cut in cuts(extent)]
        return parts, whole

    def grouped(source, target, place, steps):
        s, r = free_send.pop(0), free_recv.pop(0)
        three = target.at[pl.ds(0, 3)]
        whole = wire(three, three, steps[0], s, r)
        copies.append((whole, s))
        return [wire(source(peers[t]), target.at[place], t, s, r) for t in steps], whole

    def place(i):
        design = design_of(pall[i * rows : (i + 1) * rows, :])
        at = slice(i * rows, (i + 1) * rows)
        dtri[at, :] = triple(design)
        turned = jnp.transpose(design)[:REGRESSORS, :].astype(BF16)
        dturn[:, at] = turned
        return turned

    path_core = remote(pb_hbm, slot(1), CORE)
    trade_side, side_all = parcel(w_hbm, wall.at[2], SIDE, trades)
    trade_near = pieces(w_hbm, wall.at[1], NEAR, trades)
    path_mid = pieces(pb_hbm, slot(2), MID, rows, inner_copies)
    path_far = pieces(pb_hbm, slot(4), FAR, rows, outer_copies)
    small_side = remote(small.at[0], small.at[2], SIDE)
    small_near = remote(small.at[0], small.at[1], NEAR)

    lower = bits[0] + bits[1] + bits[2] + bits[3] + inner * high

    @pl.when(lower > 0)
    def _():
        pl.semaphore_wait(barrier, lower)

    for i, step in enumerate((CORE, SIDE, NEAR)):

        @pl.when(bits[i] == 1)
        def _():
            greet(ready.at[i], step)

    @pl.when(inner * high == 1)
    def _():
        greet(ready.at[3], FAR)
        greet(ready.at[5], MID)

    def down(i, *group):
        @pl.when(bits[i] == 1)
        def _():
            start(*group)

    def up(i, *group):
        @pl.when(bits[i] == 0)
        def _():
            pl.semaphore_wait(ready.at[i], 1)
            start(*group)

    split = PIECES // 2
    down(2, *trade_near[:split])

    @pl.when(inner * high == 1)
    def _():
        start(*path_mid)

    down(1, *trade_side[:split])
    down(0, path_core)
    loads[0].wait()
    own_turned = place(0)
    loads[1].wait()
    note = jnp.broadcast_to(not_ref[...].astype(F32), (16, trades)).astype(BF16)
    small[0] = jnp.concatenate([own_turned, note], axis=0)
    down(2, small_near, *trade_near[split:])
    down(1, small_side, *trade_side[split:])
    up(0, path_core)
    up(1, small_side, *trade_side)
    up(2, small_near, *trade_near)

    @pl.when((1 - inner) * high == 1)
    def _():
        start(*path_far)

    @pl.when(inner * (1 - high) == 1)
    def _():
        pl.semaphore_wait(ready.at[5], 1)
        start(*path_mid)

    @pl.when((1 - inner) * (1 - high) == 1)
    def _():
        pl.semaphore_wait(ready.at[3], 1)
        start(*path_far)

    loads[2].wait()
    small_pass = remote(small.at[1], small.at[3], SIDE)
    trade_pass, pass_all = parcel(wall.at[1], wall.at[3], SIDE, trades)
    mid_pass, mid_all = parcel(slot(2), slot(3), CORE, rows, inner_copies)
    far_pass, far_all = parcel(slot(4), slot(5), CORE, rows, inner_copies)
    used = [r for r in range(ARRIVALS) if r not in free_recv]
    front = pl.ds(0, REGRESSORS)
    design_core = remote(small.at[:, front], dall.at[0], CORE)
    design_far = remote(small.at[:, front], dall.at[1], FAR)
    design_pass = remote(dall.at[1], dall.at[2], CORE)

    for load in loads[3:]:
        load.wait()
    labels = jnp.concatenate([set_ref[pl.ds(peers[s], 1), :] for s in trade_steps], axis=1)
    table[...] = set_table(labels, set_total)

    def value(top, bottom, left, right):
        paths = pall[top:bottom, :]
        weights = wall[left:right].reshape((right - left) * trades, feats)
        notional = jnp.concatenate(
            [small[s, REGRESSORS:, :].astype(F32)[:1, :] for s in range(left, right)], axis=1
        )
        pre_act = mm(paths, weights, NT)
        fade = jnp.exp(-jnp.abs(pre_act))
        at = (slice(top, bottom), slice(left * trades, right * trades))
        tval[at] = (notional * (jnp.maximum(pre_act, 0.0) + jnp.log1p(fade))).astype(BF16)
        nsig[at] = pre_act

    def sigmoid(top, bottom):
        notional = jnp.concatenate(
            [small[s, REGRESSORS:, :].astype(F32)[:1, :] for s in range(4)], axis=1
        )
        pre_act = nsig[top:bottom, :]
        fade = jnp.exp(-jnp.abs(pre_act))
        nsig[top:bottom, :] = notional * (jnp.where(pre_act >= 0.0, 1.0, fade) / (1.0 + fade))

    pair, head, tail, last = 2 * rows, 4 * rows, 5 * rows, 6 * rows
    arrive(path_core)
    place(1)

    for p, (copy, onward) in enumerate(zip(trade_near, trade_pass)):
        if p == split:
            arrive(small_near)
            start(small_pass)
        arrive(copy)
        start(onward)
    @pl.when(inner == 1)
    def _():
        for copy, onward in zip(path_mid, mid_pass):
            arrive(copy)
            start(onward)

    arrive(side_all, small_side)
    value(0, pair, 0, 3)

    @pl.when(inner == 1)
    def _():
        place(2)
        arrive(mid_all)
        place(3)
        value(pair, head, 0, 3)
        for copy, onward in zip(path_far, far_pass):
            arrive(copy)
            start(onward)
        greet(ready.at[4], FAR)
        fence()
        place(4)
        value(head, tail, 0, 3)

    arrive(small_pass)
    start(design_core, design_far)
    fence()

    def gather(depth, left, right):
        at = slice(left * trades, right * trades)
        by_trade = mm(dturn[:, :depth], tval[:depth, at])
        by_set = mm(jnp.concatenate(split3(by_trade), axis=0), table[:, at], NT)
        return (
            by_set[:REGRESSORS] + by_set[REGRESSORS : 2 * REGRESSORS] + by_set[2 * REGRESSORS :]
        )

    @pl.when(inner == 0)
    def _():
        partial[...] = gather(pair, 0, 3)
        arrive(pass_all)
        value(0, pair, 3, 4)
        partial[...] = partial[...] + gather(pair, 3, 4)

    @pl.when(inner == 1)
    def _():
        arrive(far_all)
        place(5)
        value(tail, last, 0, 3)
        partial[...] = gather(last, 0, 3)
        arrive(pass_all)
        value(0, last, 3, 4)
        partial[...] = partial[...] + gather(last, 3, 4)

    moments = partial[...]
    for i in range(4):
        bown[i] = moments[:, i * quarter : (i + 1) * quarter]
    quads = (CORE + SIDE, SIDE, CORE)
    lines = (NEAR + FAR, FAR, NEAR)

    def total(ref, count):
        result = ref[0].astype(F32)
        for i in range(1, count):
            result = result + ref[i].astype(F32)
        return result

    moment_q, moment_all = grouped(lambda peer: bown.at[lax.rem(peer, 4)], bq, q, quads)
    start(*moment_q)
    fence()
    bq[q] = bown[q]

    @pl.when(inner == 1)
    def _():
        arrive(design_far)
        start(design_pass)

    arrive(moment_all)
    bzsend[...] = total(bq, 4)

    @pl.when(inner == 0)
    def _():
        pl.semaphore_wait(ready.at[4], 1)

    moment_z, moment_all = grouped(lambda peer: bzsend, bz, z, lines)
    start(*moment_z)
    fence()
    bz[z] = bzsend[...]
    @pl.when(inner == 0)
    def _():
        arrive(design_far)
        start(design_pass)

    fence()
    arrive(design_core, design_pass)
    for s in range(4):
        dgrid[peers[trade_steps[s]]] = small[s, :REGRESSORS, :]
    for k in range(1, 4):
        for s in range(4):
            dgrid[peers[trade_steps[s] + design_steps[k]]] = dall[k - 1, s]
    turned_all = jnp.concatenate([dgrid[i] for i in range(16)], axis=1)
    dstack[...] = jnp.concatenate(
        [turned_all, turned_all, turned_all, jnp.zeros_like(turned_all)], axis=0
    )
    gram = mm(turned_all, turned_all, NT)
    gram = jnp.concatenate([gram, jnp.zeros((REGRESSORS, LANES - REGRESSORS), F32)], axis=1)
    gram_row = lax.broadcasted_iota(jnp.int32, (REGRESSORS, LANES), 0)
    gram_lane = lax.broadcasted_iota(jnp.int32, (REGRESSORS, LANES), 1)
    ridge = jnp.where(gram_row == gram_lane, RIDGE_SCALE * paths_all, 0.0)
    invert[...] = pair_inverse(gram + ridge)
    fence()
    sigmoid(0, pair)

    @pl.when(inner == 1)
    def _():
        sigmoid(pair, last)

    all_levels = tidx_ref[...]
    all_thresholds = jnp.zeros((4, quarter), F32)
    levels = tidx_ref[pl.ds(q, 1), :]
    thresholds = jnp.zeros((1, quarter), F32)
    for i in range(level_ref.shape[0]):
        thresholds = jnp.where(levels == i, level_ref[i], thresholds)
        all_thresholds = jnp.where(all_levels == i, level_ref[i], all_thresholds)
    thresholds = jnp.transpose(jnp.broadcast_to(thresholds, (quarter, quarter)))[:, :1]
    rate = jnp.transpose(
        jnp.broadcast_to(rate_ref[pl.ds(q, 1), :], (quarter, quarter))
    )[:, :1]
    all_rates = rate_ref[...]
    full_thresholds = jnp.concatenate([all_thresholds[i : i + 1] for i in range(4)], axis=1)
    full_rates = jnp.concatenate([all_rates[i : i + 1] for i in range(4)], axis=1)

    arrive(moment_all)
    inverse = invert[:, :REGRESSORS]
    coeffs = precise(inverse, total(bz, 4))
    csend[...] = coeffs
    coeffs_q, coeffs_all_sent = grouped(lambda peer: csend, cq, q, quads)
    cq[q] = coeffs
    excess = mm(stack3(coeffs), dstack[...], TN) - thresholds
    over_ref[...] = excess
    fade = jnp.exp(-jnp.abs(excess))
    seed = jnp.where(excess >= 0.0, 1.0, fade) / (1.0 + fade)
    seed_cut = mm(dstack[:REGRESSORS, :], jnp.concatenate(split2(seed), axis=0), NT)
    seed_sum = (seed_cut[:, :quarter] + seed_cut[:, quarter:]) * rate_ref[pl.ds(q, 1), :]
    solved = precise(inverse, seed_sum)
    ssend[...] = solved
    answer_q, answer_all = grouped(lambda peer: ssend, sq, q, quads)
    start(*answer_q)
    start(*coeffs_q)
    fence()
    sq[q] = solved

    excess = over_ref[...]
    loss = jnp.maximum(excess, 0.0) + jnp.log1p(jnp.exp(-jnp.abs(excess)))
    loss_part = jnp.sum(rate * jnp.sum(loss, axis=1, keepdims=True), axis=0, keepdims=True)
    lsend[...] = jnp.broadcast_to(loss_part, lsend.shape)
    lq[q] = lsend[...]
    loss_q, loss_all = grouped(lambda peer: lsend, lq, q, quads)
    start(*loss_q)
    fence()

    drain(answer_all, coeffs_all_sent, loss_all)
    arrive(answer_all)
    solved_all = jnp.concatenate([sq[i] for i in range(4)], axis=1)
    picked = mm(jnp.concatenate(split3(solved_all), axis=0), table[...])
    solved3 = jnp.concatenate(
        [picked.astype(BF16), jnp.zeros((LANES - 3 * REGRESSORS, picked.shape[1]), BF16)], axis=0
    )

    def slope(top, bottom, left, right):
        at = (slice(top, bottom), slice(left * trades, right * trades))
        spread = mm(dtri[top:bottom, :], solved3[:, at[1]]).astype(BF16).astype(F32)
        slopes[at] = (nsig[at] * spread).astype(BF16)

    scale = 1.0 / math.sqrt(paths_all)

    def basis_part(first, final):
        return mm(slopes[first * rows : final * rows, :], wall[...].reshape(4 * trades, feats))

    def weight_part(left, right, depth):
        cut = slopes[:depth, left * trades : right * trades]
        return mm(cut, pall[:depth, :], TN) * scale

    free_recv.extend(used)
    basis_via = [remote(psend.at[i], pvia.at[i], CORE, inner_copies) for i in range(2)]
    basis_core = remote(psend.at[2], pq.at[0], CORE)
    basis_far = remote(pjoin.at[0], pq.at[1], FAR, inner_copies)
    basis_mid = remote(pjoin.at[1], pq.at[1], MID, inner_copies)
    pull_via = [remote(esend.at[i], evia.at[i], CORE, inner_copies) for i in range(2)]
    pull_core = remote(esend.at[2], eq.at[0], CORE)
    pull_far = remote(ejoin.at[0], eq.at[1], FAR, inner_copies)
    pull_mid = remote(ejoin.at[1], eq.at[1], MID, inner_copies)
    weight_via = pieces(wsend.at[0], wvia, SIDE, trades)
    weight_side = remote(wsend.at[1], wz.at[0], SIDE)

    def give(i, slot, depth, *group):
        wsend[i] = weight_part(slot, slot + 1, depth).astype(BF16)
        start(*group)
        fence()

    def join(i, onward):
        arrive(basis_via[i])
        pjoin[i] = (pown[i] + pvia[i].astype(F32)).astype(BF16)
        start(onward)
        fence()

    def pull(depth):
        pulled = mm(solved3, tval[:depth, :], NT)
        pulls[:, :depth] = (
            pulled[:REGRESSORS]
            + pulled[REGRESSORS : 2 * REGRESSORS]
            + pulled[2 * REGRESSORS : 3 * REGRESSORS]
        )

    @pl.when(inner == 1)
    def _():
        slope(head, last, 0, 4)
        part = basis_part(4, 6)
        psend[0] = part[rows:].astype(BF16)
        start(basis_via[0])
        fence()
        pown[0] = part[:rows]
        slope(0, head, 3, 4)
        give(0, 3, last, *weight_via)
        slope(0, head, 0, 3)
        psend[1] = basis_part(3, 4).astype(BF16)
        start(basis_via[1])
        fence()
        join(0, basis_far)
        give(1, 2, last, weight_side)
        pull(last)
        esend[0] = pulls[:, tail:]
        esend[1] = pulls[:, 3 * rows : head]
        esend[2] = pulls[:, rows:pair]
        start(*pull_via, pull_core)
        fence()
        part = basis_part(1, 3)
        pown[1] = part[rows:]
        psend[2] = part[:rows].astype(BF16)
        start(basis_core)
        fence()
        arrive(*pull_via)
        ejoin[0] = pulls[:, head:tail] + evia[0]
        ejoin[1] = pulls[:, pair : 3 * rows] + evia[1]
        start(pull_far, pull_mid)
        fence()
        join(1, basis_mid)
        wnear[...] = weight_part(1, 2, last)

    @pl.when(inner == 0)
    def _():
        slope(0, pair, 3, 4)
        give(0, 3, pair, *weight_via)
        slope(0, pair, 0, 3)
        give(1, 2, pair, weight_side)
        psend[2] = basis_part(1, 2).astype(BF16)
        start(basis_core)
        fence()
        wnear[...] = weight_part(1, 2, pair)
        pull(pair)
        esend[2] = pulls[:, rows:pair]
        start(pull_core)
        fence()

    weight_near = pieces(wjoin, wz.at[1], NEAR, trades)
    near_all = copies[-1][0]
    for p, (copy, onward) in enumerate(zip(weight_via, weight_near)):
        cut = slice(p * trades // PIECES, (p + 1) * trades // PIECES)
        arrive(copy)
        wjoin[cut, :] = (wnear[cut, :] + wvia[cut, :].astype(F32)).astype(BF16)
        start(onward)

    fence()

    @pl.when(inner == 1)
    def _():
        wadj_ref[...] = weight_part(0, 1, last)

    @pl.when(inner == 0)
    def _():
        wadj_ref[...] = weight_part(0, 1, pair)

    basis_ref[...] = basis_part(0, 1)

    arrive(coeffs_all_sent)
    own_triple = dtri[:rows, :]
    coeffs_all = jnp.concatenate([cq[i] for i in range(4)], axis=1)
    fitted = mm(own_triple, stack3(coeffs_all))
    over = fitted - full_thresholds
    fall = jnp.exp(-jnp.abs(over))
    own_seed = full_rates * (jnp.where(over >= 0.0, 1.0, fall) / (1.0 + fall))
    residual = own_seed - mm(own_triple, stack3(solved_all))
    term = precise(coeffs_all, residual, NT) - precise(solved_all, fitted, NT)
    term = term + pulls[:, :rows]
    arrive(loss_all)
    answers = jnp.concatenate([lq[i] for i in range(4)], axis=1)
    loss_sum = jnp.sum(answers[:1], axis=1, keepdims=True) / quarter
    loss_ref[...] = jnp.broadcast_to(loss_sum / (paths_all * set_total), loss_ref.shape)
    arrive(basis_core)
    basis_ref[...] = basis_ref[...] + pq[0].astype(F32)
    arrive(weight_side)
    wadj_ref[...] = wadj_ref[...] + wz[0].astype(F32)

    @pl.when(inner == 1)
    def _():
        arrive(basis_mid)

    @pl.when(inner == 0)
    def _():
        arrive(basis_far)

    basis_ref[...] = basis_ref[...] + pq[1].astype(F32)
    drain(near_all, basis_mid, pull_far, pull_mid)
    arrive(pull_core)

    @pl.when(inner == 1)
    def _():
        arrive(pull_mid)

    @pl.when(inner == 0)
    def _():
        arrive(pull_far)

    term = term + eq[0] + eq[1]
    padded = jnp.concatenate([term, jnp.zeros((LANES - REGRESSORS, rows), F32)], axis=0)
    turned = pltpu.roll(jnp.transpose(padded), LANES - 1, 1)
    lane = lax.broadcasted_iota(jnp.int32, turned.shape, 1)
    turned = jnp.where(lane < REGRESSORS - 1, turned, 0.0)
    basis_ref[:, :LANES] = basis_ref[:, :LANES] + turned
    for p, copy in enumerate(weight_near):
        cut = slice(p * trades // PIECES, (p + 1) * trades // PIECES)
        arrive(copy)
        wadj_ref[cut, :] = wadj_ref[cut, :] + wz[1, cut, :].astype(F32)
    drain()


def square_scratch(rows, trades, feats, set_total):
    size, quarter = REGRESSORS, set_total // 4
    return [
        pltpu.VMEM((6 * rows, feats), BF16),
        pltpu.VMEM((4, trades, feats), BF16),
        pltpu.VMEM((4, size + 16, trades), BF16),
        pltpu.VMEM((3, 4, size, rows), BF16),
        pltpu.VMEM((16, size, rows), BF16),
        pltpu.VMEM((LANES, 16 * rows), BF16),
        pltpu.VMEM((6 * rows, LANES), BF16),
        pltpu.VMEM((size, 6 * rows), BF16),
        pltpu.VMEM((set_total, 4 * trades), BF16),
        pltpu.VMEM((size, LANES), F32),
        pltpu.VMEM((4, size, quarter), F32),
        pltpu.VMEM((4, size, quarter), F32),
        pltpu.VMEM((size, quarter), F32),
        pltpu.VMEM((4, size, quarter), F32),
        pltpu.VMEM((size, quarter), F32),
        pltpu.VMEM((4, size, quarter), F32),
        pltpu.VMEM((size, quarter), F32),
        pltpu.VMEM((4, size, quarter), F32),
        pltpu.VMEM((8, quarter), F32),
        pltpu.VMEM((4, 8, quarter), F32),
        pltpu.VMEM((quarter, 16 * rows), F32),
        pltpu.VMEM((size, set_total), F32),
        pltpu.VMEM((6 * rows, 4 * trades), BF16),
        pltpu.VMEM((6 * rows, 4 * trades), F32),
        pltpu.VMEM((6 * rows, 4 * trades), BF16),
        pltpu.VMEM((size, 6 * rows), F32),
        pltpu.VMEM((2, trades, feats), BF16),
        pltpu.VMEM((trades, feats), BF16),
        pltpu.VMEM((trades, feats), F32),
        pltpu.VMEM((trades, feats), BF16),
        pltpu.VMEM((2, trades, feats), BF16),
        pltpu.VMEM((3, rows, feats), BF16),
        pltpu.VMEM((2, rows, feats), BF16),
        pltpu.VMEM((2, rows, feats), F32),
        pltpu.VMEM((2, rows, feats), BF16),
        pltpu.VMEM((2, rows, feats), BF16),
        pltpu.VMEM((3, size, rows), F32),
        pltpu.VMEM((2, size, rows), F32),
        pltpu.VMEM((2, size, rows), F32),
        pltpu.VMEM((2, size, rows), F32),
        pltpu.SemaphoreType.DMA((7,)),
        pltpu.SemaphoreType.DMA((SENDS,)),
        pltpu.SemaphoreType.DMA((ARRIVALS,)),
        pltpu.SemaphoreType.REGULAR((6,)),
        pltpu.SemaphoreType.REGULAR,
    ]


def chain_scratch(inner, outer, rows, trades, feats, set_total):
    size, quarter, count = REGRESSORS, set_total // inner, inner * outer
    z_pairs, q_pairs = max(outer - 1, 1), max(inner - 1, 1)
    return [
        pltpu.VMEM((inner, rows, feats), BF16),
        pltpu.VMEM((outer, trades, feats), BF16),
        pltpu.VMEM((outer, 8, trades), F32),
        pltpu.VMEM((8, trades), F32),
        pltpu.VMEM((size, rows), BF16),
        pltpu.VMEM((outer, size, rows), BF16),
        pltpu.VMEM((inner, outer, size, rows), BF16),
        pltpu.VMEM((LANES, count * rows), BF16),
        pltpu.VMEM((set_total, outer * trades), BF16),
        pltpu.VMEM((size, LANES), F32),
        pltpu.VMEM((inner, size, quarter), F32),
        pltpu.VMEM((inner, size, quarter), F32),
        pltpu.VMEM((size, quarter), F32),
        pltpu.VMEM((outer, size, quarter), F32),
        pltpu.VMEM((size, quarter), F32),
        pltpu.VMEM((inner, size, quarter), F32),
        pltpu.VMEM((size + 8, quarter), F32),
        pltpu.VMEM((inner, size + 8, quarter), F32),
        pltpu.VMEM((inner, size, rows), F32),
        pltpu.VMEM((inner, size, rows), F32),
        pltpu.VMEM((outer, trades, feats), BF16),
        pltpu.VMEM((outer, trades, feats), BF16),
        pltpu.VMEM((inner, rows, feats), BF16),
        pltpu.VMEM((inner, rows, feats), BF16),
        pltpu.VMEM((inner * rows, outer * trades), F32),
        pltpu.VMEM((inner * rows, outer * trades), BF16),
        pltpu.SemaphoreType.DMA((7,)),
        pltpu.SemaphoreType.DMA((5, z_pairs)),
        pltpu.SemaphoreType.DMA((5, z_pairs)),
        pltpu.SemaphoreType.DMA((7, q_pairs)),
        pltpu.SemaphoreType.DMA((7, q_pairs)),
    ]


def publish(*refs):
    sources, targets, done = refs[:3], refs[3:6], refs[6]
    copies = [
        pltpu.make_async_copy(source, target, done.at[i])
        for i, (source, target) in enumerate(zip(sources, targets))
    ]
    for copy in copies:
        copy.start()
    for copy in copies:
        copy.wait()


def shards(
    path_basis, proxy_weight, notional, set_of, threshold_index, threshold_levels, loss_rate
):
    count = lax.axis_size("paths")
    inner = math.gcd(4, count)
    outer = count // inner
    rows, feats = path_basis.shape
    trades = proxy_weight.shape[0]
    set_total = loss_rate.shape[0]
    quarter = set_total // inner
    vmem = pl.BlockSpec(memory_space=pltpu.VMEM)
    if count == 16 and rows == trades and rows % (16 * PIECES) == 0:
        body = functools.partial(square, rows * count, set_total)
        scratch = square_scratch(rows, trades, feats, set_total)
    else:
        body = functools.partial(kernel, inner, outer, rows * count, set_total)
        scratch = chain_scratch(inner, outer, rows, trades, feats, set_total)
    loss, basis_adjoint, weight_adjoint = pl.pallas_call(
        body,
        out_shape=(
            jax.ShapeDtypeStruct((1, LANES), F32),
            jax.ShapeDtypeStruct((rows, feats), F32),
            jax.ShapeDtypeStruct((trades, feats), F32),
        ),
        in_specs=[pl.BlockSpec(memory_space=pltpu.HBM)] * 7,
        out_specs=(vmem, vmem, vmem),
        scratch_shapes=[
            pltpu.VMEM((1, trades), BF16),
            pltpu.VMEM((inner * outer, trades), jnp.int32),
            pltpu.VMEM((inner, quarter), jnp.int32),
            pltpu.SMEM(threshold_levels.shape, F32),
            pltpu.VMEM((inner, quarter), F32),
            *scratch,
        ],
        compiler_params=pltpu.CompilerParams(
            collective_id=0, has_side_effects=True, vmem_limit_bytes=48 * 1024 * 1024
        ),
    )(
        *(
            pltpu.with_memory_space_constraint(operand, pltpu.HBM)
            for operand in (
                path_basis,
                proxy_weight,
                notional.reshape(1, trades),
                set_of.reshape(-1, trades),
                threshold_index.reshape(inner, quarter),
                threshold_levels,
                loss_rate.reshape(inner, quarter),
            )
        )
    )
    results = (loss, basis_adjoint, weight_adjoint)
    loss, basis_adjoint, weight_adjoint = pl.pallas_call(
        publish,
        out_shape=[jax.ShapeDtypeStruct(result.shape, result.dtype) for result in results],
        in_specs=[pl.BlockSpec(memory_space=pl.ANY)] * 3,
        out_specs=[pl.BlockSpec(memory_space=pl.ANY)] * 3,
        scratch_shapes=[pltpu.SemaphoreType.DMA((3,))],
        compiler_params=pltpu.CompilerParams(vmem_limit_bytes=1024 * 1024),
    )(*results)
    return loss[0, :1], basis_adjoint, weight_adjoint


def solution(mesh):
    placed = (
        P(("groups", "paths"), None),
        P(("groups", "paths"), None),
        P(("groups", "paths")),
        P("groups"),
        P("groups"),
        P("groups"),
        P("groups"),
    )
    return jax.shard_map(
        shards,
        mesh=mesh,
        in_specs=placed,
        out_specs=(P("groups"), P(("groups", "paths"), None), P(("groups", "paths"), None)),
        check_vma=False,
    )
```

```python
import functools
import math

import jax
import jax.numpy as jnp
from jax import lax
from jax.experimental import pallas as pl
from jax.experimental.pallas import tpu as pltpu
from jax.sharding import PartitionSpec as P

REGRESSORS = 32
RIDGE_SCALE = 0.01
PRECISE = lax.Precision.HIGHEST
LANES = 128
PIECES = 4
SENDS = 19
ARRIVALS = 28
F32 = jnp.float32
BF16 = jnp.bfloat16

NN = (((1,), (0,)), ((), ()))
NT = (((1,), (1,)), ((), ()))
TN = (((0,), (0,)), ((), ()))


def mm(a, b, dims=NN):
    return lax.dot_general(a, b, dims, preferred_element_type=F32)


def precise(a, b, dims=NN):
    return lax.dot_general(a, b, dims, precision=PRECISE, preferred_element_type=F32)


def split3(x):
    hi = x.astype(BF16)
    rest = x - hi.astype(F32)
    mid = rest.astype(BF16)
    lo = (rest - mid.astype(F32)).astype(BF16)
    return hi, mid, lo


def stack3(x):
    hi, mid, lo = split3(x)
    return jnp.concatenate([hi, mid, lo, jnp.zeros_like(hi)], axis=0)


def design_of(basis):
    front = pltpu.roll(basis[:, :LANES].astype(F32), 1, 1)
    lane = lax.broadcasted_iota(jnp.int32, front.shape, 1)
    return jnp.where(lane == 0, 1.0, jnp.where(lane < REGRESSORS, front, 0.0))


def triple(design):
    return (
        design + pltpu.roll(design, REGRESSORS, 1) + pltpu.roll(design, 2 * REGRESSORS, 1)
    ).astype(BF16)


def augmented(gram):
    row = lax.broadcasted_iota(jnp.int32, gram.shape, 0)
    lane = lax.broadcasted_iota(jnp.int32, gram.shape, 1)
    return jnp.where(lane < REGRESSORS, gram, jnp.where(lane == row + REGRESSORS, 1.0, 0.0))


def eliminate(work, first, last):
    row = lax.broadcasted_iota(jnp.int32, work.shape, 0)
    for k in range(first, last):
        column = jnp.broadcast_to(work[:, k : k + 1], work.shape)
        pivot = work[k : k + 1, :] / column[k : k + 1, :]
        work = jnp.where(row == k, pivot, work - column * pivot)
    return work


def spd_inverse(gram):
    work = eliminate(augmented(gram), 0, REGRESSORS)
    return pltpu.roll(work, LANES - REGRESSORS, 1)


def set_table(labels, set_total):
    sets = lax.broadcasted_iota(jnp.int32, (set_total, labels.shape[1]), 0)
    return jnp.where(sets == labels, 1.0, 0.0).astype(BF16)


def partner(index, step, count):
    if count & (count - 1):
        return lax.rem(index + step, count)
    result, weight = 0, 1
    while weight < count:
        bit = lax.rem(lax.div(index, weight), 2)
        result = result + weight * (1 - bit if step & weight else bit)
        weight *= 2
    return result


def kernel(
    inner, outer, paths_all, set_total,
    pb_hbm, w_hbm, not_hbm, set_hbm, tidx_hbm, level_hbm, rate_hbm,
    loss_ref, basis_ref, wadj_ref,
    not_ref, set_ref, tidx_ref, level_ref, rate_ref,
    pall, wall, nall, nsend, gown, gall, gq, dstack, table, invert,
    bown, bq, bzsend, bz, csend, cq, ssend, sq,
    eown, eq, wown, wz, pown, pq, nsig, tval,
    local, zsend, zrecv, qsend, qrecv,
):
    rows, feats = basis_ref.shape
    trades = wadj_ref.shape[0]
    quarter = set_total // inner
    me = lax.axis_index("paths")
    q = lax.rem(me, inner)
    z = lax.div(me, inner)

    loads = [
        pltpu.make_async_copy(source, target, local.at[i])
        for i, (source, target) in enumerate(
            [
                (pb_hbm, pall.at[q]),
                (not_hbm, not_ref),
                (w_hbm, wall.at[z]),
                (set_hbm, set_ref),
                (tidx_hbm, tidx_ref),
                (level_hbm, level_ref),
                (rate_hbm, rate_ref),
            ]
        )
    ]
    for load in loads:
        load.start()

    barrier = pltpu.get_barrier_semaphore()
    for d in range(1, inner):
        pl.semaphore_signal(
            barrier, inc=1, device_id={"paths": z * inner + lax.rem(q + d, inner)},
            device_id_type=pl.DeviceIdType.MESH,
        )
    for d in range(1, outer):
        pl.semaphore_signal(
            barrier, inc=1, device_id={"paths": lax.rem(z + d, outer) * inner + q},
            device_id_type=pl.DeviceIdType.MESH,
        )

    pending = []

    def over_q(which, source, target):
        copies = []
        for d in range(inner - 1, 0, -1):
            peer = partner(q, d, inner)
            copy = pltpu.make_async_remote_copy(
                src_ref=source(peer), dst_ref=target.at[q],
                send_sem=qsend.at[which, d - 1], recv_sem=qrecv.at[which, d - 1],
                device_id={"paths": z * inner + peer},
                device_id_type=pl.DeviceIdType.MESH,
            )
            copy.start()
            copies.append(copy)
        pending.extend(copies)
        return copies

    def over_z(which, source, target):
        copies = []
        for d in range(outer - 1, 0, -1):
            peer = partner(z, d, outer)
            copy = pltpu.make_async_remote_copy(
                src_ref=source(peer), dst_ref=target.at[z],
                send_sem=zsend.at[which, d - 1], recv_sem=zrecv.at[which, d - 1],
                device_id={"paths": peer * inner + q},
                device_id_type=pl.DeviceIdType.MESH,
            )
            copy.start()
            copies.append(copy)
        pending.extend(copies)
        return copies

    def arrive(copies):
        for copy in copies:
            copy.wait_recv()

    def total(ref, count):
        result = ref[0].astype(F32)
        for i in range(1, count):
            result = result + ref[i].astype(F32)
        return result

    loads[0].wait()
    own_design = design_of(pall[q])
    own_triple = triple(own_design)
    own_turned = jnp.transpose(own_design)[:REGRESSORS, :].astype(BF16)
    gown[...] = own_turned
    loads[1].wait()
    nrow = jnp.broadcast_to(not_ref[...].astype(F32), (8, trades))
    nsend[...] = nrow
    loads[2].wait()
    pl.semaphore_wait(barrier, inner + outer - 2)

    gram_z = over_z(0, lambda peer: gown, gall)
    note_z = over_z(1, lambda peer: nsend, nall)
    trade_z = over_z(2, lambda peer: wall.at[z], wall)
    path_q = over_q(0, lambda peer: pall.at[q], pall)
    gall[z] = own_turned
    nall[z] = nrow

    arrive(gram_z)
    gram_q = over_q(1, lambda peer: gall, gq)
    gq[q] = gall[...]

    for load in loads[3:]:
        load.wait()
    all_levels = tidx_ref[...]
    all_thresholds = jnp.zeros((inner, quarter), F32)
    levels = tidx_ref[pl.ds(q, 1), :]
    thresholds = jnp.zeros((1, quarter), F32)
    for i in range(level_ref.shape[0]):
        thresholds = jnp.where(levels == i, level_ref[i], thresholds)
        all_thresholds = jnp.where(all_levels == i, level_ref[i], all_thresholds)
    thresholds = jnp.transpose(jnp.broadcast_to(thresholds, (quarter, quarter)))[:, :1]
    rate = jnp.transpose(
        jnp.broadcast_to(rate_ref[pl.ds(q, 1), :], (quarter, quarter))
    )[:, :1]
    all_rates = rate_ref[...]
    labels = jnp.concatenate(
        [set_ref[pl.ds(i * inner + q, 1), :] for i in range(outer)], axis=1
    )
    table[...] = set_table(labels, set_total)

    arrive(path_q)
    paths = pall[...].reshape(inner * rows, feats)
    design = design_of(paths)
    design3 = triple(design)
    design_t = jnp.transpose(design)[:REGRESSORS, :].astype(BF16)

    arrive(gram_q)
    turned_all = jnp.concatenate(
        [gq[i, j] for i in range(inner) for j in range(outer)], axis=1
    )
    dstack[...] = jnp.concatenate(
        [turned_all, turned_all, turned_all, jnp.zeros_like(turned_all)], axis=0
    )
    gram = mm(turned_all, dstack[...], NT)
    gram_row = lax.broadcasted_iota(jnp.int32, (REGRESSORS, LANES), 0)
    gram_lane = lax.broadcasted_iota(jnp.int32, (REGRESSORS, LANES), 1)
    ridge = jnp.where(gram_row == gram_lane, RIDGE_SCALE * paths_all, 0.0)
    invert[...] = spd_inverse(gram + ridge)

    arrive(note_z)
    notional = jnp.concatenate([nall[i][0:1, :] for i in range(outer)], axis=1)
    arrive(trade_z)
    weights = wall[...].reshape(outer * trades, feats)
    pre_act = mm(paths, weights, NT)
    small = jnp.exp(-jnp.abs(pre_act))
    tval[...] = (notional * (jnp.maximum(pre_act, 0.0) + jnp.log1p(small))).astype(BF16)
    nsig[...] = notional * (jnp.where(pre_act >= 0.0, 1.0, small) / (1.0 + small))

    by_trade = mm(design_t, tval[...])
    by_set = mm(jnp.concatenate(split3(by_trade), axis=0), table[...], NT)
    moments = (
        by_set[:REGRESSORS] + by_set[REGRESSORS : 2 * REGRESSORS] + by_set[2 * REGRESSORS :]
    )
    for i in range(inner):
        bown[i] = moments[:, i * quarter : (i + 1) * quarter]
    moment_q = over_q(2, lambda peer: bown.at[peer], bq)
    bq[q] = bown[q]
    arrive(moment_q)
    moment_mid = total(bq, inner)
    bzsend[...] = moment_mid
    moment_z = over_z(3, lambda peer: bzsend, bz)
    bz[z] = moment_mid
    arrive(moment_z)
    inverse = invert[:, :REGRESSORS]
    coeffs = precise(inverse, total(bz, outer))
    csend[...] = coeffs
    coeffs_q = over_q(3, lambda peer: csend, cq)
    cq[q] = coeffs
    excess = mm(stack3(coeffs), dstack[...], TN) - thresholds
    fade = jnp.exp(-jnp.abs(excess))
    loss = jnp.maximum(excess, 0.0) + jnp.log1p(fade)
    seed = rate * (jnp.where(excess >= 0.0, 1.0, fade) / (1.0 + fade))
    seed_cut = mm(dstack[:REGRESSORS, :], jnp.concatenate(split3(seed), axis=0), NT)
    seed_sum = (
        seed_cut[:, :quarter] + seed_cut[:, quarter : 2 * quarter] + seed_cut[:, 2 * quarter :]
    )
    solved = precise(inverse, seed_sum)
    loss_part = jnp.sum(rate * jnp.sum(loss, axis=1, keepdims=True), axis=0, keepdims=True)
    answer = jnp.concatenate([solved, jnp.broadcast_to(loss_part, (8, quarter))], axis=0)
    ssend[...] = answer
    answer_q = over_q(4, lambda peer: ssend, sq)
    sq[q] = answer
    arrive(coeffs_q)
    coeffs_all = jnp.concatenate([cq[i] for i in range(inner)], axis=1)
    arrive(answer_q)
    answers = jnp.concatenate([sq[i] for i in range(inner)], axis=1)
    solved_all = answers[:REGRESSORS]
    loss_sum = jnp.sum(answers[REGRESSORS : REGRESSORS + 1], axis=1, keepdims=True) / quarter
    loss_ref[...] = jnp.broadcast_to(loss_sum / (paths_all * set_total), loss_ref.shape)

    picked = mm(jnp.concatenate(split3(solved_all), axis=0), table[...])
    solved3 = jnp.concatenate(
        [picked.astype(BF16), jnp.zeros((LANES - 3 * REGRESSORS, picked.shape[1]), BF16)], axis=0
    )
    spread = mm(design3, solved3).astype(BF16).astype(F32)
    slopes = (nsig[...] * spread).astype(BF16)
    scale = 1.0 / math.sqrt(paths_all)
    weight_part = mm(slopes, paths, TN) * scale
    wown[...] = weight_part.astype(BF16).reshape(outer, trades, feats)
    weight_z = over_z(4, lambda peer: wown.at[peer], wz)
    wz[z] = wown[z]

    pulled = mm(solved3, tval[...], NT)
    pulled = (
        pulled[:REGRESSORS]
        + pulled[REGRESSORS : 2 * REGRESSORS]
        + pulled[2 * REGRESSORS : 3 * REGRESSORS]
    )
    for i in range(inner):
        eown[i] = pulled[:, i * rows : (i + 1) * rows]
    pull_q = over_q(5, lambda peer: eown.at[peer], eq)
    eq[q] = eown[q]
    basis_part = mm(slopes, weights)
    pown[...] = basis_part.astype(BF16).reshape(inner, rows, feats)
    basis_q = over_q(6, lambda peer: pown.at[peer], pq)
    pq[q] = pown[q]

    fitted = mm(own_triple, stack3(coeffs_all))
    full_thresholds = jnp.concatenate([all_thresholds[i : i + 1] for i in range(inner)], axis=1)
    full_rates = jnp.concatenate([all_rates[i : i + 1] for i in range(inner)], axis=1)
    over = fitted - full_thresholds
    tail = jnp.exp(-jnp.abs(over))
    own_seed = full_rates * (jnp.where(over >= 0.0, 1.0, tail) / (1.0 + tail))
    residual = own_seed - mm(own_triple, stack3(solved_all))
    term = precise(coeffs_all, residual, NT) - precise(solved_all, fitted, NT)
    arrive(pull_q)
    term = term + total(eq, inner)
    padded = jnp.concatenate([term, jnp.zeros((LANES - REGRESSORS, rows), F32)], axis=0)
    turned = pltpu.roll(jnp.transpose(padded), LANES - 1, 1)
    lane = lax.broadcasted_iota(jnp.int32, turned.shape, 1)
    turned = jnp.where(lane < REGRESSORS - 1, turned, 0.0)
    arrive(basis_q)
    basis_ref[...] = total(pq, inner)
    basis_ref[:, :LANES] = basis_ref[:, :LANES] + turned
    arrive(weight_z)
    wadj_ref[...] = total(wz, outer)
    for copy in pending:
        copy.wait_send()


def pair_inverse(gram):
    work = augmented(gram)
    row = lax.broadcasted_iota(jnp.int32, work.shape, 0)
    for k in range(0, REGRESSORS, 2):
        left = jnp.broadcast_to(work[:, k : k + 1], work.shape)
        right = jnp.broadcast_to(work[:, k + 1 : k + 2], work.shape)
        a, c = left[k : k + 1, :], left[k + 1 : k + 2, :]
        b, d = right[k : k + 1, :], right[k + 1 : k + 2, :]
        above, below = work[k : k + 1, :], work[k + 1 : k + 2, :]
        factor = 1.0 / (a * d - b * c)
        upper = (d * above - b * below) * factor
        lower = (a * below - c * above) * factor
        rest = work - left * upper - right * lower
        work = jnp.where(row == k, upper, jnp.where(row == k + 1, lower, rest))
    return pltpu.roll(work, LANES - REGRESSORS, 1)


def split2(x):
    hi = x.astype(BF16)
    return hi, (x - hi.astype(F32)).astype(BF16)


def square(
    paths_all, set_total,
    pb_hbm, w_hbm, not_hbm, set_hbm, tidx_hbm, level_hbm, rate_hbm,
    loss_ref, basis_ref, wadj_ref,
    not_ref, set_ref, tidx_ref, level_ref, rate_ref,
    pall, wall, small, dall, dgrid, dstack, dtri, dturn, table, invert,
    bown, bq, bzsend, bz, csend, cq, ssend, sq, lsend, lq, over_ref,
    partial, tval, nsig, slopes, pulls,
    wsend, wvia, wnear, wjoin, wz, psend, pvia, pown, pjoin, pq, esend, evia, ejoin, eq,
    local, send, recv, ready, order,
):
    rows, feats = basis_ref.shape
    trades = wadj_ref.shape[0]
    quarter = set_total // 4
    me = lax.axis_index("paths")
    q, z = lax.rem(me, 4), lax.div(me, 4)
    bits = [lax.rem(lax.div(me, weight), 2) for weight in (1, 2, 4, 8)]
    peers = [me] + [partner(me, step, 16) for step in range(1, 16)]
    low, high = bits[2], bits[3]
    inner = low + high - 2 * low * high
    CORE, SIDE, NEAR, FAR = 1, 2, 4, 8
    MID = NEAR + FAR
    trade_steps = (0, NEAR, SIDE, NEAR + SIDE)
    design_steps = (0, CORE, FAR, CORE + FAR)

    loads = [
        pltpu.make_async_copy(source, target, local.at[i])
        for i, (source, target) in enumerate(
            [
                (pb_hbm, pall.at[pl.ds(0, rows)]),
                (not_hbm, not_ref),
                (w_hbm, wall.at[0]),
                (set_hbm, set_ref),
                (tidx_hbm, tidx_ref),
                (level_hbm, level_ref),
                (rate_hbm, rate_ref),
            ]
        )
    ]
    barrier = pltpu.get_barrier_semaphore()

    def greet(semaphore, step):
        pl.semaphore_signal(
            semaphore, inc=1, device_id={"paths": peers[step]},
            device_id_type=pl.DeviceIdType.MESH,
        )

    for i, step in enumerate((CORE, SIDE, NEAR, FAR)):

        @pl.when(bits[i] == 0)
        def _():
            greet(barrier, step)

    @pl.when(inner * (1 - high) == 1)
    def _():
        greet(barrier, MID)

    for load in loads:
        load.start()

    copies, inner_copies, outer_copies = [], [], []
    free_send, free_recv = list(range(SENDS)), list(range(ARRIVALS))

    def wire(source, target, step, s, r):
        return pltpu.make_async_remote_copy(
            src_ref=source, dst_ref=target, send_sem=send.at[s], recv_sem=recv.at[r],
            device_id={"paths": peers[step]}, device_id_type=pl.DeviceIdType.MESH,
        )

    def remote(source, target, step, bag=copies):
        s, r = free_send.pop(0), free_recv.pop(0)
        copy = wire(source, target, step, s, r)
        bag.append((copy, s))
        return copy

    def slot(i):
        return pall.at[pl.ds(i * rows, rows)]

    def start(*group):
        for copy in group:
            copy.start()

    def fence():
        pl.semaphore_signal(order, inc=1)
        pl.semaphore_wait(order, 1)

    def drain(*keep):
        kept = [id(copy) for copy in keep]

        def settle(bag):
            for copy, s in bag:
                if id(copy) not in kept:
                    copy.wait_send()
                    free_send.append(s)
            bag[:] = [pair for pair in bag if id(pair[0]) in kept]

        settle(copies)

        @pl.when(inner == 1)
        def _():
            settle(inner_copies)

        @pl.when(inner == 0)
        def _():
            settle(outer_copies)

    def arrive(*group):
        for copy in group:
            copy.wait_recv()

    def cuts(extent):
        part = extent // PIECES
        return [pl.ds(p * part, part) for p in range(PIECES)]

    def pieces(source, target, step, extent, bag=copies):
        s = free_send.pop(0)
        rs = [free_recv.pop(0) for _ in range(PIECES)]
        bag.append((wire(source, target, step, s, rs[0]), s))
        return [
            wire(source.at[cut], target.at[cut], step, s, r) for cut, r in zip(cuts(extent), rs)
        ]

    def parcel(source, target, step, extent, bag=copies):
        s, r = free_send.pop(0), free_recv.pop(0)
        whole = wire(source, target, step, s, r)
        bag.append((whole, s))
        parts = [wire(source.at[cut], target.at[cut], step, s, r) for cut in cuts(extent)]
        return parts, whole

    def grouped(source, target, place, steps):
        s, r = free_send.pop(0), free_recv.pop(0)
        three = target.at[pl.ds(0, 3)]
        whole = wire(three, three, steps[0], s, r)
        copies.append((whole, s))
        return [wire(source(peers[t]), target.at[place], t, s, r) for t in steps], whole

    def place(i):
        design = design_of(pall[i * rows : (i + 1) * rows, :])
        at = slice(i * rows, (i + 1) * rows)
        dtri[at, :] = triple(design)
        turned = jnp.transpose(design)[:REGRESSORS, :].astype(BF16)
        dturn[:, at] = turned
        return turned

    path_core = remote(pb_hbm, slot(1), CORE)
    trade_side, side_all = parcel(w_hbm, wall.at[2], SIDE, trades)
    trade_near = pieces(w_hbm, wall.at[1], NEAR, trades)
    path_mid = pieces(pb_hbm, slot(2), MID, rows, inner_copies)
    path_far = pieces(pb_hbm, slot(4), FAR, rows, outer_copies)
    small_side = remote(small.at[0], small.at[2], SIDE)
    small_near = remote(small.at[0], small.at[1], NEAR)

    lower = bits[0] + bits[1] + bits[2] + bits[3] + inner * high

    @pl.when(lower > 0)
    def _():
        pl.semaphore_wait(barrier, lower)

    for i, step in enumerate((CORE, SIDE, NEAR)):

        @pl.when(bits[i] == 1)
        def _():
            greet(ready.at[i], step)

    @pl.when(inner * high == 1)
    def _():
        greet(ready.at[3], FAR)
        greet(ready.at[5], MID)

    def down(i, *group):
        @pl.when(bits[i] == 1)
        def _():
            start(*group)

    def up(i, *group):
        @pl.when(bits[i] == 0)
        def _():
            pl.semaphore_wait(ready.at[i], 1)
            start(*group)

    split = PIECES // 2
    down(2, *trade_near[:split])

    @pl.when(inner * high == 1)
    def _():
        start(*path_mid)

    down(1, *trade_side[:split])
    down(0, path_core)
    loads[0].wait()
    own_turned = place(0)
    loads[1].wait()
    note = jnp.broadcast_to(not_ref[...].astype(F32), (16, trades)).astype(BF16)
    small[0] = jnp.concatenate([own_turned, note], axis=0)
    down(2, small_near, *trade_near[split:])
    down(1, small_side, *trade_side[split:])
    up(0, path_core)
    up(1, small_side, *trade_side)
    up(2, small_near, *trade_near)

    @pl.when((1 - inner) * high == 1)
    def _():
        start(*path_far)

    @pl.when(inner * (1 - high) == 1)
    def _():
        pl.semaphore_wait(ready.at[5], 1)
        start(*path_mid)

    @pl.when((1 - inner) * (1 - high) == 1)
    def _():
        pl.semaphore_wait(ready.at[3], 1)
        start(*path_far)

    loads[2].wait()
    small_pass = remote(small.at[1], small.at[3], SIDE)
    trade_pass, pass_all = parcel(wall.at[1], wall.at[3], SIDE, trades)
    mid_pass, mid_all = parcel(slot(2), slot(3), CORE, rows, inner_copies)
    far_pass, far_all = parcel(slot(4), slot(5), CORE, rows, inner_copies)
    used = [r for r in range(ARRIVALS) if r not in free_recv]
    front = pl.ds(0, REGRESSORS)
    design_core = remote(small.at[:, front], dall.at[0], CORE)
    design_far = remote(small.at[:, front], dall.at[1], FAR)
    design_pass = remote(dall.at[1], dall.at[2], CORE)

    for load in loads[3:]:
        load.wait()
    labels = jnp.concatenate([set_ref[pl.ds(peers[s], 1), :] for s in trade_steps], axis=1)
    table[...] = set_table(labels, set_total)

    def value(top, bottom, left, right):
        paths = pall[top:bottom, :]
        weights = wall[left:right].reshape((right - left) * trades, feats)
        notional = jnp.concatenate(
            [small[s, REGRESSORS:, :].astype(F32)[:1, :] for s in range(left, right)], axis=1
        )
        pre_act = mm(paths, weights, NT)
        fade = jnp.exp(-jnp.abs(pre_act))
        at = (slice(top, bottom), slice(left * trades, right * trades))
        tval[at] = (notional * (jnp.maximum(pre_act, 0.0) + jnp.log1p(fade))).astype(BF16)
        nsig[at] = pre_act

    def sigmoid(top, bottom):
        notional = jnp.concatenate(
            [small[s, REGRESSORS:, :].astype(F32)[:1, :] for s in range(4)], axis=1
        )
        pre_act = nsig[top:bottom, :]
        fade = jnp.exp(-jnp.abs(pre_act))
        nsig[top:bottom, :] = notional * (jnp.where(pre_act >= 0.0, 1.0, fade) / (1.0 + fade))

    pair, head, tail, last = 2 * rows, 4 * rows, 5 * rows, 6 * rows
    arrive(path_core)
    place(1)

    for p, (copy, onward) in enumerate(zip(trade_near, trade_pass)):
        if p == split:
            arrive(small_near)
            start(small_pass)
        arrive(copy)
        start(onward)
    @pl.when(inner == 1)
    def _():
        for copy, onward in zip(path_mid, mid_pass):
            arrive(copy)
            start(onward)

    arrive(side_all, small_side)
    value(0, pair, 0, 3)

    @pl.when(inner == 1)
    def _():
        place(2)
        arrive(mid_all)
        place(3)
        value(pair, head, 0, 3)
        for copy, onward in zip(path_far, far_pass):
            arrive(copy)
            start(onward)
        greet(ready.at[4], FAR)
        fence()
        place(4)
        value(head, tail, 0, 3)

    arrive(small_pass)
    start(design_core, design_far)
    fence()

    def gather(depth, left, right):
        at = slice(left * trades, right * trades)
        by_trade = mm(dturn[:, :depth], tval[:depth, at])
        by_set = mm(jnp.concatenate(split3(by_trade), axis=0), table[:, at], NT)
        return (
            by_set[:REGRESSORS] + by_set[REGRESSORS : 2 * REGRESSORS] + by_set[2 * REGRESSORS :]
        )

    @pl.when(inner == 0)
    def _():
        partial[...] = gather(pair, 0, 3)
        arrive(pass_all)
        value(0, pair, 3, 4)
        partial[...] = partial[...] + gather(pair, 3, 4)

    @pl.when(inner == 1)
    def _():
        arrive(far_all)
        place(5)
        value(tail, last, 0, 3)
        partial[...] = gather(last, 0, 3)
        arrive(pass_all)
        value(0, last, 3, 4)
        partial[...] = partial[...] + gather(last, 3, 4)

    moments = partial[...]
    for i in range(4):
        bown[i] = moments[:, i * quarter : (i + 1) * quarter]
    quads = (CORE + SIDE, SIDE, CORE)
    lines = (NEAR + FAR, FAR, NEAR)

    def total(ref, count):
        result = ref[0].astype(F32)
        for i in range(1, count):
            result = result + ref[i].astype(F32)
        return result

    moment_q, moment_all = grouped(lambda peer: bown.at[lax.rem(peer, 4)], bq, q, quads)
    start(*moment_q)
    fence()
    bq[q] = bown[q]

    @pl.when(inner == 1)
    def _():
        arrive(design_far)
        start(design_pass)

    arrive(moment_all)
    bzsend[...] = total(bq, 4)

    @pl.when(inner == 0)
    def _():
        pl.semaphore_wait(ready.at[4], 1)

    moment_z, moment_all = grouped(lambda peer: bzsend, bz, z, lines)
    start(*moment_z)
    fence()
    bz[z] = bzsend[...]
    @pl.when(inner == 0)
    def _():
        arrive(design_far)
        start(design_pass)

    fence()
    arrive(design_core, design_pass)
    for s in range(4):
        dgrid[peers[trade_steps[s]]] = small[s, :REGRESSORS, :]
    for k in range(1, 4):
        for s in range(4):
            dgrid[peers[trade_steps[s] + design_steps[k]]] = dall[k - 1, s]
    turned_all = jnp.concatenate([dgrid[i] for i in range(16)], axis=1)
    dstack[...] = jnp.concatenate(
        [turned_all, turned_all, turned_all, jnp.zeros_like(turned_all)], axis=0
    )
    gram = mm(turned_all, turned_all, NT)
    gram = jnp.concatenate([gram, jnp.zeros((REGRESSORS, LANES - REGRESSORS), F32)], axis=1)
    gram_row = lax.broadcasted_iota(jnp.int32, (REGRESSORS, LANES), 0)
    gram_lane = lax.broadcasted_iota(jnp.int32, (REGRESSORS, LANES), 1)
    ridge = jnp.where(gram_row == gram_lane, RIDGE_SCALE * paths_all, 0.0)
    invert[...] = pair_inverse(gram + ridge)
    fence()
    sigmoid(0, pair)

    @pl.when(inner == 1)
    def _():
        sigmoid(pair, last)

    all_levels = tidx_ref[...]
    all_thresholds = jnp.zeros((4, quarter), F32)
    levels = tidx_ref[pl.ds(q, 1), :]
    thresholds = jnp.zeros((1, quarter), F32)
    for i in range(level_ref.shape[0]):
        thresholds = jnp.where(levels == i, level_ref[i], thresholds)
        all_thresholds = jnp.where(all_levels == i, level_ref[i], all_thresholds)
    thresholds = jnp.transpose(jnp.broadcast_to(thresholds, (quarter, quarter)))[:, :1]
    rate = jnp.transpose(
        jnp.broadcast_to(rate_ref[pl.ds(q, 1), :], (quarter, quarter))
    )[:, :1]
    all_rates = rate_ref[...]
    full_thresholds = jnp.concatenate([all_thresholds[i : i + 1] for i in range(4)], axis=1)
    full_rates = jnp.concatenate([all_rates[i : i + 1] for i in range(4)], axis=1)

    arrive(moment_all)
    inverse = invert[:, :REGRESSORS]
    coeffs = precise(inverse, total(bz, 4))
    csend[...] = coeffs
    coeffs_q, coeffs_all_sent = grouped(lambda peer: csend, cq, q, quads)
    cq[q] = coeffs
    excess = mm(stack3(coeffs), dstack[...], TN) - thresholds
    over_ref[...] = excess
    fade = jnp.exp(-jnp.abs(excess))
    seed = jnp.where(excess >= 0.0, 1.0, fade) / (1.0 + fade)
    seed_cut = mm(dstack[:REGRESSORS, :], jnp.concatenate(split2(seed), axis=0), NT)
    seed_sum = (seed_cut[:, :quarter] + seed_cut[:, quarter:]) * rate_ref[pl.ds(q, 1), :]
    solved = precise(inverse, seed_sum)
    ssend[...] = solved
    answer_q, answer_all = grouped(lambda peer: ssend, sq, q, quads)
    start(*answer_q)
    start(*coeffs_q)
    fence()
    sq[q] = solved

    excess = over_ref[...]
    loss = jnp.maximum(excess, 0.0) + jnp.log1p(jnp.exp(-jnp.abs(excess)))
    loss_part = jnp.sum(rate * jnp.sum(loss, axis=1, keepdims=True), axis=0, keepdims=True)
    lsend[...] = jnp.broadcast_to(loss_part, lsend.shape)
    lq[q] = lsend[...]
    loss_q, loss_all = grouped(lambda peer: lsend, lq, q, quads)
    start(*loss_q)
    fence()

    drain(answer_all, coeffs_all_sent, loss_all)
    arrive(answer_all)
    solved_all = jnp.concatenate([sq[i] for i in range(4)], axis=1)
    picked = mm(jnp.concatenate(split3(solved_all), axis=0), table[...])
    solved3 = jnp.concatenate(
        [picked.astype(BF16), jnp.zeros((LANES - 3 * REGRESSORS, picked.shape[1]), BF16)], axis=0
    )

    def slope(top, bottom, left, right):
        at = (slice(top, bottom), slice(left * trades, right * trades))
        spread = mm(dtri[top:bottom, :], solved3[:, at[1]]).astype(BF16).astype(F32)
        slopes[at] = (nsig[at] * spread).astype(BF16)

    scale = 1.0 / math.sqrt(paths_all)

    def basis_part(first, final):
        return mm(slopes[first * rows : final * rows, :], wall[...].reshape(4 * trades, feats))

    def weight_part(left, right, depth):
        cut = slopes[:depth, left * trades : right * trades]
        return mm(cut, pall[:depth, :], TN) * scale

    free_recv.extend(used)
    basis_via = [remote(psend.at[i], pvia.at[i], CORE, inner_copies) for i in range(2)]
    basis_core = remote(psend.at[2], pq.at[0], CORE)
    basis_far = remote(pjoin.at[0], pq.at[1], FAR, inner_copies)
    basis_mid = remote(pjoin.at[1], pq.at[1], MID, inner_copies)
    pull_via = [remote(esend.at[i], evia.at[i], CORE, inner_copies) for i in range(2)]
    pull_core = remote(esend.at[2], eq.at[0], CORE)
    pull_far = remote(ejoin.at[0], eq.at[1], FAR, inner_copies)
    pull_mid = remote(ejoin.at[1], eq.at[1], MID, inner_copies)
    weight_via = pieces(wsend.at[0], wvia, SIDE, trades)
    weight_side = remote(wsend.at[1], wz.at[0], SIDE)

    def give(i, slot, depth, *group):
        wsend[i] = weight_part(slot, slot + 1, depth).astype(BF16)
        start(*group)
        fence()

    def join(i, onward):
        arrive(basis_via[i])
        pjoin[i] = (pown[i] + pvia[i].astype(F32)).astype(BF16)
        start(onward)
        fence()

    def pull(depth):
        pulled = mm(solved3, tval[:depth, :], NT)
        pulls[:, :depth] = (
            pulled[:REGRESSORS]
            + pulled[REGRESSORS : 2 * REGRESSORS]
            + pulled[2 * REGRESSORS : 3 * REGRESSORS]
        )

    @pl.when(inner == 1)
    def _():
        slope(tail, last, 0, 4)
        psend[0] = basis_part(5, 6).astype(BF16)
        start(basis_via[0])
        fence()
        slope(head, tail, 0, 4)
        pown[0] = basis_part(4, 5)
        slope(0, head, 3, 4)
        give(0, 3, last, *weight_via)
        slope(0, head, 0, 3)
        psend[1] = basis_part(3, 4).astype(BF16)
        start(basis_via[1])
        fence()
        join(0, basis_far)
        give(1, 2, last, weight_side)
        pull(last)
        esend[0] = pulls[:, tail:]
        esend[1] = pulls[:, 3 * rows : head]
        esend[2] = pulls[:, rows:pair]
        start(*pull_via, pull_core)
        fence()
        part = basis_part(1, 3)
        pown[1] = part[rows:]
        psend[2] = part[:rows].astype(BF16)
        start(basis_core)
        fence()
        arrive(*pull_via)
        ejoin[0] = pulls[:, head:tail] + evia[0]
        ejoin[1] = pulls[:, pair : 3 * rows] + evia[1]
        start(pull_far, pull_mid)
        fence()
        join(1, basis_mid)
        wnear[...] = weight_part(1, 2, last)

    @pl.when(inner == 0)
    def _():
        slope(0, pair, 3, 4)
        give(0, 3, pair, *weight_via)
        slope(0, pair, 0, 3)
        give(1, 2, pair, weight_side)
        psend[2] = basis_part(1, 2).astype(BF16)
        start(basis_core)
        fence()
        wnear[...] = weight_part(1, 2, pair)
        pull(pair)
        esend[2] = pulls[:, rows:pair]
        start(pull_core)
        fence()

    weight_near = pieces(wjoin, wz.at[1], NEAR, trades)
    near_all = copies[-1][0]
    for p, (copy, onward) in enumerate(zip(weight_via, weight_near)):
        cut = slice(p * trades // PIECES, (p + 1) * trades // PIECES)
        arrive(copy)
        wjoin[cut, :] = (wnear[cut, :] + wvia[cut, :].astype(F32)).astype(BF16)
        start(onward)

    fence()

    @pl.when(inner == 1)
    def _():
        wadj_ref[...] = weight_part(0, 1, last)

    @pl.when(inner == 0)
    def _():
        wadj_ref[...] = weight_part(0, 1, pair)

    basis_ref[...] = basis_part(0, 1)

    arrive(coeffs_all_sent)
    own_triple = dtri[:rows, :]
    coeffs_all = jnp.concatenate([cq[i] for i in range(4)], axis=1)
    fitted = mm(own_triple, stack3(coeffs_all))
    over = fitted - full_thresholds
    fall = jnp.exp(-jnp.abs(over))
    own_seed = full_rates * (jnp.where(over >= 0.0, 1.0, fall) / (1.0 + fall))
    residual = own_seed - mm(own_triple, stack3(solved_all))
    term = precise(coeffs_all, residual, NT) - precise(solved_all, fitted, NT)
    term = term + pulls[:, :rows]
    arrive(loss_all)
    answers = jnp.concatenate([lq[i] for i in range(4)], axis=1)
    loss_sum = jnp.sum(answers[:1], axis=1, keepdims=True) / quarter
    loss_ref[...] = jnp.broadcast_to(loss_sum / (paths_all * set_total), loss_ref.shape)
    arrive(basis_core)
    basis_ref[...] = basis_ref[...] + pq[0].astype(F32)
    arrive(weight_side)
    wadj_ref[...] = wadj_ref[...] + wz[0].astype(F32)

    @pl.when(inner == 1)
    def _():
        arrive(basis_mid)

    @pl.when(inner == 0)
    def _():
        arrive(basis_far)

    basis_ref[...] = basis_ref[...] + pq[1].astype(F32)
    drain(near_all, basis_mid, pull_far, pull_mid)
    arrive(pull_core)

    @pl.when(inner == 1)
    def _():
        arrive(pull_mid)

    @pl.when(inner == 0)
    def _():
        arrive(pull_far)

    term = term + eq[0] + eq[1]
    padded = jnp.concatenate([term, jnp.zeros((LANES - REGRESSORS, rows), F32)], axis=0)
    turned = pltpu.roll(jnp.transpose(padded), LANES - 1, 1)
    lane = lax.broadcasted_iota(jnp.int32, turned.shape, 1)
    turned = jnp.where(lane < REGRESSORS - 1, turned, 0.0)
    basis_ref[:, :LANES] = basis_ref[:, :LANES] + turned
    for p, copy in enumerate(weight_near):
        cut = slice(p * trades // PIECES, (p + 1) * trades // PIECES)
        arrive(copy)
        wadj_ref[cut, :] = wadj_ref[cut, :] + wz[1, cut, :].astype(F32)
    drain()


def square_scratch(rows, trades, feats, set_total):
    size, quarter = REGRESSORS, set_total // 4
    return [
        pltpu.VMEM((6 * rows, feats), BF16),
        pltpu.VMEM((4, trades, feats), BF16),
        pltpu.VMEM((4, size + 16, trades), BF16),
        pltpu.VMEM((3, 4, size, rows), BF16),
        pltpu.VMEM((16, size, rows), BF16),
        pltpu.VMEM((LANES, 16 * rows), BF16),
        pltpu.VMEM((6 * rows, LANES), BF16),
        pltpu.VMEM((size, 6 * rows), BF16),
        pltpu.VMEM((set_total, 4 * trades), BF16),
        pltpu.VMEM((size, LANES), F32),
        pltpu.VMEM((4, size, quarter), F32),
        pltpu.VMEM((4, size, quarter), F32),
        pltpu.VMEM((size, quarter), F32),
        pltpu.VMEM((4, size, quarter), F32),
        pltpu.VMEM((size, quarter), F32),
        pltpu.VMEM((4, size, quarter), F32),
        pltpu.VMEM((size, quarter), F32),
        pltpu.VMEM((4, size, quarter), F32),
        pltpu.VMEM((8, quarter), F32),
        pltpu.VMEM((4, 8, quarter), F32),
        pltpu.VMEM((quarter, 16 * rows), F32),
        pltpu.VMEM((size, set_total), F32),
        pltpu.VMEM((6 * rows, 4 * trades), BF16),
        pltpu.VMEM((6 * rows, 4 * trades), F32),
        pltpu.VMEM((6 * rows, 4 * trades), BF16),
        pltpu.VMEM((size, 6 * rows), F32),
        pltpu.VMEM((2, trades, feats), BF16),
        pltpu.VMEM((trades, feats), BF16),
        pltpu.VMEM((trades, feats), F32),
        pltpu.VMEM((trades, feats), BF16),
        pltpu.VMEM((2, trades, feats), BF16),
        pltpu.VMEM((3, rows, feats), BF16),
        pltpu.VMEM((2, rows, feats), BF16),
        pltpu.VMEM((2, rows, feats), F32),
        pltpu.VMEM((2, rows, feats), BF16),
        pltpu.VMEM((2, rows, feats), BF16),
        pltpu.VMEM((3, size, rows), F32),
        pltpu.VMEM((2, size, rows), F32),
        pltpu.VMEM((2, size, rows), F32),
        pltpu.VMEM((2, size, rows), F32),
        pltpu.SemaphoreType.DMA((7,)),
        pltpu.SemaphoreType.DMA((SENDS,)),
        pltpu.SemaphoreType.DMA((ARRIVALS,)),
        pltpu.SemaphoreType.REGULAR((6,)),
        pltpu.SemaphoreType.REGULAR,
    ]


def chain_scratch(inner, outer, rows, trades, feats, set_total):
    size, quarter, count = REGRESSORS, set_total // inner, inner * outer
    z_pairs, q_pairs = max(outer - 1, 1), max(inner - 1, 1)
    return [
        pltpu.VMEM((inner, rows, feats), BF16),
        pltpu.VMEM((outer, trades, feats), BF16),
        pltpu.VMEM((outer, 8, trades), F32),
        pltpu.VMEM((8, trades), F32),
        pltpu.VMEM((size, rows), BF16),
        pltpu.VMEM((outer, size, rows), BF16),
        pltpu.VMEM((inner, outer, size, rows), BF16),
        pltpu.VMEM((LANES, count * rows), BF16),
        pltpu.VMEM((set_total, outer * trades), BF16),
        pltpu.VMEM((size, LANES), F32),
        pltpu.VMEM((inner, size, quarter), F32),
        pltpu.VMEM((inner, size, quarter), F32),
        pltpu.VMEM((size, quarter), F32),
        pltpu.VMEM((outer, size, quarter), F32),
        pltpu.VMEM((size, quarter), F32),
        pltpu.VMEM((inner, size, quarter), F32),
        pltpu.VMEM((size + 8, quarter), F32),
        pltpu.VMEM((inner, size + 8, quarter), F32),
        pltpu.VMEM((inner, size, rows), F32),
        pltpu.VMEM((inner, size, rows), F32),
        pltpu.VMEM((outer, trades, feats), BF16),
        pltpu.VMEM((outer, trades, feats), BF16),
        pltpu.VMEM((inner, rows, feats), BF16),
        pltpu.VMEM((inner, rows, feats), BF16),
        pltpu.VMEM((inner * rows, outer * trades), F32),
        pltpu.VMEM((inner * rows, outer * trades), BF16),
        pltpu.SemaphoreType.DMA((7,)),
        pltpu.SemaphoreType.DMA((5, z_pairs)),
        pltpu.SemaphoreType.DMA((5, z_pairs)),
        pltpu.SemaphoreType.DMA((7, q_pairs)),
        pltpu.SemaphoreType.DMA((7, q_pairs)),
    ]


def publish(*refs):
    sources, targets, done = refs[:3], refs[3:6], refs[6]
    copies = [
        pltpu.make_async_copy(source, target, done.at[i])
        for i, (source, target) in enumerate(zip(sources, targets))
    ]
    for copy in copies:
        copy.start()
    for copy in copies:
        copy.wait()


def shards(
    path_basis, proxy_weight, notional, set_of, threshold_index, threshold_levels, loss_rate
):
    count = lax.axis_size("paths")
    inner = math.gcd(4, count)
    outer = count // inner
    rows, feats = path_basis.shape
    trades = proxy_weight.shape[0]
    set_total = loss_rate.shape[0]
    quarter = set_total // inner
    vmem = pl.BlockSpec(memory_space=pltpu.VMEM)
    if count == 16 and rows == trades and rows % (16 * PIECES) == 0:
        body = functools.partial(square, rows * count, set_total)
        scratch = square_scratch(rows, trades, feats, set_total)
    else:
        body = functools.partial(kernel, inner, outer, rows * count, set_total)
        scratch = chain_scratch(inner, outer, rows, trades, feats, set_total)
    loss, basis_adjoint, weight_adjoint = pl.pallas_call(
        body,
        out_shape=(
            jax.ShapeDtypeStruct((1, LANES), F32),
            jax.ShapeDtypeStruct((rows, feats), F32),
            jax.ShapeDtypeStruct((trades, feats), F32),
        ),
        in_specs=[pl.BlockSpec(memory_space=pltpu.HBM)] * 7,
        out_specs=(vmem, vmem, vmem),
        scratch_shapes=[
            pltpu.VMEM((1, trades), BF16),
            pltpu.VMEM((inner * outer, trades), jnp.int32),
            pltpu.VMEM((inner, quarter), jnp.int32),
            pltpu.SMEM(threshold_levels.shape, F32),
            pltpu.VMEM((inner, quarter), F32),
            *scratch,
        ],
        compiler_params=pltpu.CompilerParams(
            collective_id=0, has_side_effects=True, vmem_limit_bytes=48 * 1024 * 1024
        ),
    )(
        *(
            pltpu.with_memory_space_constraint(operand, pltpu.HBM)
            for operand in (
                path_basis,
                proxy_weight,
                notional.reshape(1, trades),
                set_of.reshape(-1, trades),
                threshold_index.reshape(inner, quarter),
                threshold_levels,
                loss_rate.reshape(inner, quarter),
            )
        )
    )
    results = (loss, basis_adjoint, weight_adjoint)
    loss, basis_adjoint, weight_adjoint = pl.pallas_call(
        publish,
        out_shape=[jax.ShapeDtypeStruct(result.shape, result.dtype) for result in results],
        in_specs=[pl.BlockSpec(memory_space=pl.ANY)] * 3,
        out_specs=[pl.BlockSpec(memory_space=pl.ANY)] * 3,
        scratch_shapes=[pltpu.SemaphoreType.DMA((3,))],
        compiler_params=pltpu.CompilerParams(vmem_limit_bytes=1024 * 1024),
    )(*results)
    return loss[0, :1], basis_adjoint, weight_adjoint


def solution(mesh):
    placed = (
        P(("groups", "paths"), None),
        P(("groups", "paths"), None),
        P(("groups", "paths")),
        P("groups"),
        P("groups"),
        P("groups"),
        P("groups"),
    )
    return jax.shard_map(
        shards,
        mesh=mesh,
        in_specs=placed,
        out_specs=(P("groups"), P(("groups", "paths"), None), P(("groups", "paths"), None)),
        check_vma=False,
    )
```
